32 devices in a mesh: bricks: 8 (over z, y), group: 4 (over x, core).
Axes of the slice: x: 2, y: 2, z: 4, core: 2. Of those that a mesh axis runs over, the one named last changes fastest.
Arguments:
- right_side: float32 [3, 128, 64, 128], P(None, 'bricks', 'group'), may hold values from -6 to 6
- material: int32 [128, 64, 128], P('bricks', 'group'), may hold values from 0 to 3
- brick_level: int32 [8, 4], P('bricks', 'group'), may hold values from 0 to 2
- mortar_rows: int32 [8, 4, 16], P('bricks', 'group'), may hold values from 0 to 15, each once within a row
- material_mu: float32 [4], replicated, may hold values from 0.5 to 4
- material_lam: float32 [4], replicated, may hold values from 0.25 to 2
- coarse_inverse: float32 [8, 48, 48], P('bricks'), may hold values from -1 to 5, as said below
Outputs:
- solution: float32 [3, 128, 64, 128], P(None, 'bricks', 'group')
- residual: float32 [3, 128, 64, 128], P(None, 'bricks', 'group')
The draws below stay inside these ranges and needn't reach their ends.
Inputs may be any that keep to these rules, and one draw needn't show every extreme that they name: `coarse_inverse`: each brick row's matrix is of full rank with a positive diagonal.
All inputs are finite; a program needn't handle non-finite values.
Results may differ from the reference program's by a relative error of at most 0.00027.
Values sent between devices are 32-bit elements; how exact they have to be, the bound alone decides.
A program may use at most 64 MiB of HBM per device.

```python
import math
import jax
import jax.numpy as jnp
from jax import lax

BX = 16
BY = 16
BZ = 128
BLOCK_XY = 16
BLOCK_Z = 32
CHEB = 4
NX = 128
NY = 64
CG = 48
N_BRICKS = 8
N_GROUP = 4


def draw_coarse_inverse(key, part):
    noise_key, diagonal_key = jax.random.split(jax.random.fold_in(key, 11))
    spread = 0.5 * jax.random.truncated_normal(noise_key, -4.0, 4.0, (N_BRICKS, CG, CG), jnp.float32)
    noise_part = spread / CG ** 0.5
    diagonal = jax.random.uniform(diagonal_key, (N_BRICKS, CG), jnp.float32, 2.0, 4.0)
    identity = (lax.broadcasted_iota(jnp.int32, (CG, CG), 0) == lax.broadcasted_iota(jnp.int32, (CG, CG), 1)).astype(jnp.float32)
    return noise_part + diagonal[:, :, None] * identity[None]


def plant(values, rng, low, top_value):
    longest = values.shape.index(max(values.shape))
    spots = []
    for shift in (0, 1):
        where = [jax.random.randint(jax.random.fold_in(rng, axis), (), 0, length) for axis, length in enumerate(values.shape)]
        where[longest] = (where[longest] + shift) % values.shape[longest]
        spots.append(tuple(where))
    return values.at[spots[0]].set(low).at[spots[1]].set(top_value)


def levels(own_key, shape, pieces, low, high):
    factor_of = 1.0
    for position, shards_of in pieces:
        steps = jax.random.uniform(jax.random.fold_in(jax.random.fold_in(own_key, 6), position), (shards_of,), jnp.float32, low / len(pieces), high / len(pieces))
        factor_of = factor_of * jnp.repeat(jnp.exp(steps), shape[position] // shards_of).reshape((-1,) + (1,) * (len(shape) - 1 - position))
    return factor_of


def noise(own_key, shape, scale, reach, cuts=(), kind=jnp.bfloat16):
    factor_of = levels(own_key, shape, cuts, -0.22, 0.18) if cuts else 1.0
    array = jax.random.normal(own_key, shape, jnp.float32) * scale * factor_of
    return jnp.minimum(jnp.maximum(array, -reach), reach).astype(kind)


def setup_inputs(seed: int = 0) -> dict:
    streams_of = jax.random.split(jax.random.key(seed), 8)
    right_side = noise(streams_of[0], (3, NX, NY, BZ), 1.0, 6.0, ((1, 8), (2, 4)), jnp.float32)
    material = plant(jax.random.randint(streams_of[1], (NX, NY, BZ), 0, 4), jax.random.fold_in(streams_of[1], 1), 0, 3).astype(jnp.int32)
    brick_level = plant(jax.random.randint(streams_of[2], (N_BRICKS, N_GROUP), 0, 3), jax.random.fold_in(streams_of[2], 1), 0, 2).astype(jnp.int32)
    mortar_rows = jax.vmap(lambda own: jax.random.permutation(own, BY))(jax.random.split(streams_of[3], N_BRICKS * N_GROUP)).reshape((N_BRICKS, N_GROUP, BY)).astype(jnp.int32)
    material_mu = jnp.clip(jnp.exp(jax.random.uniform(streams_of[4], (4,), jnp.float32, math.log(0.5), math.log(4.0))), 0.5, 4.0)
    material_lam = jnp.clip(jnp.exp(jax.random.uniform(streams_of[5], (4,), jnp.float32, math.log(0.25), math.log(2.0))), 0.25, 2.0)
    coarse_inverse = draw_coarse_inverse(jax.random.fold_in(streams_of[7], 71), 0)
    return dict(right_side=right_side, material=material, brick_level=brick_level, mortar_rows=mortar_rows, material_mu=material_mu, material_lam=material_lam, coarse_inverse=coarse_inverse)


low_ratio = 0.15
bound_margin = 1.1


def lookup(ids, table):
    total = jnp.zeros(ids.shape, table.dtype)
    for entry in range(4):
        total = total + jnp.where(ids == entry, table[entry], 0.0)
    return total


def neighbours(field, order, undo):
    count = field.shape[0]
    blocks = field.reshape(count, N_BRICKS, BX, N_GROUP, BY, BZ)
    last_face = blocks[:, :, BX - 1]
    first_face = blocks[:, :, 0]
    sent = jnp.take_along_axis(last_face, jnp.broadcast_to(order[None, :, :, :, None], last_face.shape), axis=3)
    below = jnp.concatenate([jnp.zeros_like(sent[:, :1]), sent[:, :-1]], axis=1)
    upper_faces = jnp.concatenate([first_face[:, 1:], jnp.zeros_like(first_face[:, :1])], axis=1)
    above = jnp.take_along_axis(upper_faces, jnp.broadcast_to(undo[None, :, :, :, None], upper_faces.shape), axis=3)
    x_plus = jnp.concatenate([blocks[:, :, 1:], above[:, :, None]], axis=2).reshape(field.shape)
    x_minus = jnp.concatenate([below[:, :, None], blocks[:, :, :-1]], axis=2).reshape(field.shape)
    y_plus = jnp.pad(field[:, :, 1:], ((0, 0), (0, 0), (0, 1), (0, 0)))
    y_minus = jnp.pad(field[:, :, :-1], ((0, 0), (0, 0), (1, 0), (0, 0)))
    z_plus = jnp.pad(field[:, :, :, 1:], ((0, 0), (0, 0), (0, 0), (0, 1)))
    z_minus = jnp.pad(field[:, :, :, :-1], ((0, 0), (0, 0), (0, 0), (1, 0)))
    return [x_plus, x_minus, y_plus, y_minus, z_plus, z_minus]


def chebyshev(solution, residual, apply, diagonal, lower, upper):
    theta = 0.5 * (upper + lower)
    delta = 0.5 * (upper - lower)
    sigma = theta / delta
    damping = 1.0 / sigma
    update = residual / (diagonal * theta)
    for turn in range(CHEB):
        solution = solution + update
        residual = residual - apply(update)
        if turn + 1 < CHEB:
            damping_next = 1.0 / (2.0 * sigma - damping)
            update = damping_next * damping * update + (2.0 * damping_next / delta) * (residual / diagonal)
            damping = damping_next
    return solution, residual


def reference(right_side, material, brick_level, mortar_rows, material_mu, material_lam, coarse_inverse):
    order = mortar_rows
    undo = jnp.argsort(mortar_rows, axis=-1).astype(jnp.int32)
    level_scale = jnp.exp2(2.0 * brick_level.astype(right_side.dtype))
    cell_scale = jnp.repeat(jnp.repeat(level_scale, BX, axis=0), BY, axis=1)[:, :, None]
    shear = lookup(material, material_mu) * cell_scale
    bulk = lookup(material, material_lam) * cell_scale
    x_index = lax.broadcasted_iota(jnp.int32, (NX, NY, BZ), 0)
    y_index = lax.broadcasted_iota(jnp.int32, (NX, NY, BZ), 1)
    z_index = lax.broadcasted_iota(jnp.int32, (NX, NY, BZ), 2)
    outside = [x_index == NX - 1, x_index == 0, y_index == NY - 1, y_index == 0, z_index == BZ - 1, z_index == 0]
    shear_near = neighbours(shear[None], order, undo)
    weights = [jnp.where(edge, shear, 0.5 * (shear + other[0])) for edge, other in zip(outside, shear_near)]
    weight_total = weights[0]
    for extra in weights[1:]:
        weight_total = weight_total + extra
    diagonal = weight_total + 1.5 * bulk
    bound_ratio = (2.0 * weight_total + 2.5 * bulk) / diagonal
    upper = bound_margin * jnp.max(bound_ratio)
    lower = low_ratio * upper

    def apply(field):
        near = neighbours(field, order, undo)
        coupled = jnp.sum(field, axis=0)
        result = weight_total * field + bulk * (field + 0.5 * coupled)
        for weight, value in zip(weights, near):
            result = result - weight * value
        return result

    solution = jnp.zeros_like(right_side)
    solution, residual = chebyshev(solution, right_side, apply, diagonal, lower, upper)
    cells_x = BX // BLOCK_XY
    cells_y = BY // BLOCK_XY
    cells_z = BZ // BLOCK_Z
    shaped = residual.reshape(3, N_BRICKS, cells_x, BLOCK_XY, N_GROUP, cells_y, BLOCK_XY, cells_z, BLOCK_Z)
    coarse = jnp.mean(shaped, axis=(3, 6, 8))
    coarse = coarse.transpose(1, 3, 0, 2, 4, 5).reshape(N_BRICKS, CG)
    correction = jnp.einsum('bij,bj->bi', coarse_inverse, coarse, precision=lax.Precision.HIGHEST)
    spread = correction.reshape(N_BRICKS, N_GROUP, 3, cells_x, cells_y, cells_z).transpose(2, 0, 3, 1, 4, 5)
    fine = jnp.broadcast_to(spread[:, :, :, None, :, :, None, :, None], (3, N_BRICKS, cells_x, BLOCK_XY, N_GROUP, cells_y, BLOCK_XY, cells_z, BLOCK_Z)).reshape(3, NX, NY, BZ)
    solution = solution + fine
    residual = residual - apply(fine)
    solution, residual = chebyshev(solution, residual, apply, diagonal, lower, upper)
    return solution, residual
```

```python
import functools

import jax
import jax.numpy as jnp
from jax import lax
from jax.experimental import pallas as pl
from jax.experimental.pallas import tpu as pltpu
from jax.sharding import PartitionSpec as P

BLOCK_Z = 32
CHEB = 4
LOW_RATIO = 0.15
BOUND_MARGIN = 1.1
ROUNDS = 5
DEPTH = (2, 2, 1, 2, 1)
UNROLL = 4
SWEEP = 7
INNER = 6
HIGHEST = lax.Precision.HIGHEST


def kernel(
    nb, ng, dx, dy, dz,
    rhs_in, material_in, level, mortar, mu, lam, inverse_in,
    sol, res, rhs, material, inverse,
    u, r, shear, wx, wyp, wym, wzp, wzm, dg, hb, invd, coef,
    s_send_up, s_send_y, s_recv, static_send, static_recv, index_send, index_recv, index,
    faces, mixed, y_send, corner_send, recv_x, recv_y, recv_d, ghost, gy, before,
    m_own, m_all, m2_own, m2_all, c_own, c_all, f_all, inv_recv, in_sem,
    s_ssem, s_rsem, t_ssem, t_rsem, h_ssem, h_rsem,
    m_ssem, m_rsem, m2_ssem, m2_rsem, c_ssem, c_rsem, i_ssem, i_rsem,
):
    b = lax.axis_index("bricks")
    g = lax.axis_index("group")
    has = [b > 0, b < nb - 1, g > 0, g < ng - 1]
    sends = [has[1], has[0], has[3], has[2]]
    peers = [(b + 1, g), (b - 1, g), (b, g + 1), (b, g - 1)]
    corners = [(0, 0), (0, 1), (1, 0), (1, 1)]
    has_corner = [has[sx] & has[2 + sy] for sx, sy in corners]
    corner_peer = [(b + 2 * sx - 1, g + 2 * sy - 1) for sx, sy in corners]

    def remote(src, dst, ssem, rsem, peer):
        return pltpu.make_async_remote_copy(
            src_ref=src, dst_ref=dst, send_sem=ssem, recv_sem=rsem,
            device_id=peer, device_id_type=pl.DeviceIdType.MESH,
        )

    barrier = pltpu.get_barrier_semaphore()
    others = [(b, lax.rem(g + k, ng)) for k in range(1, ng)]
    others += [(lax.rem(b + k, nb), g) for k in range(1, nb)]
    around = [(lax.rem(g + k, ng)) for k in range(1, ng)]
    for peer in others:
        pl.semaphore_signal(
            barrier, inc=1, device_id=peer, device_id_type=pl.DeviceIdType.MESH
        )
    for d in range(2):
        @pl.when(has[d])
        def _():
            for at in around:
                pl.semaphore_signal(
                    barrier, inc=1, device_id=(b - 1 + 2 * d, at),
                    device_id_type=pl.DeviceIdType.MESH,
                )

    def fetch(k):
        source = [material_in, rhs_in, inverse_in.at[0]][k]
        return pltpu.make_async_copy(source, [material, rhs, inverse][k], in_sem.at[k])

    for k in range(3):
        fetch(k).start()

    row = lax.broadcasted_iota(jnp.int32, (dy, dz), 0)
    lane = lax.broadcasted_iota(jnp.int32, (dy, dz), 1)
    grade = jnp.broadcast_to(level[...], (dy, dz))
    scale = jnp.where(grade == 0, 1.0, jnp.where(grade == 1, 4.0, 16.0))
    zero_face = jnp.zeros((dy, dz), jnp.float32)

    order = [mortar[0, 0, k] for k in range(dy)]
    order_here = jnp.zeros((dy, dz), jnp.int32)
    undo_here = jnp.zeros((dy, dz), jnp.int32)
    for k in range(dy):
        order_here = jnp.where(row == k, order[k], order_here)
        undo_here = jnp.where(row == order[k], k, undo_here)
    index_send[...] = order_here
    index[0] = order_here
    index[1] = undo_here

    def permute(value, k):
        half = dy // 2
        parts = []
        for h in range(2):
            at = index[k, h * half : (h + 1) * half]
            within = jnp.bitwise_and(at, half - 1)
            low = jnp.take_along_axis(value[:half], within, axis=0)
            high = jnp.take_along_axis(value[half:], within, axis=0)
            parts.append(jnp.where(at < half, low, high))
        return jnp.concatenate(parts, axis=0)

    def lookup(ids, table):
        total = jnp.where(ids == 0, table[0], 0.0)
        for entry in range(1, 4):
            total = jnp.where(ids == entry, table[entry], total)
        return total * scale

    def shear_plane(i, _):
        ids = material[i]
        plane = lookup(ids, mu)
        bulk = lookup(ids, lam)
        shear[i + 1] = plane
        hb[i] = bulk
        s_send_y[0, pl.ds(i, 1), :] = plane[dy - 1 : dy]
        s_send_y[1, pl.ds(i, 1), :] = plane[0:1]
        for d, near, far in ((2, dy - 1, dy - 2), (3, 0, 1)):
            static_send[d, 0, pl.ds(i, 1), :] = plane[near : near + 1]
            static_send[d, 1, pl.ds(i, 1), :] = plane[far : far + 1]
            static_send[d, 2, pl.ds(i, 1), :] = bulk[near : near + 1]
        return 0

    fetch(0).wait()
    lax.fori_loop(0, dx, shear_plane, 0, unroll=UNROLL)
    s_send_up[...] = permute(shear[dx], 0)
    for d, near, far in ((0, dx - 1, dx - 2), (1, 0, 1)):
        static_send[d, 0] = shear[near + 1]
        static_send[d, 1] = shear[far + 1]
        static_send[d, 2] = hb[near]

    both = jnp.where(has[0], len(around), 0) + jnp.where(has[1], len(around), 0)
    pl.semaphore_wait(barrier, len(others) + both)

    def s_copy(d):
        src = [s_send_up, shear.at[1], s_send_y.at[0], s_send_y.at[1]][d]
        return remote(src, s_recv.at[d], s_ssem.at[d], s_rsem.at[d], peers[d])

    def t_copy(d):
        if d == 4:
            return remote(index_send, index_recv, t_ssem.at[4], t_rsem.at[4], peers[0])
        return remote(
            static_send.at[d], static_recv.at[d], t_ssem.at[d], t_rsem.at[d], peers[d]
        )

    def exchange_start(copy, directions=(0, 1, 2, 3)):
        for d in directions:
            @pl.when(sends[d % 4])
            def _():
                copy(d).start()

    def arrive_wait(copy, directions=(0, 1, 2, 3)):
        for d in directions:
            @pl.when(has[d % 4])
            def _():
                copy(d).wait_recv()

    def sent_wait(copy, directions=(0, 1, 2, 3)):
        for d in directions:
            @pl.when(sends[d % 4])
            def _():
                copy(d).wait_send()

    def exchange_wait(copy, directions=(0, 1, 2, 3)):
        arrive_wait(copy, directions)
        sent_wait(copy, directions)

    exchange_start(s_copy)
    exchange_start(t_copy, (4, 0, 1, 2, 3))

    @pl.when(b == 0)
    def _():
        s_recv[0] = shear[1]
        index_recv[...] = row

    @pl.when(b == nb - 1)
    def _():
        s_recv[1] = shear[dx]

    @pl.when(g == 0)
    def _():
        s_recv[2] = s_send_y[1]

    @pl.when(g == ng - 1)
    def _():
        s_recv[3] = s_send_y[0]

    for d in range(4):
        @pl.when(jnp.logical_not(has[d]))
        def _():
            one = jnp.ones((dy, dz), jnp.float32)
            for k in range(3):
                static_recv[d, k] = one
            for turn in range(ROUNDS):
                for c in range(3):
                    for j in range(2):
                        if d < 2:
                            recv_x[turn, d, c, j] = zero_face
                        else:
                            recv_y[turn, d - 2, j, c] = zero_face
            if d < 2:
                inv_recv[d] = jnp.zeros(inv_recv.shape[1:], jnp.float32)
                c_all[2 * d] = jnp.zeros(c_all.shape[1:], jnp.float32)

    for k in range(4):
        @pl.when(jnp.logical_not(has_corner[k]))
        def _():
            for turn in range(ROUNDS):
                if DEPTH[turn] == 2:
                    recv_d[turn, k] = jnp.zeros(recv_d.shape[2:], jnp.float32)

    fetch(1).wait()
    fetch(2).wait()
    exchange_wait(s_copy)
    shear[0] = s_recv[0]

    @pl.when(b < nb - 1)
    def _():
        shear[dx + 1] = permute(s_recv[1], 1)

    @pl.when(b == nb - 1)
    def _():
        shear[dx + 1] = shear[dx]

    def rows_near(v, low, high):
        m = jnp.where(row == 0, jnp.broadcast_to(low, v.shape), pltpu.roll(v, 1, 0))
        p = jnp.where(
            row == dy - 1, jnp.broadcast_to(high, v.shape), pltpu.roll(v, dy - 1, 0)
        )
        return m, p

    def z_near(v):
        return pltpu.roll(v, 1, 1), pltpu.roll(v, dz - 1, 1)

    def h_copy(turn, slot):
        deep = DEPTH[turn]

        def copy(d):
            if d == 0:
                src = u.at[slot, :, dx + 1 - deep : dx + 1]
                dst = recv_x.at[turn, 0, :, 2 - deep : 2]
            elif d == 1:
                src = u.at[slot, :, 1 : 1 + deep]
                dst = recv_x.at[turn, 1, :, 0:deep]
            else:
                src = y_send.at[turn, d - 2, 0:deep]
                dst = recv_y.at[turn, d - 2, 0:deep]
            return remote(src, dst, h_ssem.at[turn, d], h_rsem.at[turn, d], peers[d])
        return copy

    def corner_copy(turn, k):
        return remote(
            corner_send.at[turn, k], recv_d.at[turn, 3 - k],
            h_ssem.at[turn, 4 + k], h_rsem.at[turn, 7 - k], corner_peer[k],
        )

    def corner_arrival(turn, k):
        return remote(
            corner_send.at[turn, k], recv_d.at[turn, k],
            h_ssem.at[turn, 4 + k], h_rsem.at[turn, 4 + k], corner_peer[k],
        )

    even = lax.rem(b, 2) == 0

    def send_faces(turn, slot):
        copy = h_copy(turn, slot)

        @pl.when(sends[1] & even)
        def _():
            copy(1).start()

        exchange_start(copy, (0,))

        @pl.when(sends[1] & jnp.logical_not(even))
        def _():
            copy(1).start()

        if DEPTH[turn] == 1:
            return
        for c in range(3):
            bottom, top = u[slot, c, 1], u[slot, c, dx]
            mixed_low, mixed_high = permute(bottom, 3), permute(top, 0)
            mixed[0, c] = mixed_low
            mixed[1, c] = mixed_high
            for k, (sx, sy) in enumerate(corners):
                y = (dy - 1) * sy
                plane, other = ((bottom, mixed_low), (top, mixed_high))[sx]
                corner_send[turn, k, c : c + 1, :] = plane[y : y + 1]
                corner_send[turn, k, 3 + c : 4 + c, :] = other[y : y + 1]
        for k in range(4):
            @pl.when(has_corner[k])
            def _():
                corner_copy(turn, k).start()

    def send_rows(turn, slot):
        exchange_start(h_copy(turn, slot), (2, 3))

    def store_rows(turn, c, i, value):
        y_send[turn, 0, 0, c, pl.ds(i, 1), :] = value[dy - 1 : dy]
        y_send[turn, 1, 0, c, pl.ds(i, 1), :] = value[0:1]
        if DEPTH[turn] == 2:
            y_send[turn, 0, 1, c, pl.ds(i, 1), :] = value[dy - 2 : dy - 1]
            y_send[turn, 1, 1, c, pl.ds(i, 1), :] = value[1:2]

    def corners_wait(turn):
        for k in range(4):
            @pl.when(has_corner[k])
            def _():
                corner_arrival(turn, k).wait_recv()
        for k in range(4):
            @pl.when(has_corner[k])
            def _():
                corner_copy(turn, k).wait_send()

    def nearest(turn, s, c):
        return recv_x[turn, s, c, 1 - s]

    def place_faces(turn, slot):
        for c in range(3):
            u[slot, c, 0] = permute(nearest(turn, 0, c), 2)
            u[slot, c, dx + 1] = permute(nearest(turn, 1, c), 1)

    def sweep_send(plane, turn, slot, carry):
        deep = DEPTH[turn]
        for i in range(deep):
            carry = plane(i, carry)
            carry = plane(dx - 1 - i, carry)
        send_faces(turn, slot)
        unroll = INNER if deep == 2 else SWEEP
        carry = lax.fori_loop(deep, dx - deep, plane, carry, unroll=unroll)
        send_rows(turn, slot)
        return carry

    def sweep_receive(plane, turn, slot, carry, faces_done=None):
        exchange_wait(h_copy(turn, slot), (2, 3))
        carry = lax.fori_loop(1, dx - 1, plane, carry, unroll=SWEEP)
        exchange_wait(h_copy(turn, slot), (0, 1))
        if DEPTH[turn] == 2:
            corners_wait(turn)
        place_faces(turn, slot)
        if faces_done is not None:
            faces_done()
        carry = plane(0, carry)
        carry = plane(dx - 1, carry)
        return carry

    wx[0] = 0.5 * (shear[0] + shear[1])
    wx[dx] = 0.5 * (shear[dx] + shear[dx + 1])

    exchange_wait(t_copy, (4,))
    index[2] = index_recv[...]
    undo_below = jnp.zeros((dy, dz), jnp.int32)
    for k in range(dy):
        at = jnp.broadcast_to(index_recv[k : k + 1, :], (dy, dz))
        undo_below = jnp.where(row == at, k, undo_below)
    index[3] = undo_below

    def weight_plane(i, best):
        s = shear[i + 1]
        xp = 0.5 * (s + shear[i + 2])
        wx[i + 1] = xp
        xm = 0.5 * (s + shear[i])
        ym, yp = rows_near(s, s_recv[2, pl.ds(i, 1), :], s_recv[3, pl.ds(i, 1), :])
        ym = 0.5 * (s + ym)
        yp = 0.5 * (s + yp)
        zm, zp = z_near(s)
        zm = 0.5 * (s + zm)
        zp = 0.5 * (s + zp)
        wyp[i] = yp
        wym[i] = ym
        wzp[i] = jnp.where(lane == dz - 1, 0.0, zp)
        wzm[i] = jnp.where(lane == 0, 0.0, zm)
        total = xp + xm + yp + ym + jnp.where(lane == dz - 1, s, zp) + jnp.where(lane == 0, s, zm)
        bulk = hb[i]
        diagonal = total + 1.5 * bulk
        inv = 1.0 / diagonal
        invd[i] = inv
        dg[i] = total + bulk
        hb[i] = 0.5 * bulk
        for c in range(3):
            d0 = rhs[c, i] * inv
            u[0, c, i + 1] = d0
            store_rows(0, c, i, d0)
        return jnp.maximum(best, (2.0 * total + 2.5 * bulk) / diagonal)

    below_shear = permute(shear[1], 3)
    faces[0] = below_shear
    for k, (sx, sy) in enumerate(corners):
        y = (dy - 1) * sy
        plane = shear[(1, dx)[sx]]
        other = (below_shear, s_send_up[...])[sx]
        corner_send[0, k, 6:7, :] = plane[y : y + 1]
        corner_send[0, k, 7:8, :] = other[y : y + 1]

    best = sweep_send(weight_plane, 0, 0, jnp.zeros((dy, dz), jnp.float32))
    m_own[...] = jnp.broadcast_to(jnp.max(best, axis=0, keepdims=True), m_own.shape)

    def apply_plane(i, slot, low, high):
        v = [u[slot, c, i + 1] for c in range(3)]
        coupled = hb[i] * (v[0] + v[1] + v[2])
        out = []
        for c in range(3):
            ym, yp = rows_near(v[c], low(c, i), high(c, i))
            zm, zp = z_near(v[c])
            near = wx[i] * u[slot, c, i] + wx[i + 1] * u[slot, c, i + 2]
            near = near + wym[i] * ym + wyp[i] * yp + wzm[i] * zm + wzp[i] * zp
            out.append(dg[i] * v[c] + coupled - near)
        return v, out

    def recv_rows(turn):
        return (
            lambda c, i: recv_y[turn, 0, 0, c, pl.ds(i, 1), :],
            lambda c, i: recv_y[turn, 1, 0, c, pl.ds(i, 1), :],
        )

    ghost_rows = (
        lambda c, i: gy[0, c, pl.ds(i, 1), :],
        lambda c, i: gy[1, c, pl.ds(i, 1), :],
    )

    def bcoef(k):
        return jnp.broadcast_to(coef[k : k + 1, :], (dy, dz))

    def ghost_weights(d, cross, low, high):
        near, far, bulk = [static_recv[d, k] for k in range(3)]
        inner = 0.5 * (near + far)
        across = 0.5 * (near + cross)
        rm, rp = rows_near(near, low, high)
        rm = 0.5 * (near + rm)
        rp = 0.5 * (near + rp)
        zm, zp = z_near(near)
        zm = 0.5 * (near + zm)
        zp = 0.5 * (near + zp)
        total = inner + across + rm + rp
        total = total + jnp.where(lane == dz - 1, near, zp) + jnp.where(lane == 0, near, zm)
        inv = jnp.where(has[d], 1.0, 0.0) / (total + 1.5 * bulk)
        zm = jnp.where(lane == 0, 0.0, zm)
        zp = jnp.where(lane == dz - 1, 0.0, zp)
        for k, value in enumerate(
            (inner, across, rm, rp, zm, zp, total + bulk, 0.5 * bulk, inv)
        ):
            ghost[d, k] = value

    def all_ghost_weights():
        def edge(inside, corner, at, own):
            return jnp.where(inside, recv_d[0, corner, at : at + 1, :], own)

        for d in range(4):
            s = d % 2
            near = static_recv[d, 0]
            ends = near[0:1], near[dy - 1 : dy]
            if d < 2:
                cross = (faces[0], s_send_up[...])[s]
                low = edge(has[2], 2 * s, 6, ends[0])
                high = edge(has[3], 2 * s + 1, 6, ends[1])
            else:
                cross = s_send_y[1 - s]
                low = edge(has[0], s, 7, ends[0])
                high = edge(has[1], 2 + s, 7, ends[1])
            ghost_weights(d, cross, low, high)

    def ghost_apply(d, v, inner, cross, low, high):
        w = [ghost[d, k] for k in range(9)]
        coupled = w[7] * (v[0] + v[1] + v[2])
        out = []
        for c in range(3):
            rm, rp = rows_near(v[c], low[c], high[c])
            zm, zp = z_near(v[c])
            near = w[0] * inner[c] + w[1] * cross[c] + w[2] * rm + w[3] * rp
            near = near + w[4] * zm + w[5] * zp
            out.append(w[8] * (w[6] * v[c] + coupled - near))
        return out

    def ghost_step(turn, other, update):
        for d in range(4):
            s = d % 2
            if d < 2:
                v = [nearest(turn, s, c) for c in range(3)]
                inner = [recv_x[turn, s, c, s] for c in range(3)]
                cross = [mixed[s, c] for c in range(3)]
                low = [recv_d[turn, 2 * s, c : c + 1, :] for c in range(3)]
                high = [recv_d[turn, 2 * s + 1, c : c + 1, :] for c in range(3)]
            else:
                v = [recv_y[turn, s, 0, c] for c in range(3)]
                inner = [recv_y[turn, s, 1, c] for c in range(3)]
                cross = [y_send[turn, 1 - s, 0, c] for c in range(3)]
                low = [recv_d[turn, s, 3 + c : 4 + c, :] for c in range(3)]
                high = [recv_d[turn, 2 + s, 3 + c : 4 + c, :] for c in range(3)]
            out = ghost_apply(d, v, inner, cross, low, high)
            for c in range(3):
                new = update(d, c, v[c], out[c])
                if d < 2:
                    u[other, c, (dx + 1) * s] = permute(new, 2 - s)
                else:
                    gy[s, c] = new

    def ring_start(own, store, ssem, rsem, peer_of, count, mine):
        copies = []
        for k in range(1, count):
            copies.append(remote(own, store.at[k], ssem.at[k], rsem.at[k], peer_of(k)))
        for copy in copies:
            copy.start()
        return copies

    group_peer = lambda k: (b, lax.rem(g + k, ng))
    brick_peer = lambda k: (lax.rem(b + k, nb), g)

    m_copies = ring_start(m_own, m_all, m_ssem, m_rsem, group_peer, ng, g)
    top = m_own[...]
    for k, copy in enumerate(m_copies):
        copy.wait()
        top = jnp.maximum(top, m_all[k + 1])
    m2_own[...] = top
    m2_copies = ring_start(m2_own, m2_all, m2_ssem, m2_rsem, brick_peer, nb, b)
    exchange_wait(t_copy)

    low, high = recv_rows(0)

    def first_plane(i, _):
        _, out = apply_plane(i, 0, low, high)
        inv = invd[i]
        for c in range(3):
            r[c, i] = out[c]
            u[1, c, i + 1] = out[c] * inv
        return 0

    def first_ghosts():
        all_ghost_weights()

        def update(d, c, v, out):
            before[d, c] = out
            return out

        ghost_step(0, 1, update)

    sweep_receive(first_plane, 0, 0, 0, first_ghosts)

    def second_plane(i, _):
        _, out = apply_plane(i, 1, *ghost_rows)
        for c in range(3):
            res[c, i] = out[c]
        return 0

    lax.fori_loop(0, dx, second_plane, 0, unroll=8)

    for k, copy in enumerate(m2_copies):
        copy.wait()
        top = jnp.maximum(top, m2_all[k + 1])
    upper = BOUND_MARGIN * jnp.broadcast_to(jnp.max(top, axis=1, keepdims=True), top.shape)
    lower = LOW_RATIO * upper
    theta = 0.5 * (upper + lower)
    delta = 0.5 * (upper - lower)
    sigma = theta / delta
    damping = 1.0 / sigma
    inv_theta = 1.0 / theta
    coef[0:8] = inv_theta
    rows = []
    for turn in range(1, CHEB):
        following = 1.0 / (2.0 * sigma - damping)
        rows.append((following * damping, 2.0 * following / delta))
        damping = following
    for turn, (a, c2) in enumerate(rows):
        coef[8 + 2 * turn : 9 + 2 * turn] = a[0:1]
        coef[9 + 2 * turn : 10 + 2 * turn] = c2[0:1]
    coef[14:15] = (rows[0][0] * inv_theta + rows[0][1])[0:1]
    coef[15:16] = (rows[0][1] * inv_theta)[0:1]
    for k in range(CHEB - 2):
        (a, c2), (a_next, c_next) = rows[k], rows[k + 1]
        ratio = c_next / c2
        coef[16 + 2 * k : 17 + 2 * k] = (a_next + ratio)[0:1]
        coef[17 + 2 * k : 18 + 2 * k] = (ratio * a)[0:1]

    alpha, beta, it = bcoef(14), bcoef(15), bcoef(0)
    both_it = alpha + it
    a_two, c_two = bcoef(10), bcoef(11)

    def combine_plane(i, _):
        inv = invd[i]
        for c in range(3):
            d0 = u[0, c, i + 1]
            one = alpha * d0 - beta * u[1, c, i + 1]
            sol[c, i] = it * d0 + one
            rest = rhs[c, i] - both_it * r[c, i] + beta * res[c, i]
            res[c, i] = rest
            two = a_two * one + c_two * (rest * inv)
            u[0, c, i + 1] = two
            store_rows(1, c, i, two)
        return 0

    sweep_send(combine_plane, 1, 0, 0)
    for d in range(4):
        for c in range(3):
            v = nearest(0, d, c) if d < 2 else recv_y[0, d - 2, 0, c]
            before[d, c] = alpha * v - beta * before[d, c]

    def step_plane(slot, low, high, a, c2, following, summed=False, rows_of=None):
        other = 1 - slot

        def plane(i, sums):
            v, out = apply_plane(i, slot, low, high)
            inv = invd[i]
            new = []
            for c in range(3):
                rest = res[c, i] - out[c]
                res[c, i] = rest
                sol[c, i] = sol[c, i] + v[c]
                if summed:
                    new.append(sums[c] + rest)
                if not following:
                    continue
                ahead = c2 * (rest * inv)
                if a is not None:
                    ahead = ahead + a * v[c]
                u[other, c, i + 1] = ahead
                if rows_of is not None:
                    store_rows(rows_of, c, i, ahead)
            return tuple(new)
        return plane

    def pair_ghosts(turn, other, k):
        def done():
            e1, e2, e3 = bcoef(16 + 2 * k), bcoef(17 + 2 * k), bcoef(11 + 2 * k)

            def update(d, c, v, out):
                return e1 * v - e2 * before[d, c] - e3 * out

            ghost_step(turn, other, update)
        return done

    def i_copy(d):
        return remote(inverse, inv_recv.at[d], i_ssem.at[d], i_rsem.at[d], peers[d])

    exchange_start(i_copy, (0, 1))
    plane = step_plane(0, *recv_rows(1), bcoef(12), bcoef(13), True)
    sweep_receive(plane, 1, 0, (), pair_ghosts(1, 1, 1))
    plane = step_plane(1, *ghost_rows, None, bcoef(0), True, summed=True, rows_of=2)
    init = tuple(jnp.zeros((dy, dz), jnp.float32) for _ in range(3))
    sums = sweep_send(plane, 2, 0, init)

    c_own[...] = jnp.zeros(c_own.shape, jnp.float32)
    for c in range(3):
        c_own[c : c + 1, :] = jnp.sum(sums[c], axis=0, keepdims=True)
    c_all[1, g] = c_own[...]

    def c_copy(q, k):
        slot = q * ng + k
        return remote(
            c_own, c_all.at[q, g], c_ssem.at[slot], c_rsem.at[slot],
            (b + 1 - q, lax.rem(g + k, ng)),
        )

    def c_arrival(q, k):
        slot = q * ng + k
        source = lax.rem(g + ng - k, ng)
        return remote(
            c_own, c_all.at[q, source], c_ssem.at[slot], c_rsem.at[slot],
            (b + 1 - q, lax.rem(g + k, ng)),
        )

    def coarse_all(to_do, flags):
        for q in (0, 2, 1):
            first = 1 if q == 1 else 0
            if q == 1:
                for k in range(first, ng):
                    to_do(q, k)
                continue

            @pl.when(flags[q])
            def _():
                for k in range(first, ng):
                    to_do(q, k)

    coarse_all(lambda q, k: c_copy(q, k).start(), {0: has[1], 2: has[0]})
    f_all[...] = jnp.zeros(f_all.shape, jnp.float32)
    exchange_wait(i_copy, (0, 1))
    coarse_all(lambda q, k: c_arrival(q, k).wait_recv(), {0: has[0], 2: has[1]})
    coarse_all(lambda q, k: c_copy(q, k).wait_send(), {0: has[1], 2: has[0]})

    cells_z = dz // BLOCK_Z
    size = 3 * cells_z * ng
    flat = c_all[...].reshape(3 * ng * 8, dz)
    li = lax.broadcasted_iota(jnp.int32, (dz, size), 0)
    ki = lax.broadcasted_iota(jnp.int32, (dz, size), 1)
    gather = jnp.where(li // BLOCK_Z == ki % cells_z, 1.0 / (dx * dy * BLOCK_Z), 0.0)
    spread = jnp.dot(flat, gather, precision=HIGHEST, preferred_element_type=jnp.float32)
    ri = lax.broadcasted_iota(jnp.int32, (ng * 8, size), 0)
    kk = lax.broadcasted_iota(jnp.int32, (ng * 8, size), 1) // cells_z
    mine = (ri // 8 == kk // 3) & (ri % 8 == kk % 3)
    bi = lax.broadcasted_iota(jnp.int32, (size, dz), 0)
    bl = lax.broadcasted_iota(jnp.int32, (size, dz), 1)
    placed = bi % cells_z == bl // BLOCK_Z
    for q in range(3):
        part = spread[q * ng * 8 : (q + 1) * ng * 8]
        vector = jnp.sum(jnp.where(mine, part, 0.0), axis=0, keepdims=True)
        matrix = inverse[...] if q == 1 else inv_recv[q // 2]
        correction = jnp.sum(matrix * vector, axis=1, keepdims=True)
        table = jnp.where(placed, jnp.broadcast_to(correction, (size, dz)), 0.0)
        for k in range(ng):
            for c in range(3):
                start = (k * 3 + c) * cells_z
                f_all[q, k + 1, c : c + 1, :] = jnp.sum(
                    table[start : start + cells_z], axis=0, keepdims=True
                )

    def full(q, at, c):
        return jnp.broadcast_to(f_all[q, at, c : c + 1, :], (dy, dz))

    own_fine = [full(1, g + 1, c) for c in range(3)]

    def fill_plane(i, _):
        for c in range(3):
            u[1, c, i + 1] = own_fine[c]
        return 0

    lax.fori_loop(0, dx, fill_plane, 0, unroll=UNROLL)
    for c in range(3):
        u[1, c, 0] = full(0, g + 1, c)
        u[1, c, dx + 1] = full(2, g + 1, c)
    exchange_wait(h_copy(2, 0))
    plane = step_plane(
        1,
        lambda c, i: f_all[1, g, c : c + 1, :],
        lambda c, i: f_all[1, g + 2, c : c + 1, :],
        None,
        bcoef(0),
        True,
    )
    lax.fori_loop(0, dx, plane, (), unroll=8)

    it = bcoef(0)
    for d in range(4):
        s = d % 2
        if d < 2:
            q = 2 * s
            here = [full(q, g + 1, c) for c in range(3)]
            low = [f_all[q, g, c : c + 1, :] for c in range(3)]
            high = [f_all[q, g + 2, c : c + 1, :] for c in range(3)]
        else:
            at = g + 2 * s
            here = [full(1, at, c) for c in range(3)]
            low = [f_all[0, at, c : c + 1, :] for c in range(3)]
            high = [f_all[2, at, c : c + 1, :] for c in range(3)]
        out = ghost_apply(d, here, here, own_fine, low, high)
        for c in range(3):
            value = nearest(2, s, c) if d < 2 else recv_y[2, s, 0, c]
            value = value - it * out[c]
            before[d, c] = value
            if d < 2:
                u[0, c, (dx + 1) * s] = permute(value, 2 - s)
            else:
                gy[s, c] = value

    plane = step_plane(0, *ghost_rows, bcoef(8), bcoef(9), True, rows_of=3)
    sweep_send(plane, 3, 1, ())
    plane = step_plane(1, *recv_rows(3), bcoef(10), bcoef(11), True)
    sweep_receive(plane, 3, 1, (), pair_ghosts(3, 0, 0))
    plane = step_plane(0, *ghost_rows, bcoef(12), bcoef(13), True, rows_of=4)
    sweep_send(plane, 4, 1, ())
    plane = step_plane(1, *recv_rows(4), None, None, False)
    sweep_receive(plane, 4, 1, ())


def per_device(rhs, material, level, mortar, mu, lam, inverse):
    nb = lax.axis_size("bricks")
    ng = lax.axis_size("group")
    dx, dy, dz = material.shape
    f32 = jnp.float32
    vmem = pl.BlockSpec(memory_space=pltpu.VMEM)
    smem = pl.BlockSpec(memory_space=pltpu.SMEM)
    hbm = pl.BlockSpec(memory_space=pltpu.HBM)
    dma = pltpu.SemaphoreType.DMA
    grid = pltpu.VMEM((dx, dy, dz), f32)
    cg = inverse.shape[1]
    scratch = [
        pltpu.VMEM((3, dx, dy, dz), f32),
        pltpu.VMEM((dx, dy, dz), jnp.int32),
        pltpu.VMEM((cg, cg), f32),
        pltpu.VMEM((2, 3, dx + 2, dy, dz), f32),
        pltpu.VMEM((3, dx, dy, dz), f32),
        pltpu.VMEM((dx + 2, dy, dz), f32),
        pltpu.VMEM((dx + 1, dy, dz), f32),
        grid, grid, grid, grid, grid, grid, grid,
        pltpu.VMEM((24, dz), f32),
        pltpu.VMEM((dy, dz), f32),
        pltpu.VMEM((2, dx, dz), f32),
        pltpu.VMEM((4, dx, dz), f32),
        pltpu.VMEM((4, 3, dx, dz), f32),
        pltpu.VMEM((4, 3, dx, dz), f32),
        pltpu.VMEM((dy, dz), jnp.int32),
        pltpu.VMEM((dy, dz), jnp.int32),
        pltpu.VMEM((4, dy, dz), jnp.int32),
        pltpu.VMEM((1, dy, dz), f32),
        pltpu.VMEM((2, 3, dy, dz), f32),
        pltpu.VMEM((ROUNDS, 2, 2, 3, dx, dz), f32),
        pltpu.VMEM((ROUNDS, 4, 8, dz), f32),
        pltpu.VMEM((ROUNDS, 2, 3, 2, dy, dz), f32),
        pltpu.VMEM((ROUNDS, 2, 2, 3, dx, dz), f32),
        pltpu.VMEM((ROUNDS, 4, 8, dz), f32),
        pltpu.VMEM((4, 9, dy, dz), f32),
        pltpu.VMEM((2, 3, dx, dz), f32),
        pltpu.VMEM((4, 3, dy, dz), f32),
        pltpu.VMEM((8, dz), f32),
        pltpu.VMEM((ng, 8, dz), f32),
        pltpu.VMEM((8, dz), f32),
        pltpu.VMEM((nb, 8, dz), f32),
        pltpu.VMEM((8, dz), f32),
        pltpu.VMEM((3, ng, 8, dz), f32),
        pltpu.VMEM((3, ng + 2, 8, dz), f32),
        pltpu.VMEM((2, cg, cg), f32),
        dma((3,)),
        dma((4,)), dma((4,)),
        dma((5,)), dma((5,)),
        dma((ROUNDS, 8)), dma((ROUNDS, 8)),
        dma((ng,)), dma((ng,)),
        dma((nb,)), dma((nb,)),
        dma((3 * ng,)), dma((3 * ng,)),
        dma((2,)), dma((2,)),
    ]
    rhs, material, inverse, mortar, mu, lam = (
        pltpu.with_memory_space_constraint(x, pltpu.HBM)
        for x in (rhs, material, inverse, mortar, mu, lam)
    )
    return pl.pallas_call(
        functools.partial(kernel, nb, ng, dx, dy, dz),
        out_shape=(
            jax.ShapeDtypeStruct(rhs.shape, f32),
            jax.ShapeDtypeStruct(rhs.shape, f32),
        ),
        in_specs=[hbm, hbm, vmem, smem, smem, smem, hbm],
        out_specs=(vmem, vmem),
        scratch_shapes=scratch,
        compiler_params=pltpu.CompilerParams(
            collective_id=0, has_side_effects=True, vmem_limit_bytes=16 * 2**20
        ),
    )(rhs, material, level, mortar, mu, lam, inverse)


def solution(mesh):
    return jax.shard_map(
        per_device,
        mesh=mesh,
        in_specs=(
            P(None, "bricks", "group", None),
            P("bricks", "group", None),
            P("bricks", "group"),
            P("bricks", "group", None),
            P(),
            P(),
            P("bricks", None, None),
        ),
        out_specs=(P(None, "bricks", "group", None), P(None, "bricks", "group", None)),
        check_vma=False,
    )
```

```python
import functools

import jax
import jax.numpy as jnp
from jax import lax
from jax.experimental import pallas as pl
from jax.experimental.pallas import tpu as pltpu
from jax.sharding import PartitionSpec as P

BLOCK_Z = 32
CHEB = 4
LOW_RATIO = 0.15
BOUND_MARGIN = 1.1
ROUNDS = 4
UNROLL = 4
DEPTH = 2
SWEEP = 7
INNER = 6
HIGHEST = lax.Precision.HIGHEST


def kernel(
    nb, ng, dx, dy, dz,
    rhs_in, material_in, level, mortar, mu, lam, inverse_in,
    sol, res, rhs, material, inverse,
    u, r, shear, wx, wyp, wym, wzp, wzm, dg, hb, invd, coef,
    s_send_up, s_send_y, s_recv, static_send, static_recv, index_send, index_recv, index,
    faces, mixed, y_send, corner_send, recv_x, recv_y, recv_d, ghost, gy, before,
    pack_send, pack_recv, corner_pack, recv_k, corner_rows, spread_k,
    m_own, m_all, m2_own, m2_all, c_own, c_all, f_all, inv_recv, in_sem,
    s_ssem, s_rsem, t_ssem, t_rsem, h_ssem, h_rsem, p_ssem, p_rsem,
    m_ssem, m_rsem, m2_ssem, m2_rsem, c_ssem, c_rsem, i_ssem, i_rsem,
):
    b = lax.axis_index("bricks")
    g = lax.axis_index("group")
    has = [b > 0, b < nb - 1, g > 0, g < ng - 1]
    sends = [has[1], has[0], has[3], has[2]]
    peers = [(b + 1, g), (b - 1, g), (b, g + 1), (b, g - 1)]
    corners = [(0, 0), (0, 1), (1, 0), (1, 1)]
    has_corner = [has[sx] & has[2 + sy] for sx, sy in corners]
    corner_peer = [(b + 2 * sx - 1, g + 2 * sy - 1) for sx, sy in corners]

    def remote(src, dst, ssem, rsem, peer):
        return pltpu.make_async_remote_copy(
            src_ref=src, dst_ref=dst, send_sem=ssem, recv_sem=rsem,
            device_id=peer, device_id_type=pl.DeviceIdType.MESH,
        )

    barrier = pltpu.get_barrier_semaphore()
    others = [(b, lax.rem(g + k, ng)) for k in range(1, ng)]
    others += [(lax.rem(b + k, nb), g) for k in range(1, nb)]
    around = [(lax.rem(g + k, ng)) for k in range(1, ng)]
    for peer in others:
        pl.semaphore_signal(
            barrier, inc=1, device_id=peer, device_id_type=pl.DeviceIdType.MESH
        )
    for d in range(2):
        @pl.when(has[d])
        def _():
            for at in around:
                pl.semaphore_signal(
                    barrier, inc=1, device_id=(b - 1 + 2 * d, at),
                    device_id_type=pl.DeviceIdType.MESH,
                )

    def fetch(k):
        source = [material_in, rhs_in, inverse_in.at[0]][k]
        return pltpu.make_async_copy(source, [material, rhs, inverse][k], in_sem.at[k])

    for k in range(3):
        fetch(k).start()

    row = lax.broadcasted_iota(jnp.int32, (dy, dz), 0)
    lane = lax.broadcasted_iota(jnp.int32, (dy, dz), 1)
    grade = jnp.broadcast_to(level[...], (dy, dz))
    scale = jnp.where(grade == 0, 1.0, jnp.where(grade == 1, 4.0, 16.0))
    zero_face = jnp.zeros((dy, dz), jnp.float32)

    order = [mortar[0, 0, k] for k in range(dy)]
    order_here = jnp.zeros((dy, dz), jnp.int32)
    undo_here = jnp.zeros((dy, dz), jnp.int32)
    for k in range(dy):
        order_here = jnp.where(row == k, order[k], order_here)
        undo_here = jnp.where(row == order[k], k, undo_here)
    index_send[...] = order_here
    index[0] = order_here
    index[1] = undo_here

    def permute(value, k):
        half = dy // 2
        parts = []
        for h in range(2):
            at = index[k, h * half : (h + 1) * half]
            within = jnp.bitwise_and(at, half - 1)
            low = jnp.take_along_axis(value[:half], within, axis=0)
            high = jnp.take_along_axis(value[half:], within, axis=0)
            parts.append(jnp.where(at < half, low, high))
        return jnp.concatenate(parts, axis=0)

    def lookup(ids, table):
        total = jnp.where(ids == 0, table[0], 0.0)
        for entry in range(1, 4):
            total = jnp.where(ids == entry, table[entry], total)
        return total * scale

    def shear_plane(i, _):
        ids = material[i]
        plane = lookup(ids, mu)
        bulk = lookup(ids, lam)
        shear[i + 1] = plane
        hb[i] = bulk
        s_send_y[0, pl.ds(i, 1), :] = plane[dy - 1 : dy]
        s_send_y[1, pl.ds(i, 1), :] = plane[0:1]
        for d, near, far in ((2, dy - 1, dy - 2), (3, 0, 1)):
            static_send[d, 0, pl.ds(i, 1), :] = plane[near : near + 1]
            static_send[d, 1, pl.ds(i, 1), :] = plane[far : far + 1]
            static_send[d, 2, pl.ds(i, 1), :] = bulk[near : near + 1]
        return 0

    fetch(0).wait()
    lax.fori_loop(0, dx, shear_plane, 0, unroll=UNROLL)
    s_send_up[...] = permute(shear[dx], 0)
    for d, near, far in ((0, dx - 1, dx - 2), (1, 0, 1)):
        static_send[d, 0] = shear[near + 1]
        static_send[d, 1] = shear[far + 1]
        static_send[d, 2] = hb[near]

    both = jnp.where(has[0], len(around), 0) + jnp.where(has[1], len(around), 0)
    pl.semaphore_wait(barrier, len(others) + both)

    def s_copy(d):
        src = [s_send_up, shear.at[1], s_send_y.at[0], s_send_y.at[1]][d]
        return remote(src, s_recv.at[d], s_ssem.at[d], s_rsem.at[d], peers[d])

    def t_copy(d):
        if d == 4:
            return remote(index_send, index_recv, t_ssem.at[4], t_rsem.at[4], peers[0])
        return remote(
            static_send.at[d], static_recv.at[d], t_ssem.at[d], t_rsem.at[d], peers[d]
        )

    def exchange_start(copy, directions=(0, 1, 2, 3)):
        for d in directions:
            @pl.when(sends[d % 4])
            def _():
                copy(d).start()

    def arrive_wait(copy, directions=(0, 1, 2, 3)):
        for d in directions:
            @pl.when(has[d % 4])
            def _():
                copy(d).wait_recv()

    def sent_wait(copy, directions=(0, 1, 2, 3)):
        for d in directions:
            @pl.when(sends[d % 4])
            def _():
                copy(d).wait_send()

    def exchange_wait(copy, directions=(0, 1, 2, 3)):
        arrive_wait(copy, directions)
        sent_wait(copy, directions)

    exchange_start(s_copy)
    exchange_start(t_copy, (4, 0, 1, 2, 3))

    @pl.when(b == 0)
    def _():
        s_recv[0] = shear[1]
        index_recv[...] = row

    @pl.when(b == nb - 1)
    def _():
        s_recv[1] = shear[dx]

    @pl.when(g == 0)
    def _():
        s_recv[2] = s_send_y[1]

    @pl.when(g == ng - 1)
    def _():
        s_recv[3] = s_send_y[0]

    for d in range(4):
        @pl.when(jnp.logical_not(has[d]))
        def _():
            one = jnp.ones((dy, dz), jnp.float32)
            for k in range(3):
                static_recv[d, k] = one
                pack_recv[d, k] = zero_face
            for turn in range(ROUNDS):
                for c in range(3):
                    for j in range(2):
                        if d < 2:
                            recv_x[turn, d, c, j] = zero_face
                        else:
                            recv_y[turn, d - 2, j, c] = zero_face
            if d < 2:
                inv_recv[d] = jnp.zeros(inv_recv.shape[1:], jnp.float32)
                c_all[2 * d] = jnp.zeros(c_all.shape[1:], jnp.float32)

    for k in range(4):
        @pl.when(jnp.logical_not(has_corner[k]))
        def _():
            for turn in range(ROUNDS):
                recv_d[turn, k] = jnp.zeros(recv_d.shape[2:], jnp.float32)
            recv_k[k] = jnp.zeros(recv_k.shape[1:], jnp.float32)

    fetch(1).wait()
    fetch(2).wait()
    exchange_wait(s_copy)
    shear[0] = s_recv[0]

    @pl.when(b < nb - 1)
    def _():
        shear[dx + 1] = permute(s_recv[1], 1)

    @pl.when(b == nb - 1)
    def _():
        shear[dx + 1] = shear[dx]

    def rows_near(v, low, high):
        m = jnp.where(row == 0, jnp.broadcast_to(low, v.shape), pltpu.roll(v, 1, 0))
        p = jnp.where(
            row == dy - 1, jnp.broadcast_to(high, v.shape), pltpu.roll(v, dy - 1, 0)
        )
        return m, p

    def z_near(v):
        return pltpu.roll(v, 1, 1), pltpu.roll(v, dz - 1, 1)

    def h_copy(turn, slot):
        deep = DEPTH

        def copy(d):
            if d == 0:
                src = u.at[slot, :, dx + 1 - deep : dx + 1]
                dst = recv_x.at[turn, 0, :, 2 - deep : 2]
            elif d == 1:
                src = u.at[slot, :, 1 : 1 + deep]
                dst = recv_x.at[turn, 1, :, 0:deep]
            else:
                src = y_send.at[turn, d - 2, 0:deep]
                dst = recv_y.at[turn, d - 2, 0:deep]
            return remote(src, dst, h_ssem.at[turn, d], h_rsem.at[turn, d], peers[d])
        return copy

    def corner_copy(turn, k):
        return remote(
            corner_send.at[turn, k], recv_d.at[turn, 3 - k],
            h_ssem.at[turn, 4 + k], h_rsem.at[turn, 7 - k], corner_peer[k],
        )

    def corner_arrival(turn, k):
        return remote(
            corner_send.at[turn, k], recv_d.at[turn, k],
            h_ssem.at[turn, 4 + k], h_rsem.at[turn, 4 + k], corner_peer[k],
        )

    even = lax.rem(b, 2) == 0

    def send_faces(turn, slot):
        copy = h_copy(turn, slot)

        @pl.when(sends[1] & even)
        def _():
            copy(1).start()

        exchange_start(copy, (0,))

        @pl.when(sends[1] & jnp.logical_not(even))
        def _():
            copy(1).start()

        for c in range(3):
            bottom, top = u[slot, c, 1], u[slot, c, dx]
            mixed_low, mixed_high = permute(bottom, 3), permute(top, 0)
            mixed[0, c] = mixed_low
            mixed[1, c] = mixed_high
            for k, (sx, sy) in enumerate(corners):
                y = (dy - 1) * sy
                plane, other = ((bottom, mixed_low), (top, mixed_high))[sx]
                corner_send[turn, k, c : c + 1, :] = plane[y : y + 1]
                corner_send[turn, k, 3 + c : 4 + c, :] = other[y : y + 1]
        for k in range(4):
            @pl.when(has_corner[k])
            def _():
                corner_copy(turn, k).start()

    def send_rows(turn, slot):
        exchange_start(h_copy(turn, slot), (2, 3))

    def store_rows(turn, c, i, value):
        y_send[turn, 0, 0, c, pl.ds(i, 1), :] = value[dy - 1 : dy]
        y_send[turn, 1, 0, c, pl.ds(i, 1), :] = value[0:1]
        y_send[turn, 0, 1, c, pl.ds(i, 1), :] = value[dy - 2 : dy - 1]
        y_send[turn, 1, 1, c, pl.ds(i, 1), :] = value[1:2]

    def corners_wait(turn):
        for k in range(4):
            @pl.when(has_corner[k])
            def _():
                corner_arrival(turn, k).wait_recv()
        for k in range(4):
            @pl.when(has_corner[k])
            def _():
                corner_copy(turn, k).wait_send()

    def nearest(turn, s, c):
        return recv_x[turn, s, c, 1 - s]

    def place_faces(turn, slot):
        for c in range(3):
            u[slot, c, 0] = permute(nearest(turn, 0, c), 2)
            u[slot, c, dx + 1] = permute(nearest(turn, 1, c), 1)

    def sweep_send(plane, turn, slot, carry):
        for i in range(DEPTH):
            carry = plane(i, carry)
            carry = plane(dx - 1 - i, carry)
        send_faces(turn, slot)
        carry = lax.fori_loop(DEPTH, dx - DEPTH, plane, carry, unroll=INNER)
        send_rows(turn, slot)
        return carry

    def sweep_receive(plane, turn, slot, carry, faces_done):
        exchange_wait(h_copy(turn, slot), (2, 3))
        carry = lax.fori_loop(1, dx - 1, plane, carry, unroll=SWEEP)
        exchange_wait(h_copy(turn, slot), (0, 1))
        corners_wait(turn)
        place_faces(turn, slot)
        faces_done()
        carry = plane(0, carry)
        carry = plane(dx - 1, carry)
        return carry

    wx[0] = 0.5 * (shear[0] + shear[1])
    wx[dx] = 0.5 * (shear[dx] + shear[dx + 1])

    exchange_wait(t_copy, (4,))
    index[2] = index_recv[...]
    undo_below = jnp.zeros((dy, dz), jnp.int32)
    for k in range(dy):
        at = jnp.broadcast_to(index_recv[k : k + 1, :], (dy, dz))
        undo_below = jnp.where(row == at, k, undo_below)
    index[3] = undo_below

    def weight_plane(i, best):
        s = shear[i + 1]
        xp = 0.5 * (s + shear[i + 2])
        wx[i + 1] = xp
        xm = 0.5 * (s + shear[i])
        ym, yp = rows_near(s, s_recv[2, pl.ds(i, 1), :], s_recv[3, pl.ds(i, 1), :])
        ym = 0.5 * (s + ym)
        yp = 0.5 * (s + yp)
        zm, zp = z_near(s)
        zm = 0.5 * (s + zm)
        zp = 0.5 * (s + zp)
        wyp[i] = yp
        wym[i] = ym
        wzp[i] = jnp.where(lane == dz - 1, 0.0, zp)
        wzm[i] = jnp.where(lane == 0, 0.0, zm)
        total = xp + xm + yp + ym + jnp.where(lane == dz - 1, s, zp) + jnp.where(lane == 0, s, zm)
        bulk = hb[i]
        diagonal = total + 1.5 * bulk
        inv = 1.0 / diagonal
        invd[i] = inv
        dg[i] = total + bulk
        hb[i] = 0.5 * bulk
        for c in range(3):
            d0 = rhs[c, i] * inv
            u[0, c, i + 1] = d0
            store_rows(0, c, i, d0)
        return jnp.maximum(best, (2.0 * total + 2.5 * bulk) / diagonal)

    below_shear = permute(shear[1], 3)
    faces[0] = below_shear
    for k, (sx, sy) in enumerate(corners):
        y = (dy - 1) * sy
        plane = shear[(1, dx)[sx]]
        other = (below_shear, s_send_up[...])[sx]
        corner_send[0, k, 6:7, :] = plane[y : y + 1]
        corner_send[0, k, 7:8, :] = other[y : y + 1]

    best = sweep_send(weight_plane, 0, 0, jnp.zeros((dy, dz), jnp.float32))
    m_own[...] = jnp.broadcast_to(jnp.max(best, axis=0, keepdims=True), m_own.shape)

    def apply_plane(i, slot, low, high):
        v = [u[slot, c, i + 1] for c in range(3)]
        coupled = hb[i] * (v[0] + v[1] + v[2])
        out = []
        for c in range(3):
            ym, yp = rows_near(v[c], low(c, i), high(c, i))
            zm, zp = z_near(v[c])
            near = wx[i] * u[slot, c, i] + wx[i + 1] * u[slot, c, i + 2]
            near = near + wym[i] * ym + wyp[i] * yp + wzm[i] * zm + wzp[i] * zp
            out.append(dg[i] * v[c] + coupled - near)
        return v, out

    def recv_rows(turn):
        return (
            lambda c, i: recv_y[turn, 0, 0, c, pl.ds(i, 1), :],
            lambda c, i: recv_y[turn, 1, 0, c, pl.ds(i, 1), :],
        )

    ghost_rows = (
        lambda c, i: gy[0, c, pl.ds(i, 1), :],
        lambda c, i: gy[1, c, pl.ds(i, 1), :],
    )

    def bcoef(k):
        return jnp.broadcast_to(coef[k : k + 1, :], (dy, dz))

    def ghost_weights(d, cross, low, high):
        near, far, bulk = [static_recv[d, k] for k in range(3)]
        inner = 0.5 * (near + far)
        across = 0.5 * (near + cross)
        rm, rp = rows_near(near, low, high)
        rm = 0.5 * (near + rm)
        rp = 0.5 * (near + rp)
        zm, zp = z_near(near)
        zm = 0.5 * (near + zm)
        zp = 0.5 * (near + zp)
        total = inner + across + rm + rp
        total = total + jnp.where(lane == dz - 1, near, zp) + jnp.where(lane == 0, near, zm)
        inv = jnp.where(has[d], 1.0, 0.0) / (total + 1.5 * bulk)
        zm = jnp.where(lane == 0, 0.0, zm)
        zp = jnp.where(lane == dz - 1, 0.0, zp)
        for k, value in enumerate(
            (inner, across, rm, rp, zm, zp, total + bulk, 0.5 * bulk, inv)
        ):
            ghost[d, k] = value

    def all_ghost_weights():
        def edge(inside, corner, at, own):
            return jnp.where(inside, recv_d[0, corner, at : at + 1, :], own)

        for d in range(4):
            s = d % 2
            near = static_recv[d, 0]
            ends = near[0:1], near[dy - 1 : dy]
            if d < 2:
                cross = (faces[0], s_send_up[...])[s]
                low = edge(has[2], 2 * s, 6, ends[0])
                high = edge(has[3], 2 * s + 1, 6, ends[1])
            else:
                cross = s_send_y[1 - s]
                low = edge(has[0], s, 7, ends[0])
                high = edge(has[1], 2 + s, 7, ends[1])
            ghost_weights(d, cross, low, high)

    def ghost_apply(d, v, inner, cross, low, high):
        w = [ghost[d, k] for k in range(9)]
        coupled = w[7] * (v[0] + v[1] + v[2])
        out = []
        for c in range(3):
            rm, rp = rows_near(v[c], low[c], high[c])
            zm, zp = z_near(v[c])
            near = w[0] * inner[c] + w[1] * cross[c] + w[2] * rm + w[3] * rp
            near = near + w[4] * zm + w[5] * zp
            out.append(w[8] * (w[6] * v[c] + coupled - near))
        return out

    def ghost_step(turn, other, update):
        for d in range(4):
            s = d % 2
            if d < 2:
                v = [nearest(turn, s, c) for c in range(3)]
                inner = [recv_x[turn, s, c, s] for c in range(3)]
                cross = [mixed[s, c] for c in range(3)]
                low = [recv_d[turn, 2 * s, c : c + 1, :] for c in range(3)]
                high = [recv_d[turn, 2 * s + 1, c : c + 1, :] for c in range(3)]
            else:
                v = [recv_y[turn, s, 0, c] for c in range(3)]
                inner = [recv_y[turn, s, 1, c] for c in range(3)]
                cross = [y_send[turn, 1 - s, 0, c] for c in range(3)]
                low = [recv_d[turn, s, 3 + c : 4 + c, :] for c in range(3)]
                high = [recv_d[turn, 2 + s, 3 + c : 4 + c, :] for c in range(3)]
            out = ghost_apply(d, v, inner, cross, low, high)
            for c in range(3):
                new = update(d, c, v[c], out[c])
                if d < 2:
                    u[other, c, (dx + 1) * s] = permute(new, 2 - s)
                else:
                    gy[s, c] = new

    def ring_start(own, store, ssem, rsem, peer_of, count, mine):
        copies = []
        for k in range(1, count):
            copies.append(remote(own, store.at[k], ssem.at[k], rsem.at[k], peer_of(k)))
        for copy in copies:
            copy.start()
        return copies

    group_peer = lambda k: (b, lax.rem(g + k, ng))
    brick_peer = lambda k: (lax.rem(b + k, nb), g)

    m_copies = ring_start(m_own, m_all, m_ssem, m_rsem, group_peer, ng, g)
    top = m_own[...]
    for k, copy in enumerate(m_copies):
        copy.wait()
        top = jnp.maximum(top, m_all[k + 1])
    m2_own[...] = top
    m2_copies = ring_start(m2_own, m2_all, m2_ssem, m2_rsem, brick_peer, nb, b)

    for d in range(2):
        i = (dx - 2, 1)[d]
        pack_send[d, 0] = invd[i]
        pack_send[d, 1] = hb[i]
        pack_send[d, 2] = jnp.where(row == 0, wym[i], jnp.where(row == dy - 1, wyp[i], 0.0))
    for d, y in ((2, dy - 2), (3, 1)):
        pack_send[d, 2] = zero_face
        pack_send[d, 2, 0:1, :] = wx[0, y : y + 1, :]
        pack_send[d, 2, dx - 1 : dx, :] = wx[dx, y : y + 1, :]
        for i in range(dx):
            pack_send[d, 0, i : i + 1, :] = invd[i, y : y + 1, :]
            pack_send[d, 1, i : i + 1, :] = hb[i, y : y + 1, :]
    for sx in range(2):
        i = (dx - 1) * sx
        values = (
            invd[i], hb[i], wx[dx * sx],
            jnp.where(row == 0, wym[i], 0.0), jnp.where(row == dy - 1, wyp[i], 0.0),
            shear[i + 1],
        )
        for k, value in enumerate(values):
            other = permute(value, (3, 0)[sx])
            for sy in range(2):
                y = (dy - 1) * sy
                corner_pack[2 * sx + sy, k : k + 1, :] = value[y : y + 1]
                corner_pack[2 * sx + sy, 8 + k : 9 + k, :] = other[y : y + 1]

    def p_copy(d):
        return remote(
            pack_send.at[d], pack_recv.at[d], p_ssem.at[d], p_rsem.at[d], peers[d]
        )

    def k_copy(k, at):
        return remote(
            corner_pack.at[k], recv_k.at[at], p_ssem.at[4 + k], p_rsem.at[4 + at],
            corner_peer[k],
        )

    exchange_start(p_copy)
    for k in range(4):
        @pl.when(has_corner[k])
        def _():
            k_copy(k, 3 - k).start()
    exchange_wait(t_copy)

    low, high = recv_rows(0)

    def first_plane(i, _):
        _, out = apply_plane(i, 0, low, high)
        inv = invd[i]
        for c in range(3):
            r[c, i] = out[c]
            u[1, c, i + 1] = out[c] * inv
        return 0

    def first_ghosts():
        all_ghost_weights()

        def update(d, c, v, out):
            before[d, c] = out
            return out

        ghost_step(0, 1, update)

    sweep_receive(first_plane, 0, 0, 0, first_ghosts)

    def second_plane(i, _):
        _, out = apply_plane(i, 1, *ghost_rows)
        for c in range(3):
            res[c, i] = out[c]
        return 0

    lax.fori_loop(0, dx, second_plane, 0, unroll=8)

    for k, copy in enumerate(m2_copies):
        copy.wait()
        top = jnp.maximum(top, m2_all[k + 1])
    upper = BOUND_MARGIN * jnp.broadcast_to(jnp.max(top, axis=1, keepdims=True), top.shape)
    lower = LOW_RATIO * upper
    theta = 0.5 * (upper + lower)
    delta = 0.5 * (upper - lower)
    sigma = theta / delta
    damping = 1.0 / sigma
    inv_theta = 1.0 / theta
    coef[0:8] = inv_theta
    rows = []
    for turn in range(1, CHEB):
        following = 1.0 / (2.0 * sigma - damping)
        rows.append((following * damping, 2.0 * following / delta))
        damping = following
    for turn, (a, c2) in enumerate(rows):
        coef[8 + 2 * turn : 9 + 2 * turn] = a[0:1]
        coef[9 + 2 * turn : 10 + 2 * turn] = c2[0:1]
    coef[14:15] = (rows[0][0] * inv_theta + rows[0][1])[0:1]
    coef[15:16] = (rows[0][1] * inv_theta)[0:1]
    (a, c2), (a_next, c_next) = rows[1], rows[2]
    ratio = c_next / c2
    coef[16:17] = (a_next + ratio)[0:1]
    coef[17:18] = (ratio * a)[0:1]
    coef[18:19] = (rows[0][0] + rows[0][1] * theta)[0:1]

    alpha, beta, it = bcoef(14), bcoef(15), bcoef(0)
    both_it = alpha + it
    a_two, c_two = bcoef(10), bcoef(11)

    def combine_plane(i, _):
        inv = invd[i]
        for c in range(3):
            d0 = u[0, c, i + 1]
            one = alpha * d0 - beta * u[1, c, i + 1]
            sol[c, i] = it * d0 + one
            rest = rhs[c, i] - both_it * r[c, i] + beta * res[c, i]
            res[c, i] = rest
            two = a_two * one + c_two * (rest * inv)
            u[0, c, i + 1] = two
            store_rows(1, c, i, two)
        return 0

    sweep_send(combine_plane, 1, 0, 0)
    for d in range(4):
        for c in range(3):
            v = nearest(0, d, c) if d < 2 else recv_y[0, d - 2, 0, c]
            before[d, c] = alpha * v - beta * before[d, c]

    def step_plane(slot, low, high, a, c2, following, summed=False, rows_of=None):
        other = 1 - slot

        def plane(i, sums):
            v, out = apply_plane(i, slot, low, high)
            inv = invd[i]
            new = []
            for c in range(3):
                rest = res[c, i] - out[c]
                res[c, i] = rest
                sol[c, i] = sol[c, i] + v[c]
                if summed:
                    new.append(sums[c] + rest)
                if not following:
                    continue
                ahead = c2 * (rest * inv)
                if a is not None:
                    ahead = ahead + a * v[c]
                u[other, c, i + 1] = ahead
                if rows_of is not None:
                    store_rows(rows_of, c, i, ahead)
            return tuple(new)
        return plane

    def pair_ghosts(turn, other):
        def done():
            e1, e2, e3 = bcoef(16), bcoef(17), bcoef(13)

            def update(d, c, v, out):
                return e1 * v - e2 * before[d, c] - e3 * out

            ghost_step(turn, other, update)
        return done

    def i_copy(d):
        return remote(inverse, inv_recv.at[d], i_ssem.at[d], i_rsem.at[d], peers[d])

    exchange_start(i_copy, (0, 1))
    plane = step_plane(0, *recv_rows(1), bcoef(12), bcoef(13), True)
    sweep_receive(plane, 1, 0, (), pair_ghosts(1, 1))
    plane = step_plane(1, *ghost_rows, None, bcoef(0), True, summed=True, rows_of=2)
    init = tuple(jnp.zeros((dy, dz), jnp.float32) for _ in range(3))
    sums = sweep_send(plane, 2, 0, init)

    c_own[...] = jnp.zeros(c_own.shape, jnp.float32)
    for c in range(3):
        c_own[c : c + 1, :] = jnp.sum(sums[c], axis=0, keepdims=True)
    c_all[1, g] = c_own[...]

    def c_copy(q, k):
        slot = q * ng + k
        return remote(
            c_own, c_all.at[q, g], c_ssem.at[slot], c_rsem.at[slot],
            (b + 1 - q, lax.rem(g + k, ng)),
        )

    def c_arrival(q, k):
        slot = q * ng + k
        source = lax.rem(g + ng - k, ng)
        return remote(
            c_own, c_all.at[q, source], c_ssem.at[slot], c_rsem.at[slot],
            (b + 1 - q, lax.rem(g + k, ng)),
        )

    def coarse_all(to_do, flags):
        for q in (0, 2, 1):
            first = 1 if q == 1 else 0
            if q == 1:
                for k in range(first, ng):
                    to_do(q, k)
                continue

            @pl.when(flags[q])
            def _():
                for k in range(first, ng):
                    to_do(q, k)

    coarse_all(lambda q, k: c_copy(q, k).start(), {0: has[1], 2: has[0]})
    f_all[...] = jnp.zeros(f_all.shape, jnp.float32)
    exchange_wait(p_copy)
    for k in range(4):
        @pl.when(has_corner[k])
        def _():
            k_copy(k, k).wait_recv()
    for k in range(4):
        @pl.when(has_corner[k])
        def _():
            k_copy(k, k).wait_send()
    for k in range(4):
        for n in range(6):
            for side in range(2):
                at = 2 * k + side
                corner_rows[n, at : at + 1, :] = recv_k[k, 8 * side + n : 8 * side + n + 1, :]
    exchange_wait(i_copy, (0, 1))
    coarse_all(lambda q, k: c_arrival(q, k).wait_recv(), {0: has[0], 2: has[1]})
    coarse_all(lambda q, k: c_copy(q, k).wait_send(), {0: has[1], 2: has[0]})

    cells_z = dz // BLOCK_Z
    size = 3 * cells_z * ng
    flat = c_all[...].reshape(3 * ng * 8, dz)
    li = lax.broadcasted_iota(jnp.int32, (dz, size), 0)
    ki = lax.broadcasted_iota(jnp.int32, (dz, size), 1)
    gather = jnp.where(li // BLOCK_Z == ki % cells_z, 1.0 / (dx * dy * BLOCK_Z), 0.0)
    spread = jnp.dot(flat, gather, precision=HIGHEST, preferred_element_type=jnp.float32)
    ri = lax.broadcasted_iota(jnp.int32, (ng * 8, size), 0)
    kk = lax.broadcasted_iota(jnp.int32, (ng * 8, size), 1) // cells_z
    mine = (ri // 8 == kk // 3) & (ri % 8 == kk % 3)
    bi = lax.broadcasted_iota(jnp.int32, (size, dz), 0)
    bl = lax.broadcasted_iota(jnp.int32, (size, dz), 1)
    placed = bi % cells_z == bl // BLOCK_Z
    for q in range(3):
        part = spread[q * ng * 8 : (q + 1) * ng * 8]
        vector = jnp.sum(jnp.where(mine, part, 0.0), axis=0, keepdims=True)
        matrix = inverse[...] if q == 1 else inv_recv[q // 2]
        correction = jnp.sum(matrix * vector, axis=1, keepdims=True)
        table = jnp.where(placed, jnp.broadcast_to(correction, (size, dz)), 0.0)
        for k in range(ng):
            for c in range(3):
                start = (k * 3 + c) * cells_z
                f_all[q, k + 1, c : c + 1, :] = jnp.sum(
                    table[start : start + cells_z], axis=0, keepdims=True
                )

    def full(q, at, c):
        return jnp.broadcast_to(f_all[q, at, c : c + 1, :], (dy, dz))

    own_fine = [full(1, g + 1, c) for c in range(3)]

    fine_sides = [z_near(own_fine[c]) for c in range(3)]
    fine_rows = [
        (
            jnp.where(row == 0, full(1, g, c), own_fine[c]),
            jnp.where(row == dy - 1, full(1, g + 2, c), own_fine[c]),
        )
        for c in range(3)
    ]
    fine_sum = own_fine[0] + own_fine[1] + own_fine[2]
    it = bcoef(0)

    def fine_plane(i, _):
        inv = invd[i]
        coupled = hb[i] * fine_sum
        for c in range(3):
            f = own_fine[c]
            first, last = isinstance(i, int) and i == 0, isinstance(i, int) and i == dx - 1
            xm = full(0, g + 1, c) if first else f
            xp = full(2, g + 1, c) if last else f
            near = wx[i] * xm + wx[i + 1] * xp
            near = near + wym[i] * fine_rows[c][0] + wyp[i] * fine_rows[c][1]
            near = near + wzm[i] * fine_sides[c][0] + wzp[i] * fine_sides[c][1]
            rest = res[c, i] - (dg[i] * f + coupled - near)
            res[c, i] = rest
            sol[c, i] = sol[c, i] + f
            ahead = it * (rest * inv)
            u[0, c, i + 1] = ahead
            y_send[2, 0, 0, c, pl.ds(i, 1), :] = ahead[dy - 1 : dy]
            y_send[2, 1, 0, c, pl.ds(i, 1), :] = ahead[0:1]
        return 0

    exchange_wait(h_copy(2, 0))
    corners_wait(2)
    fine_plane(0, 0)
    fine_plane(dx - 1, 0)
    lax.fori_loop(1, dx - 1, fine_plane, 0, unroll=SWEEP)
    for c in range(3):
        mixed[0, c] = permute(u[0, c, 1], 3)
        mixed[1, c] = permute(u[0, c, dx], 0)

    def fine_far(here, low, high, inv, half, w_low, w_high, near, across=None):
        lanes = lane[: near.shape[0]]
        zm, zp = z_near(near)
        zm = jnp.where(lanes == 0, 0.0, 0.5 * (near + zm))
        zp = jnp.where(lanes == dz - 1, 0.0, 0.5 * (near + zp))
        rim = jnp.where((lanes == 0) | (lanes == dz - 1), near, 0.0)
        weight = 2.0 * half + w_low + w_high + zm + zp + rim
        if across is not None:
            weight = weight + across[0]
        coupled = half * (here[0] + here[1] + here[2])
        out = []
        for c in range(3):
            fm, fp = z_near(here[c])
            value = weight * here[c] + coupled - zm * fm - zp * fp
            value = value - w_low * low[c] - w_high * high[c]
            if across is not None:
                value = value - across[0] * across[1][c]
            out.append(inv * value)
        return out

    for d in range(4):
        s = d % 2
        if d < 2:
            spots = (2 * s, g + 1), (2 * s, g), (2 * s, g + 2)
        else:
            at = g + 2 * s
            spots = (1, at), (0, at), (2, at)
        here, low, high = [[full(*spot, c) for c in range(3)] for spot in spots]
        out = ghost_apply(d, here, here, own_fine, low, high)
        inv, half, rim = [pack_recv[d, k] for k in range(3)]
        w_low = jnp.where(row == 0, rim, 0.0)
        w_high = jnp.where(row == dy - 1, rim, 0.0)
        far = fine_far(here, low, high, inv, half, w_low, w_high, static_recv[d, 1])
        for c in range(3):
            if d < 2:
                recv_x[2, s, c, 1 - s] = nearest(2, s, c) - it * out[c]
                recv_x[2, s, c, s] = recv_x[2, s, c, s] - it * far[c]
            else:
                recv_y[2, s, 0, c] = recv_y[2, s, 0, c] - it * out[c]
                recv_y[2, s, 1, c] = recv_y[2, s, 1, c] - it * far[c]

    for k, (sx, sy) in enumerate(corners):
        q, at = 2 * sx, g + 2 * sy
        spots = (q, at), (q, jnp.maximum(at - 1, 0)), (q, jnp.minimum(at + 1, ng + 1)), (1, at)
        for n, spot in enumerate(spots):
            for c in range(3):
                value = f_all[(*spot, slice(c, c + 1))]
                spread_k[n, c, 2 * k : 2 * k + 1, :] = value
                spread_k[n, c, 2 * k + 1 : 2 * k + 2, :] = value
        for c in range(3):
            for n in range(2):
                at = 2 * k + n
                spread_k[4, c, at : at + 1, :] = recv_d[2, k, 3 * n + c : 3 * n + c + 1, :]
    here, low, high, beside = [[spread_k[n, c] for c in range(3)] for n in range(4)]
    inv, half, cross, w_low, w_high, near = [corner_rows[n] for n in range(6)]
    out = fine_far(here, low, high, inv, half, w_low, w_high, near, (cross, beside))
    for c in range(3):
        spread_k[4, c] = spread_k[4, c] - it[0:8] * out[c]
    for k in range(4):
        for c in range(3):
            for n in range(2):
                at = 2 * k + n
                recv_d[2, k, 3 * n + c : 3 * n + c + 1, :] = spread_k[4, c, at : at + 1, :]

    place_faces(2, 0)
    e1, e3 = bcoef(18), bcoef(9)

    def first_update(d, c, v, out):
        new = e1 * v - e3 * out
        before[d, c] = new
        return new

    ghost_step(2, 1, first_update)
    plane = step_plane(0, *recv_rows(2), bcoef(8), bcoef(9), True)
    lax.fori_loop(0, dx, plane, (), unroll=8)
    plane = step_plane(1, *ghost_rows, bcoef(10), bcoef(11), True, rows_of=3)
    sweep_send(plane, 3, 0, ())
    plane = step_plane(0, *recv_rows(3), bcoef(12), bcoef(13), True)
    sweep_receive(plane, 3, 0, (), pair_ghosts(3, 1))
    plane = step_plane(1, *ghost_rows, None, None, False)
    lax.fori_loop(0, dx, plane, (), unroll=8)


def per_device(rhs, material, level, mortar, mu, lam, inverse):
    nb = lax.axis_size("bricks")
    ng = lax.axis_size("group")
    dx, dy, dz = material.shape
    f32 = jnp.float32
    vmem = pl.BlockSpec(memory_space=pltpu.VMEM)
    smem = pl.BlockSpec(memory_space=pltpu.SMEM)
    hbm = pl.BlockSpec(memory_space=pltpu.HBM)
    dma = pltpu.SemaphoreType.DMA
    grid = pltpu.VMEM((dx, dy, dz), f32)
    cg = inverse.shape[1]
    scratch = [
        pltpu.VMEM((3, dx, dy, dz), f32),
        pltpu.VMEM((dx, dy, dz), jnp.int32),
        pltpu.VMEM((cg, cg), f32),
        pltpu.VMEM((2, 3, dx + 2, dy, dz), f32),
        pltpu.VMEM((3, dx, dy, dz), f32),
        pltpu.VMEM((dx + 2, dy, dz), f32),
        pltpu.VMEM((dx + 1, dy, dz), f32),
        grid, grid, grid, grid, grid, grid, grid,
        pltpu.VMEM((24, dz), f32),
        pltpu.VMEM((dy, dz), f32),
        pltpu.VMEM((2, dx, dz), f32),
        pltpu.VMEM((4, dx, dz), f32),
        pltpu.VMEM((4, 3, dx, dz), f32),
        pltpu.VMEM((4, 3, dx, dz), f32),
        pltpu.VMEM((dy, dz), jnp.int32),
        pltpu.VMEM((dy, dz), jnp.int32),
        pltpu.VMEM((4, dy, dz), jnp.int32),
        pltpu.VMEM((1, dy, dz), f32),
        pltpu.VMEM((2, 3, dy, dz), f32),
        pltpu.VMEM((ROUNDS, 2, 2, 3, dx, dz), f32),
        pltpu.VMEM((ROUNDS, 4, 8, dz), f32),
        pltpu.VMEM((ROUNDS, 2, 3, 2, dy, dz), f32),
        pltpu.VMEM((ROUNDS, 2, 2, 3, dx, dz), f32),
        pltpu.VMEM((ROUNDS, 4, 8, dz), f32),
        pltpu.VMEM((4, 9, dy, dz), f32),
        pltpu.VMEM((2, 3, dx, dz), f32),
        pltpu.VMEM((4, 3, dy, dz), f32),
        pltpu.VMEM((4, 3, dx, dz), f32),
        pltpu.VMEM((4, 3, dx, dz), f32),
        pltpu.VMEM((4, 16, dz), f32),
        pltpu.VMEM((4, 16, dz), f32),
        pltpu.VMEM((6, 8, dz), f32),
        pltpu.VMEM((5, 3, 8, dz), f32),
        pltpu.VMEM((8, dz), f32),
        pltpu.VMEM((ng, 8, dz), f32),
        pltpu.VMEM((8, dz), f32),
        pltpu.VMEM((nb, 8, dz), f32),
        pltpu.VMEM((8, dz), f32),
        pltpu.VMEM((3, ng, 8, dz), f32),
        pltpu.VMEM((3, ng + 2, 8, dz), f32),
        pltpu.VMEM((2, cg, cg), f32),
        dma((3,)),
        dma((4,)), dma((4,)),
        dma((5,)), dma((5,)),
        dma((ROUNDS, 8)), dma((ROUNDS, 8)),
        dma((8,)), dma((8,)),
        dma((ng,)), dma((ng,)),
        dma((nb,)), dma((nb,)),
        dma((3 * ng,)), dma((3 * ng,)),
        dma((2,)), dma((2,)),
    ]
    rhs, material, inverse, mortar, mu, lam = (
        pltpu.with_memory_space_constraint(x, pltpu.HBM)
        for x in (rhs, material, inverse, mortar, mu, lam)
    )
    return pl.pallas_call(
        functools.partial(kernel, nb, ng, dx, dy, dz),
        out_shape=(
            jax.ShapeDtypeStruct(rhs.shape, f32),
            jax.ShapeDtypeStruct(rhs.shape, f32),
        ),
        in_specs=[hbm, hbm, vmem, smem, smem, smem, hbm],
        out_specs=(vmem, vmem),
        scratch_shapes=scratch,
        compiler_params=pltpu.CompilerParams(
            collective_id=0, has_side_effects=True, vmem_limit_bytes=16 * 2**20
        ),
    )(rhs, material, level, mortar, mu, lam, inverse)


def solution(mesh):
    return jax.shard_map(
        per_device,
        mesh=mesh,
        in_specs=(
            P(None, "bricks", "group", None),
            P("bricks", "group", None),
            P("bricks", "group"),
            P("bricks", "group", None),
            P(),
            P(),
            P("bricks", None, None),
        ),
        out_specs=(P(None, "bricks", "group", None), P(None, "bricks", "group", None)),
        check_vma=False,
    )
```

```python
import functools

import jax
import jax.numpy as jnp
from jax import lax
from jax.experimental import pallas as pl
from jax.experimental.pallas import tpu as pltpu
from jax.sharding import PartitionSpec as P

BLOCK_Z = 32
CHEB = 4
LOW_RATIO = 0.15
BOUND_MARGIN = 1.1
ROUNDS = 4
UNROLL = 4
DEPTH = 2
SWEEP = 7
INNER = 6
HIGHEST = lax.Precision.HIGHEST


def kernel(
    nb, ng, dx, dy, dz,
    rhs_in, material_in, level, mortar, mu, lam, inverse_in,
    sol, res, rhs, material, inverse,
    u, r, shear, wx, wyp, wym, wzp, wzm, dg, hb, invd, coef,
    s_send_up, s_send_y, s_recv, static_send, static_recv, index_send, index_recv, index,
    faces, mixed, y_send, corner_send, recv_x, recv_y, recv_d, ghost, gy, before,
    pack_send, pack_recv, corner_pack, recv_k, corner_rows, spread_k,
    m_own, m_all, m2_own, m2_all, c_own, c_all, f_all, inv_recv, in_sem,
    s_ssem, s_rsem, t_ssem, t_rsem, h_ssem, h_rsem, p_ssem, p_rsem,
    m_ssem, m_rsem, m2_ssem, m2_rsem, c_ssem, c_rsem, i_ssem, i_rsem,
):
    b = lax.axis_index("bricks")
    g = lax.axis_index("group")
    has = [b > 0, b < nb - 1, g > 0, g < ng - 1]
    sends = [has[1], has[0], has[3], has[2]]
    peers = [(b + 1, g), (b - 1, g), (b, g + 1), (b, g - 1)]
    corners = [(0, 0), (0, 1), (1, 0), (1, 1)]
    has_corner = [has[sx] & has[2 + sy] for sx, sy in corners]
    corner_peer = [(b + 2 * sx - 1, g + 2 * sy - 1) for sx, sy in corners]

    def remote(src, dst, ssem, rsem, peer):
        return pltpu.make_async_remote_copy(
            src_ref=src, dst_ref=dst, send_sem=ssem, recv_sem=rsem,
            device_id=peer, device_id_type=pl.DeviceIdType.MESH,
        )

    barrier = pltpu.get_barrier_semaphore()
    paired = nb % 2 == 0
    stride = 2 if paired else 1
    partner = b + 1 - 2 * lax.rem(b, 2)
    others = [(b, lax.rem(g + k, ng)) for k in range(1, ng)]
    others += [(lax.rem(b + k, nb), g) for k in range(stride, nb, stride)]
    around = [lax.rem(g + k, ng) for k in range(0 if paired else 1, ng)]
    for peer in others:
        pl.semaphore_signal(
            barrier, inc=1, device_id=peer, device_id_type=pl.DeviceIdType.MESH
        )
    for d in range(2):
        @pl.when(has[d])
        def _():
            for at in around:
                pl.semaphore_signal(
                    barrier, inc=1, device_id=(b - 1 + 2 * d, at),
                    device_id_type=pl.DeviceIdType.MESH,
                )

    def fetch(k):
        source = [material_in, rhs_in, inverse_in.at[0]][k]
        return pltpu.make_async_copy(source, [material, rhs, inverse][k], in_sem.at[k])

    for k in range(3):
        fetch(k).start()

    row = lax.broadcasted_iota(jnp.int32, (dy, dz), 0)
    lane = lax.broadcasted_iota(jnp.int32, (dy, dz), 1)
    grade = jnp.broadcast_to(level[...], (dy, dz))
    scale = jnp.where(grade == 0, 1.0, jnp.where(grade == 1, 4.0, 16.0))
    zero_face = jnp.zeros((dy, dz), jnp.float32)

    order = [mortar[0, 0, k] for k in range(dy)]
    order_here = jnp.zeros((dy, dz), jnp.int32)
    undo_here = jnp.zeros((dy, dz), jnp.int32)
    for k in range(dy):
        order_here = jnp.where(row == k, order[k], order_here)
        undo_here = jnp.where(row == order[k], k, undo_here)
    index_send[...] = order_here
    index[0] = order_here
    index[1] = undo_here

    def permute(value, k):
        half = dy // 2
        parts = []
        for h in range(2):
            at = index[k, h * half : (h + 1) * half]
            within = jnp.bitwise_and(at, half - 1)
            low = jnp.take_along_axis(value[:half], within, axis=0)
            high = jnp.take_along_axis(value[half:], within, axis=0)
            parts.append(jnp.where(at < half, low, high))
        return jnp.concatenate(parts, axis=0)

    def lookup(ids, table):
        total = jnp.where(ids == 0, table[0], 0.0)
        for entry in range(1, 4):
            total = jnp.where(ids == entry, table[entry], total)
        return total * scale

    def shear_plane(i, _):
        ids = material[i]
        plane = lookup(ids, mu)
        bulk = lookup(ids, lam)
        shear[i + 1] = plane
        hb[i] = bulk
        s_send_y[0, pl.ds(i, 1), :] = plane[dy - 1 : dy]
        s_send_y[1, pl.ds(i, 1), :] = plane[0:1]
        for d, near, far in ((2, dy - 1, dy - 2), (3, 0, 1)):
            static_send[d, 0, pl.ds(i, 1), :] = plane[near : near + 1]
            static_send[d, 1, pl.ds(i, 1), :] = plane[far : far + 1]
            static_send[d, 2, pl.ds(i, 1), :] = bulk[near : near + 1]
        return 0

    fetch(0).wait()
    lax.fori_loop(0, dx, shear_plane, 0, unroll=UNROLL)
    s_send_up[...] = permute(shear[dx], 0)
    for d, near, far in ((0, dx - 1, dx - 2), (1, 0, 1)):
        static_send[d, 0] = shear[near + 1]
        static_send[d, 1] = shear[far + 1]
        static_send[d, 2] = hb[near]

    both = jnp.where(has[0], len(around), 0) + jnp.where(has[1], len(around), 0)
    pl.semaphore_wait(barrier, len(others) + both)

    def s_copy(d):
        src = [s_send_up, shear.at[1], s_send_y.at[0], s_send_y.at[1]][d]
        return remote(src, s_recv.at[d], s_ssem.at[d], s_rsem.at[d], peers[d])

    def t_copy(d):
        if d == 4:
            return remote(index_send, index_recv, t_ssem.at[4], t_rsem.at[4], peers[0])
        return remote(
            static_send.at[d], static_recv.at[d], t_ssem.at[d], t_rsem.at[d], peers[d]
        )

    def exchange_start(copy, directions=(0, 1, 2, 3)):
        for d in directions:
            @pl.when(sends[d % 4])
            def _():
                copy(d).start()

    def arrive_wait(copy, directions=(0, 1, 2, 3)):
        for d in directions:
            @pl.when(has[d % 4])
            def _():
                copy(d).wait_recv()

    def sent_wait(copy, directions=(0, 1, 2, 3)):
        for d in directions:
            @pl.when(sends[d % 4])
            def _():
                copy(d).wait_send()

    def exchange_wait(copy, directions=(0, 1, 2, 3)):
        arrive_wait(copy, directions)
        sent_wait(copy, directions)

    exchange_start(s_copy)
    exchange_start(t_copy, (4, 0, 1, 2, 3))

    @pl.when(b == 0)
    def _():
        s_recv[0] = shear[1]
        index_recv[...] = row

    @pl.when(b == nb - 1)
    def _():
        s_recv[1] = shear[dx]

    @pl.when(g == 0)
    def _():
        s_recv[2] = s_send_y[1]

    @pl.when(g == ng - 1)
    def _():
        s_recv[3] = s_send_y[0]

    for d in range(4):
        @pl.when(jnp.logical_not(has[d]))
        def _():
            one = jnp.ones((dy, dz), jnp.float32)
            for k in range(3):
                static_recv[d, k] = one
                pack_recv[d, k] = zero_face
            for turn in range(ROUNDS):
                for c in range(3):
                    for j in range(2):
                        if d < 2:
                            recv_x[turn, d, c, j] = zero_face
                        else:
                            recv_y[turn, d - 2, j, c] = zero_face
            if d < 2:
                inv_recv[d] = jnp.zeros(inv_recv.shape[1:], jnp.float32)
                c_all[2 * d] = jnp.zeros(c_all.shape[1:], jnp.float32)

    for k in range(4):
        @pl.when(jnp.logical_not(has_corner[k]))
        def _():
            for turn in range(ROUNDS):
                recv_d[turn, k] = jnp.zeros(recv_d.shape[2:], jnp.float32)
            recv_k[k] = jnp.zeros(recv_k.shape[1:], jnp.float32)

    fetch(1).wait()
    fetch(2).wait()
    exchange_wait(s_copy)
    shear[0] = s_recv[0]

    @pl.when(b < nb - 1)
    def _():
        shear[dx + 1] = permute(s_recv[1], 1)

    @pl.when(b == nb - 1)
    def _():
        shear[dx + 1] = shear[dx]

    def rows_near(v, low, high):
        half = dy // 2
        at = row[:half]
        parts = [v[:half], v[half:]]
        down = [pltpu.roll(part, 1, 0) for part in parts]
        up = [pltpu.roll(part, half - 1, 0) for part in parts]
        low = jnp.broadcast_to(low[:half], parts[0].shape)
        high = jnp.broadcast_to(high[:half], parts[0].shape)
        m = [jnp.where(at == 0, low, down[0]), jnp.where(at == 0, down[0], down[1])]
        p = [
            jnp.where(at == half - 1, up[1], up[0]),
            jnp.where(at == half - 1, high, up[1]),
        ]
        return jnp.concatenate(m, axis=0), jnp.concatenate(p, axis=0)

    def z_near(v):
        return pltpu.roll(v, 1, 1), pltpu.roll(v, dz - 1, 1)

    def h_copy(turn, slot):
        deep = DEPTH

        def copy(d):
            if d == 0:
                src = u.at[slot, :, dx + 1 - deep : dx + 1]
                dst = recv_x.at[turn, 0, :, 2 - deep : 2]
            elif d == 1:
                src = u.at[slot, :, 1 : 1 + deep]
                dst = recv_x.at[turn, 1, :, 0:deep]
            else:
                src = y_send.at[turn, d - 2, 0:deep]
                dst = recv_y.at[turn, d - 2, 0:deep]
            return remote(src, dst, h_ssem.at[turn, d], h_rsem.at[turn, d], peers[d])
        return copy

    def corner_copy(turn, k):
        return remote(
            corner_send.at[turn, k], recv_d.at[turn, 3 - k],
            h_ssem.at[turn, 4 + k], h_rsem.at[turn, 7 - k], corner_peer[k],
        )

    def corner_arrival(turn, k):
        return remote(
            corner_send.at[turn, k], recv_d.at[turn, k],
            h_ssem.at[turn, 4 + k], h_rsem.at[turn, 4 + k], corner_peer[k],
        )

    even = lax.rem(b, 2) == 0

    def send_faces(turn, slot):
        copy = h_copy(turn, slot)

        @pl.when(sends[1] & even)
        def _():
            copy(1).start()

        exchange_start(copy, (0,))

        @pl.when(sends[1] & jnp.logical_not(even))
        def _():
            copy(1).start()

        for c in range(3):
            bottom, top = u[slot, c, 1], u[slot, c, dx]
            mixed_low, mixed_high = permute(bottom, 3), permute(top, 0)
            mixed[0, c] = mixed_low
            mixed[1, c] = mixed_high
            for k, (sx, sy) in enumerate(corners):
                y = (dy - 1) * sy
                plane, other = ((bottom, mixed_low), (top, mixed_high))[sx]
                corner_send[turn, k, c : c + 1, :] = plane[y : y + 1]
                corner_send[turn, k, 3 + c : 4 + c, :] = other[y : y + 1]
        for k in range(4):
            @pl.when(has_corner[k])
            def _():
                corner_copy(turn, k).start()

    def send_rows(turn, slot):
        exchange_start(h_copy(turn, slot), (2, 3))

    def store_rows(turn, c, i, value):
        y_send[turn, 0, 0, c, pl.ds(i, 1), :] = value[dy - 1 : dy]
        y_send[turn, 1, 0, c, pl.ds(i, 1), :] = value[0:1]
        y_send[turn, 0, 1, c, pl.ds(i, 1), :] = value[dy - 2 : dy - 1]
        y_send[turn, 1, 1, c, pl.ds(i, 1), :] = value[1:2]

    def corners_wait(turn):
        for k in range(4):
            @pl.when(has_corner[k])
            def _():
                corner_arrival(turn, k).wait_recv()
        for k in range(4):
            @pl.when(has_corner[k])
            def _():
                corner_copy(turn, k).wait_send()

    def nearest(turn, s, c):
        return recv_x[turn, s, c, 1 - s]

    def place_faces(turn, slot):
        for c in range(3):
            u[slot, c, 0] = permute(nearest(turn, 0, c), 2)
            u[slot, c, dx + 1] = permute(nearest(turn, 1, c), 1)

    def sweep_send(plane, turn, slot, carry):
        for i in range(DEPTH):
            carry = plane(i, carry)
            carry = plane(dx - 1 - i, carry)
        send_faces(turn, slot)
        carry = lax.fori_loop(DEPTH, dx - DEPTH, plane, carry, unroll=INNER)
        send_rows(turn, slot)
        return carry

    def sweep_receive(plane, turn, slot, carry, faces_done):
        exchange_wait(h_copy(turn, slot), (2, 3))
        carry = lax.fori_loop(1, dx - 1, plane, carry, unroll=SWEEP)
        exchange_wait(h_copy(turn, slot), (0, 1))
        corners_wait(turn)
        place_faces(turn, slot)
        faces_done()
        carry = plane(0, carry)
        carry = plane(dx - 1, carry)
        return carry

    wx[0] = 0.5 * (shear[0] + shear[1])
    wx[dx] = 0.5 * (shear[dx] + shear[dx + 1])

    exchange_wait(t_copy, (4,))
    index[2] = index_recv[...]
    undo_below = jnp.zeros((dy, dz), jnp.int32)
    for k in range(dy):
        at = jnp.broadcast_to(index_recv[k : k + 1, :], (dy, dz))
        undo_below = jnp.where(row == at, k, undo_below)
    index[3] = undo_below

    def weight_plane(i, best):
        s = shear[i + 1]
        xp = 0.5 * (s + shear[i + 2])
        wx[i + 1] = xp
        xm = 0.5 * (s + shear[i])
        ym, yp = rows_near(s, s_recv[2, pl.ds(i, 1), :], s_recv[3, pl.ds(i, 1), :])
        ym = 0.5 * (s + ym)
        yp = 0.5 * (s + yp)
        zm, zp = z_near(s)
        zm = 0.5 * (s + zm)
        zp = 0.5 * (s + zp)
        wyp[i] = yp
        wym[i] = ym
        wzp[i] = jnp.where(lane == dz - 1, 0.0, zp)
        wzm[i] = jnp.where(lane == 0, 0.0, zm)
        total = xp + xm + yp + ym + jnp.where(lane == dz - 1, s, zp) + jnp.where(lane == 0, s, zm)
        bulk = hb[i]
        diagonal = total + 1.5 * bulk
        inv = 1.0 / diagonal
        invd[i] = inv
        dg[i] = total + bulk
        hb[i] = 0.5 * bulk
        for c in range(3):
            d0 = rhs[c, i] * inv
            u[0, c, i + 1] = d0
            store_rows(0, c, i, d0)
        return jnp.maximum(best, (2.0 * total + 2.5 * bulk) / diagonal)

    below_shear = permute(shear[1], 3)
    faces[0] = below_shear
    for k, (sx, sy) in enumerate(corners):
        y = (dy - 1) * sy
        plane = shear[(1, dx)[sx]]
        other = (below_shear, s_send_up[...])[sx]
        corner_send[0, k, 6:7, :] = plane[y : y + 1]
        corner_send[0, k, 7:8, :] = other[y : y + 1]

    best = jnp.zeros((dy, dz), jnp.float32)
    best = lax.fori_loop(0, dx, weight_plane, best, unroll=UNROLL)
    m_own[...] = jnp.broadcast_to(jnp.max(best, axis=0, keepdims=True), m_own.shape)

    def m_copy(k):
        peer = (b if k < ng else partner, lax.rem(g + k, ng))
        return remote(m_own, m_all.at[k], m_ssem.at[k], m_rsem.at[k], peer)

    def m2_copy(k):
        peer = (lax.rem(b + k * stride, nb), g)
        return remote(m2_own, m2_all.at[k], m2_ssem.at[k], m2_rsem.at[k], peer)

    m_copies = [m_copy(k) for k in range(1, 2 * ng if paired else ng)]
    m2_copies = [m2_copy(k) for k in range(1, nb // stride)]
    for copy in m_copies[::-1]:
        copy.start()
    send_faces(0, 0)
    send_rows(0, 0)

    def apply_plane(i, slot, low, high):
        v = [u[slot, c, i + 1] for c in range(3)]
        coupled = hb[i] * (v[0] + v[1] + v[2])
        out = []
        for c in range(3):
            ym, yp = rows_near(v[c], low(c, i), high(c, i))
            zm, zp = z_near(v[c])
            near = wx[i] * u[slot, c, i] + wx[i + 1] * u[slot, c, i + 2]
            near = near + wym[i] * ym + wyp[i] * yp + wzm[i] * zm + wzp[i] * zp
            out.append(dg[i] * v[c] + coupled - near)
        return v, out

    def recv_rows(turn):
        return (
            lambda c, i: recv_y[turn, 0, 0, c, pl.ds(i, 1), :],
            lambda c, i: recv_y[turn, 1, 0, c, pl.ds(i, 1), :],
        )

    ghost_rows = (
        lambda c, i: gy[0, c, pl.ds(i, 1), :],
        lambda c, i: gy[1, c, pl.ds(i, 1), :],
    )

    def bcoef(k):
        return jnp.broadcast_to(coef[k : k + 1, :], (dy, dz))

    def ghost_weights(d, cross, low, high):
        near, far, bulk = [static_recv[d, k] for k in range(3)]
        inner = 0.5 * (near + far)
        across = 0.5 * (near + cross)
        rm, rp = rows_near(near, low, high)
        rm = 0.5 * (near + rm)
        rp = 0.5 * (near + rp)
        zm, zp = z_near(near)
        zm = 0.5 * (near + zm)
        zp = 0.5 * (near + zp)
        total = inner + across + rm + rp
        total = total + jnp.where(lane == dz - 1, near, zp) + jnp.where(lane == 0, near, zm)
        inv = jnp.where(has[d], 1.0, 0.0) / (total + 1.5 * bulk)
        zm = jnp.where(lane == 0, 0.0, zm)
        zp = jnp.where(lane == dz - 1, 0.0, zp)
        for k, value in enumerate(
            (inner, across, rm, rp, zm, zp, total + bulk, 0.5 * bulk, inv)
        ):
            ghost[d, k] = value

    def all_ghost_weights():
        def edge(inside, corner, at, own):
            return jnp.where(inside, recv_d[0, corner, at : at + 1, :], own)

        for d in range(4):
            s = d % 2
            near = static_recv[d, 0]
            ends = near[0:1], near[dy - 1 : dy]
            if d < 2:
                cross = (faces[0], s_send_up[...])[s]
                low = edge(has[2], 2 * s, 6, ends[0])
                high = edge(has[3], 2 * s + 1, 6, ends[1])
            else:
                cross = s_send_y[1 - s]
                low = edge(has[0], s, 7, ends[0])
                high = edge(has[1], 2 + s, 7, ends[1])
            ghost_weights(d, cross, low, high)

    def ghost_apply(d, v, inner, cross, low, high):
        w = [ghost[d, k] for k in range(9)]
        coupled = w[7] * (v[0] + v[1] + v[2])
        out = []
        for c in range(3):
            rm, rp = rows_near(v[c], low[c], high[c])
            zm, zp = z_near(v[c])
            near = w[0] * inner[c] + w[1] * cross[c] + w[2] * rm + w[3] * rp
            near = near + w[4] * zm + w[5] * zp
            out.append(w[8] * (w[6] * v[c] + coupled - near))
        return out

    def ghost_step(turn, other, update, directions=(0, 1, 2, 3), ends=True):
        none = [jnp.zeros((1, dz), jnp.float32)] * 3
        for d in directions:
            s = d % 2
            if d < 2:
                v = [nearest(turn, s, c) for c in range(3)]
                inner = [recv_x[turn, s, c, s] for c in range(3)]
                cross = [mixed[s, c] for c in range(3)]
                low = [recv_d[turn, 2 * s, c : c + 1, :] for c in range(3)]
                high = [recv_d[turn, 2 * s + 1, c : c + 1, :] for c in range(3)]
            else:
                v = [recv_y[turn, s, 0, c] for c in range(3)]
                inner = [recv_y[turn, s, 1, c] for c in range(3)]
                cross = [y_send[turn, 1 - s, 0, c] for c in range(3)]
                low, high = none, none
                if ends:
                    low = [recv_d[turn, s, 3 + c : 4 + c, :] for c in range(3)]
                    high = [recv_d[turn, 2 + s, 3 + c : 4 + c, :] for c in range(3)]
            out = ghost_apply(d, v, inner, cross, low, high)
            for c in range(3):
                new = update(d, c, v[c], out[c])
                if d < 2:
                    u[other, c, (dx + 1) * s] = permute(new, 2 - s)
                else:
                    gy[s, c] = new

    top = m_own[...]
    for k, copy in enumerate(m_copies):
        copy.wait()
        top = jnp.maximum(top, m_all[k + 1])
    m2_own[...] = top
    for copy in m2_copies:
        copy.start()

    for d in range(2):
        i = (dx - 2, 1)[d]
        pack_send[d, 0] = invd[i]
        pack_send[d, 1] = hb[i]
        pack_send[d, 2] = jnp.where(row == 0, wym[i], jnp.where(row == dy - 1, wyp[i], 0.0))
    for d, y in ((2, dy - 2), (3, 1)):
        pack_send[d, 2] = zero_face
        pack_send[d, 2, 0:1, :] = wx[0, y : y + 1, :]
        pack_send[d, 2, dx - 1 : dx, :] = wx[dx, y : y + 1, :]
        for i in range(dx):
            pack_send[d, 0, i : i + 1, :] = invd[i, y : y + 1, :]
            pack_send[d, 1, i : i + 1, :] = hb[i, y : y + 1, :]
    for sx in range(2):
        i = (dx - 1) * sx
        values = (
            invd[i], hb[i], wx[dx * sx],
            jnp.where(row == 0, wym[i], 0.0), jnp.where(row == dy - 1, wyp[i], 0.0),
            shear[i + 1],
        )
        for k, value in enumerate(values):
            other = permute(value, (3, 0)[sx])
            for sy in range(2):
                y = (dy - 1) * sy
                corner_pack[2 * sx + sy, k : k + 1, :] = value[y : y + 1]
                corner_pack[2 * sx + sy, 8 + k : 9 + k, :] = other[y : y + 1]

    def p_copy(d):
        return remote(
            pack_send.at[d], pack_recv.at[d], p_ssem.at[d], p_rsem.at[d], peers[d]
        )

    def k_copy(k, at):
        return remote(
            corner_pack.at[k], recv_k.at[at], p_ssem.at[4 + k], p_rsem.at[4 + at],
            corner_peer[k],
        )

    exchange_start(p_copy)
    for k in range(4):
        @pl.when(has_corner[k])
        def _():
            k_copy(k, 3 - k).start()
    exchange_wait(t_copy)

    low, high = recv_rows(0)

    def first_plane(i, _):
        _, out = apply_plane(i, 0, low, high)
        inv = invd[i]
        for c in range(3):
            r[c, i] = out[c]
            u[1, c, i + 1] = out[c] * inv
        return 0

    def first_ghosts():
        all_ghost_weights()

        def update(d, c, v, out):
            before[d, c] = out
            return out

        ghost_step(0, 1, update)

    sweep_receive(first_plane, 0, 0, 0, first_ghosts)

    def second_plane(i, _):
        _, out = apply_plane(i, 1, *ghost_rows)
        for c in range(3):
            res[c, i] = out[c]
        return 0

    lax.fori_loop(0, dx, second_plane, 0, unroll=8)

    for k, copy in enumerate(m2_copies):
        copy.wait()
        top = jnp.maximum(top, m2_all[k + 1])
    upper = BOUND_MARGIN * jnp.broadcast_to(jnp.max(top, axis=1, keepdims=True), top.shape)
    lower = LOW_RATIO * upper
    theta = 0.5 * (upper + lower)
    delta = 0.5 * (upper - lower)
    sigma = theta / delta
    damping = 1.0 / sigma
    inv_theta = 1.0 / theta
    coef[0:8] = inv_theta
    rows = []
    for turn in range(1, CHEB):
        following = 1.0 / (2.0 * sigma - damping)
        rows.append((following * damping, 2.0 * following / delta))
        damping = following
    for turn, (a, c2) in enumerate(rows):
        coef[8 + 2 * turn : 9 + 2 * turn] = a[0:1]
        coef[9 + 2 * turn : 10 + 2 * turn] = c2[0:1]
    coef[14:15] = (rows[0][0] * inv_theta + rows[0][1])[0:1]
    coef[15:16] = (rows[0][1] * inv_theta)[0:1]
    (a, c2), (a_next, c_next) = rows[1], rows[2]
    ratio = c_next / c2
    coef[16:17] = (a_next + ratio)[0:1]
    coef[17:18] = (ratio * a)[0:1]
    coef[18:19] = (rows[0][0] + rows[0][1] * theta)[0:1]

    alpha, beta, it = bcoef(14), bcoef(15), bcoef(0)
    both_it = alpha + it
    a_two, c_two = bcoef(10), bcoef(11)

    def combine_plane(i, _):
        inv = invd[i]
        for c in range(3):
            d0 = u[0, c, i + 1]
            one = alpha * d0 - beta * u[1, c, i + 1]
            sol[c, i] = it * d0 + one
            rest = rhs[c, i] - both_it * r[c, i] + beta * res[c, i]
            res[c, i] = rest
            two = a_two * one + c_two * (rest * inv)
            u[0, c, i + 1] = two
            store_rows(1, c, i, two)
        return 0

    sweep_send(combine_plane, 1, 0, 0)
    for d in range(4):
        for c in range(3):
            v = nearest(0, d, c) if d < 2 else recv_y[0, d - 2, 0, c]
            before[d, c] = alpha * v - beta * before[d, c]

    def step_plane(slot, low, high, a, c2, following, summed=False, rows_of=None):
        other = 1 - slot

        def plane(i, sums):
            v, out = apply_plane(i, slot, low, high)
            inv = invd[i]
            new = []
            for c in range(3):
                rest = res[c, i] - out[c]
                res[c, i] = rest
                sol[c, i] = sol[c, i] + v[c]
                if summed:
                    new.append(sums[c] + rest)
                if not following:
                    continue
                ahead = c2 * (rest * inv)
                if a is not None:
                    ahead = ahead + a * v[c]
                u[other, c, i + 1] = ahead
                if rows_of is not None:
                    store_rows(rows_of, c, i, ahead)
            return tuple(new)
        return plane

    def pair_ghosts(turn, other):
        def done(directions=(0, 1, 2, 3), ends=True):
            e1, e2, e3 = bcoef(16), bcoef(17), bcoef(13)

            def update(d, c, v, out):
                return e1 * v - e2 * before[d, c] - e3 * out

            ghost_step(turn, other, update, directions, ends)
        return done

    def pair_receive(turn, slot, first, second, carry, ghosts):
        exchange_wait(h_copy(turn, slot), (2, 3))
        lax.fori_loop(1, dx - 1, first, (), unroll=SWEEP)
        ghosts((2, 3), False)
        carry = lax.fori_loop(2, dx - 2, second, carry, unroll=INNER)
        exchange_wait(h_copy(turn, slot), (0, 1))
        corners_wait(turn)
        place_faces(turn, slot)
        ghosts()
        for i in (0, dx - 1):
            first(i, ())
        for i in (0, 1, dx - 2, dx - 1):
            carry = second(i, carry)
        return carry

    def i_copy(d):
        return remote(inverse, inv_recv.at[d], i_ssem.at[d], i_rsem.at[d], peers[d])

    exchange_start(i_copy, (0, 1))
    first = step_plane(0, *recv_rows(1), bcoef(12), bcoef(13), True)
    second = step_plane(1, *ghost_rows, None, bcoef(0), True, summed=True, rows_of=2)
    init = tuple(jnp.zeros((dy, dz), jnp.float32) for _ in range(3))
    sums = pair_receive(1, 0, first, second, init, pair_ghosts(1, 1))

    c_own[...] = jnp.zeros(c_own.shape, jnp.float32)
    for c in range(3):
        c_own[c : c + 1, :] = jnp.sum(sums[c], axis=0, keepdims=True)
    c_all[1, g] = c_own[...]

    def c_copy(q, k):
        slot = q * ng + k
        return remote(
            c_own, c_all.at[q, g], c_ssem.at[slot], c_rsem.at[slot],
            (b + 1 - q, lax.rem(g + k, ng)),
        )

    def c_arrival(q, k):
        slot = q * ng + k
        source = lax.rem(g + ng - k, ng)
        return remote(
            c_own, c_all.at[q, source], c_ssem.at[slot], c_rsem.at[slot],
            (b + 1 - q, lax.rem(g + k, ng)),
        )

    def coarse_all(to_do, flags):
        for q in (0, 2, 1):
            first = 1 if q == 1 else 0
            if q == 1:
                for k in range(first, ng):
                    to_do(q, k)
                continue

            @pl.when(flags[q])
            def _():
                for k in range(first, ng):
                    to_do(q, k)

    coarse_all(lambda q, k: c_copy(q, k).start(), {0: has[1], 2: has[0]})
    send_faces(2, 0)
    send_rows(2, 0)
    f_all[...] = jnp.zeros(f_all.shape, jnp.float32)
    exchange_wait(p_copy)
    for k in range(4):
        @pl.when(has_corner[k])
        def _():
            k_copy(k, k).wait_recv()
    for k in range(4):
        @pl.when(has_corner[k])
        def _():
            k_copy(k, k).wait_send()
    for k in range(4):
        for n in range(6):
            for side in range(2):
                at = 2 * k + side
                corner_rows[n, at : at + 1, :] = recv_k[k, 8 * side + n : 8 * side + n + 1, :]
    exchange_wait(i_copy, (0, 1))
    coarse_all(lambda q, k: c_arrival(q, k).wait_recv(), {0: has[0], 2: has[1]})
    coarse_all(lambda q, k: c_copy(q, k).wait_send(), {0: has[1], 2: has[0]})

    cells_z = dz // BLOCK_Z
    size = 3 * cells_z * ng
    flat = c_all[...].reshape(3 * ng * 8, dz)
    li = lax.broadcasted_iota(jnp.int32, (dz, size), 0)
    ki = lax.broadcasted_iota(jnp.int32, (dz, size), 1)
    gather = jnp.where(li // BLOCK_Z == ki % cells_z, 1.0 / (dx * dy * BLOCK_Z), 0.0)
    spread = jnp.dot(flat, gather, precision=HIGHEST, preferred_element_type=jnp.float32)
    ri = lax.broadcasted_iota(jnp.int32, (ng * 8, size), 0)
    kk = lax.broadcasted_iota(jnp.int32, (ng * 8, size), 1) // cells_z
    mine = (ri // 8 == kk // 3) & (ri % 8 == kk % 3)
    bi = lax.broadcasted_iota(jnp.int32, (size, dz), 0)
    bl = lax.broadcasted_iota(jnp.int32, (size, dz), 1)
    placed = bi % cells_z == bl // BLOCK_Z
    for q in range(3):
        part = spread[q * ng * 8 : (q + 1) * ng * 8]
        vector = jnp.sum(jnp.where(mine, part, 0.0), axis=0, keepdims=True)
        matrix = inverse[...] if q == 1 else inv_recv[q // 2]
        correction = jnp.sum(matrix * vector, axis=1, keepdims=True)
        table = jnp.where(placed, jnp.broadcast_to(correction, (size, dz)), 0.0)
        for k in range(ng):
            for c in range(3):
                start = (k * 3 + c) * cells_z
                f_all[q, k + 1, c : c + 1, :] = jnp.sum(
                    table[start : start + cells_z], axis=0, keepdims=True
                )

    def full(q, at, c):
        return jnp.broadcast_to(f_all[q, at, c : c + 1, :], (dy, dz))

    own_fine = [full(1, g + 1, c) for c in range(3)]

    fine_sides = [z_near(own_fine[c]) for c in range(3)]
    fine_rows = [
        (
            jnp.where(row == 0, full(1, g, c), own_fine[c]),
            jnp.where(row == dy - 1, full(1, g + 2, c), own_fine[c]),
        )
        for c in range(3)
    ]
    fine_sum = own_fine[0] + own_fine[1] + own_fine[2]
    it = bcoef(0)

    def fine_plane(i, _):
        inv = invd[i]
        coupled = hb[i] * fine_sum
        for c in range(3):
            f = own_fine[c]
            first, last = isinstance(i, int) and i == 0, isinstance(i, int) and i == dx - 1
            xm = full(0, g + 1, c) if first else f
            xp = full(2, g + 1, c) if last else f
            near = wx[i] * xm + wx[i + 1] * xp
            near = near + wym[i] * fine_rows[c][0] + wyp[i] * fine_rows[c][1]
            near = near + wzm[i] * fine_sides[c][0] + wzp[i] * fine_sides[c][1]
            rest = res[c, i] - (dg[i] * f + coupled - near)
            res[c, i] = rest
            sol[c, i] = sol[c, i] + f
            ahead = it * (rest * inv)
            u[0, c, i + 1] = ahead
            y_send[2, 0, 0, c, pl.ds(i, 1), :] = ahead[dy - 1 : dy]
            y_send[2, 1, 0, c, pl.ds(i, 1), :] = ahead[0:1]
        return 0

    exchange_wait(h_copy(2, 0))
    corners_wait(2)
    for i in range(4):
        fine_plane(i, 0)
        fine_plane(dx - 1 - i, 0)
    for c in range(3):
        mixed[0, c] = permute(u[0, c, 1], 3)
        mixed[1, c] = permute(u[0, c, dx], 0)

    def fine_far(here, low, high, inv, half, w_low, w_high, near, across=None):
        lanes = lane[: near.shape[0]]
        zm, zp = z_near(near)
        zm = jnp.where(lanes == 0, 0.0, 0.5 * (near + zm))
        zp = jnp.where(lanes == dz - 1, 0.0, 0.5 * (near + zp))
        rim = jnp.where((lanes == 0) | (lanes == dz - 1), near, 0.0)
        weight = 2.0 * half + w_low + w_high + zm + zp + rim
        if across is not None:
            weight = weight + across[0]
        coupled = half * (here[0] + here[1] + here[2])
        out = []
        for c in range(3):
            fm, fp = z_near(here[c])
            value = weight * here[c] + coupled - zm * fm - zp * fp
            value = value - w_low * low[c] - w_high * high[c]
            if across is not None:
                value = value - across[0] * across[1][c]
            out.append(inv * value)
        return out

    for d in range(4):
        s = d % 2
        if d < 2:
            spots = (2 * s, g + 1), (2 * s, g), (2 * s, g + 2)
        else:
            at = g + 2 * s
            spots = (1, at), (0, at), (2, at)
        here, low, high = [[full(*spot, c) for c in range(3)] for spot in spots]
        out = ghost_apply(d, here, here, own_fine, low, high)
        inv, half, rim = [pack_recv[d, k] for k in range(3)]
        w_low = jnp.where(row == 0, rim, 0.0)
        w_high = jnp.where(row == dy - 1, rim, 0.0)
        far = fine_far(here, low, high, inv, half, w_low, w_high, static_recv[d, 1])
        for c in range(3):
            if d < 2:
                recv_x[2, s, c, 1 - s] = nearest(2, s, c) - it * out[c]
                recv_x[2, s, c, s] = recv_x[2, s, c, s] - it * far[c]
            else:
                recv_y[2, s, 0, c] = recv_y[2, s, 0, c] - it * out[c]
                recv_y[2, s, 1, c] = recv_y[2, s, 1, c] - it * far[c]

    for k, (sx, sy) in enumerate(corners):
        q, at = 2 * sx, g + 2 * sy
        spots = (q, at), (q, jnp.maximum(at - 1, 0)), (q, jnp.minimum(at + 1, ng + 1)), (1, at)
        for n, spot in enumerate(spots):
            for c in range(3):
                value = f_all[(*spot, slice(c, c + 1))]
                spread_k[n, c, 2 * k : 2 * k + 1, :] = value
                spread_k[n, c, 2 * k + 1 : 2 * k + 2, :] = value
        for c in range(3):
            for n in range(2):
                at = 2 * k + n
                spread_k[4, c, at : at + 1, :] = recv_d[2, k, 3 * n + c : 3 * n + c + 1, :]
    here, low, high, beside = [[spread_k[n, c] for c in range(3)] for n in range(4)]
    inv, half, cross, w_low, w_high, near = [corner_rows[n] for n in range(6)]
    out = fine_far(here, low, high, inv, half, w_low, w_high, near, (cross, beside))
    for c in range(3):
        spread_k[4, c] = spread_k[4, c] - it[0:8] * out[c]
    for k in range(4):
        for c in range(3):
            for n in range(2):
                at = 2 * k + n
                recv_d[2, k, 3 * n + c : 3 * n + c + 1, :] = spread_k[4, c, at : at + 1, :]

    place_faces(2, 0)
    e1, e3 = bcoef(18), bcoef(9)

    def first_update(d, c, v, out):
        new = e1 * v - e3 * out
        before[d, c] = new
        return new

    first = step_plane(0, *recv_rows(2), bcoef(8), bcoef(9), True)
    second = step_plane(1, *ghost_rows, bcoef(10), bcoef(11), True, rows_of=3)
    ghost_step(2, 1, first_update)
    for i in range(3):
        first(i, ())
        first(dx - 1 - i, ())
    for i in range(2):
        second(i, ())
        second(dx - 1 - i, ())
    send_faces(3, 0)
    lax.fori_loop(4, dx - 4, fine_plane, 0, unroll=8)
    ghost_step(2, 1, first_update, (2, 3))
    lax.fori_loop(3, dx - 3, first, (), unroll=5)
    lax.fori_loop(2, dx - 2, second, (), unroll=INNER)
    send_rows(3, 0)
    first = step_plane(0, *recv_rows(3), bcoef(12), bcoef(13), True)
    second = step_plane(1, *ghost_rows, None, None, False)
    pair_receive(3, 0, first, second, (), pair_ghosts(3, 1))


def per_device(rhs, material, level, mortar, mu, lam, inverse):
    nb = lax.axis_size("bricks")
    ng = lax.axis_size("group")
    dx, dy, dz = material.shape
    f32 = jnp.float32
    vmem = pl.BlockSpec(memory_space=pltpu.VMEM)
    smem = pl.BlockSpec(memory_space=pltpu.SMEM)
    hbm = pl.BlockSpec(memory_space=pltpu.HBM)
    dma = pltpu.SemaphoreType.DMA
    grid = pltpu.VMEM((dx, dy, dz), f32)
    cg = inverse.shape[1]
    scratch = [
        pltpu.VMEM((3, dx, dy, dz), f32),
        pltpu.VMEM((dx, dy, dz), jnp.int32),
        pltpu.VMEM((cg, cg), f32),
        pltpu.VMEM((2, 3, dx + 2, dy, dz), f32),
        pltpu.VMEM((3, dx, dy, dz), f32),
        pltpu.VMEM((dx + 2, dy, dz), f32),
        pltpu.VMEM((dx + 1, dy, dz), f32),
        grid, grid, grid, grid, grid, grid, grid,
        pltpu.VMEM((24, dz), f32),
        pltpu.VMEM((dy, dz), f32),
        pltpu.VMEM((2, dx, dz), f32),
        pltpu.VMEM((4, dx, dz), f32),
        pltpu.VMEM((4, 3, dx, dz), f32),
        pltpu.VMEM((4, 3, dx, dz), f32),
        pltpu.VMEM((dy, dz), jnp.int32),
        pltpu.VMEM((dy, dz), jnp.int32),
        pltpu.VMEM((4, dy, dz), jnp.int32),
        pltpu.VMEM((1, dy, dz), f32),
        pltpu.VMEM((2, 3, dy, dz), f32),
        pltpu.VMEM((ROUNDS, 2, 2, 3, dx, dz), f32),
        pltpu.VMEM((ROUNDS, 4, 8, dz), f32),
        pltpu.VMEM((ROUNDS, 2, 3, 2, dy, dz), f32),
        pltpu.VMEM((ROUNDS, 2, 2, 3, dx, dz), f32),
        pltpu.VMEM((ROUNDS, 4, 8, dz), f32),
        pltpu.VMEM((4, 9, dy, dz), f32),
        pltpu.VMEM((2, 3, dx, dz), f32),
        pltpu.VMEM((4, 3, dy, dz), f32),
        pltpu.VMEM((4, 3, dx, dz), f32),
        pltpu.VMEM((4, 3, dx, dz), f32),
        pltpu.VMEM((4, 16, dz), f32),
        pltpu.VMEM((4, 16, dz), f32),
        pltpu.VMEM((6, 8, dz), f32),
        pltpu.VMEM((5, 3, 8, dz), f32),
        pltpu.VMEM((8, dz), f32),
        pltpu.VMEM((2 * ng, 8, dz), f32),
        pltpu.VMEM((8, dz), f32),
        pltpu.VMEM((nb, 8, dz), f32),
        pltpu.VMEM((8, dz), f32),
        pltpu.VMEM((3, ng, 8, dz), f32),
        pltpu.VMEM((3, ng + 2, 8, dz), f32),
        pltpu.VMEM((2, cg, cg), f32),
        dma((3,)),
        dma((4,)), dma((4,)),
        dma((5,)), dma((5,)),
        dma((ROUNDS, 8)), dma((ROUNDS, 8)),
        dma((8,)), dma((8,)),
        dma((2 * ng,)), dma((2 * ng,)),
        dma((nb,)), dma((nb,)),
        dma((3 * ng,)), dma((3 * ng,)),
        dma((2,)), dma((2,)),
    ]
    rhs, material, inverse, mortar, mu, lam = (
        pltpu.with_memory_space_constraint(x, pltpu.HBM)
        for x in (rhs, material, inverse, mortar, mu, lam)
    )
    return pl.pallas_call(
        functools.partial(kernel, nb, ng, dx, dy, dz),
        out_shape=(
            jax.ShapeDtypeStruct(rhs.shape, f32),
            jax.ShapeDtypeStruct(rhs.shape, f32),
        ),
        in_specs=[hbm, hbm, vmem, smem, smem, smem, hbm],
        out_specs=(vmem, vmem),
        scratch_shapes=scratch,
        compiler_params=pltpu.CompilerParams(
            collective_id=0, has_side_effects=True, vmem_limit_bytes=16 * 2**20
        ),
    )(rhs, material, level, mortar, mu, lam, inverse)


def solution(mesh):
    return jax.shard_map(
        per_device,
        mesh=mesh,
        in_specs=(
            P(None, "bricks", "group", None),
            P("bricks", "group", None),
            P("bricks", "group"),
            P("bricks", "group", None),
            P(),
            P(),
            P("bricks", None, None),
        ),
        out_specs=(P(None, "bricks", "group", None), P(None, "bricks", "group", None)),
        check_vma=False,
    )
```

```python
import functools

import jax
import jax.numpy as jnp
from jax import lax
from jax.experimental import pallas as pl
from jax.experimental.pallas import tpu as pltpu
from jax.sharding import PartitionSpec as P

BLOCK_Z = 32
CHEB = 4
LOW_RATIO = 0.15
BOUND_MARGIN = 1.1
ROUNDS = 4
UNROLL = 4
DEPTH = 2
SWEEP = 14
INNER = 12
HIGHEST = lax.Precision.HIGHEST


def kernel(
    nb, ng, dx, dy, dz,
    rhs_in, material_in, level, mortar, mu, lam, inverse_in,
    result, rhs, material, inverse,
    u, r, shear, wx, wyp, wym, wzp, wzm, dg, hb, invd, coef,
    s_send_up, s_send_y, s_recv, static_send, static_recv, index_send, index_recv, index,
    faces, mixed, y_send, corner_send, recv_x, recv_y, recv_d, ghost, gy, before,
    pack_send, pack_recv, corner_pack, recv_k, corner_rows, spread_k,
    m_own, m_all, m2_own, m2_all, c_own, c_all, f_all, inv_recv, in_sem,
    s_ssem, s_rsem, t_ssem, t_rsem, h_ssem, h_rsem, p_ssem, p_rsem,
    m_ssem, m_rsem, m2_ssem, m2_rsem, c_ssem, c_rsem, i_ssem, i_rsem,
):
    sol, res = result.at[0], result.at[1]
    b = lax.axis_index("bricks")
    g = lax.axis_index("group")
    has = [b > 0, b < nb - 1, g > 0, g < ng - 1]
    sends = [has[1], has[0], has[3], has[2]]
    peers = [(b + 1, g), (b - 1, g), (b, g + 1), (b, g - 1)]
    corners = [(0, 0), (0, 1), (1, 0), (1, 1)]
    has_corner = [has[sx] & has[2 + sy] for sx, sy in corners]
    corner_peer = [(b + 2 * sx - 1, g + 2 * sy - 1) for sx, sy in corners]

    def remote(src, dst, ssem, rsem, peer):
        return pltpu.make_async_remote_copy(
            src_ref=src, dst_ref=dst, send_sem=ssem, recv_sem=rsem,
            device_id=peer, device_id_type=pl.DeviceIdType.MESH,
        )

    barrier = pltpu.get_barrier_semaphore()
    paired = nb % 2 == 0
    stride = 2 if paired else 1
    partner = b + 1 - 2 * lax.rem(b, 2)
    others = [(b, lax.rem(g + k, ng)) for k in range(1, ng)]
    others += [(lax.rem(b + k, nb), g) for k in range(stride, nb, stride)]
    around = [lax.rem(g + k, ng) for k in range(0 if paired else 1, ng)]
    for peer in others:
        pl.semaphore_signal(
            barrier, inc=1, device_id=peer, device_id_type=pl.DeviceIdType.MESH
        )
    for d in range(2):
        @pl.when(has[d])
        def _():
            for at in around:
                pl.semaphore_signal(
                    barrier, inc=1, device_id=(b - 1 + 2 * d, at),
                    device_id_type=pl.DeviceIdType.MESH,
                )

    def fetch(k):
        source = [material_in, rhs_in, inverse_in.at[0]][k]
        return pltpu.make_async_copy(source, [material, rhs, inverse][k], in_sem.at[k])

    for k in range(3):
        fetch(k).start()

    row = lax.broadcasted_iota(jnp.int32, (dy, dz), 0)
    lane = lax.broadcasted_iota(jnp.int32, (dy, dz), 1)
    grade = jnp.broadcast_to(level[...], (dy, dz))
    scale = jnp.where(grade == 0, 1.0, jnp.where(grade == 1, 4.0, 16.0))
    zero_face = jnp.zeros((dy, dz), jnp.float32)

    order = [mortar[0, 0, k] for k in range(dy)]
    order_here = jnp.zeros((dy, dz), jnp.int32)
    undo_here = jnp.zeros((dy, dz), jnp.int32)
    for k in range(dy):
        order_here = jnp.where(row == k, order[k], order_here)
        undo_here = jnp.where(row == order[k], k, undo_here)
    index_send[...] = order_here
    index[0] = order_here
    index[1] = undo_here

    def permute(value, k):
        half = dy // 2
        parts = []
        for h in range(2):
            at = index[k, h * half : (h + 1) * half]
            within = jnp.bitwise_and(at, half - 1)
            low = jnp.take_along_axis(value[:half], within, axis=0)
            high = jnp.take_along_axis(value[half:], within, axis=0)
            parts.append(jnp.where(at < half, low, high))
        return jnp.concatenate(parts, axis=0)

    def lookup(ids, table):
        total = jnp.where(ids == 0, table[0], 0.0)
        for entry in range(1, 4):
            total = jnp.where(ids == entry, table[entry], total)
        return total * scale

    def shear_plane(i, _):
        ids = material[i]
        plane = lookup(ids, mu)
        bulk = lookup(ids, lam)
        shear[i + 1] = plane
        hb[i] = bulk
        s_send_y[0, pl.ds(i, 1), :] = plane[dy - 1 : dy]
        s_send_y[1, pl.ds(i, 1), :] = plane[0:1]
        for d, near, far in ((2, dy - 1, dy - 2), (3, 0, 1)):
            static_send[d, 0, pl.ds(i, 1), :] = plane[near : near + 1]
            static_send[d, 1, pl.ds(i, 1), :] = plane[far : far + 1]
            static_send[d, 2, pl.ds(i, 1), :] = bulk[near : near + 1]
        return 0

    fetch(0).wait()
    lax.fori_loop(0, dx, shear_plane, 0, unroll=UNROLL)
    s_send_up[...] = permute(shear[dx], 0)
    for d, near, far in ((0, dx - 1, dx - 2), (1, 0, 1)):
        static_send[d, 0] = shear[near + 1]
        static_send[d, 1] = shear[far + 1]
        static_send[d, 2] = hb[near]

    both = jnp.where(has[0], len(around), 0) + jnp.where(has[1], len(around), 0)
    pl.semaphore_wait(barrier, len(others) + both)

    def s_copy(d):
        src = [s_send_up, shear.at[1], s_send_y.at[0], s_send_y.at[1]][d]
        return remote(src, s_recv.at[d], s_ssem.at[d], s_rsem.at[d], peers[d])

    def t_copy(d):
        if d == 4:
            return remote(index_send, index_recv, t_ssem.at[4], t_rsem.at[4], peers[0])
        return remote(
            static_send.at[d], static_recv.at[d], t_ssem.at[d], t_rsem.at[d], peers[d]
        )

    def exchange_start(copy, directions=(0, 1, 2, 3)):
        for d in directions:
            @pl.when(sends[d % 4])
            def _():
                copy(d).start()

    def arrive_wait(copy, directions=(0, 1, 2, 3)):
        for d in directions:
            @pl.when(has[d % 4])
            def _():
                copy(d).wait_recv()

    def sent_wait(copy, directions=(0, 1, 2, 3)):
        for d in directions:
            @pl.when(sends[d % 4])
            def _():
                copy(d).wait_send()

    def exchange_wait(copy, directions=(0, 1, 2, 3)):
        arrive_wait(copy, directions)
        sent_wait(copy, directions)

    exchange_start(s_copy)
    exchange_start(t_copy, (4, 0, 1, 2, 3))

    @pl.when(b == 0)
    def _():
        s_recv[0] = shear[1]
        index_recv[...] = row

    @pl.when(b == nb - 1)
    def _():
        s_recv[1] = shear[dx]

    @pl.when(g == 0)
    def _():
        s_recv[2] = s_send_y[1]

    @pl.when(g == ng - 1)
    def _():
        s_recv[3] = s_send_y[0]

    for d in range(4):
        @pl.when(jnp.logical_not(has[d]))
        def _():
            one = jnp.ones((dy, dz), jnp.float32)
            for k in range(3):
                static_recv[d, k] = one
                pack_recv[d, k] = zero_face
            for turn in range(ROUNDS):
                for c in range(3):
                    for j in range(2):
                        if d < 2:
                            recv_x[turn, d, c, j] = zero_face
                        else:
                            recv_y[turn, d - 2, j, c] = zero_face
            if d < 2:
                inv_recv[d] = jnp.zeros(inv_recv.shape[1:], jnp.float32)
                c_all[2 * d] = jnp.zeros(c_all.shape[1:], jnp.float32)

    for k in range(4):
        @pl.when(jnp.logical_not(has_corner[k]))
        def _():
            for turn in range(ROUNDS):
                recv_d[turn, k] = jnp.zeros(recv_d.shape[2:], jnp.float32)
            recv_k[k] = jnp.zeros(recv_k.shape[1:], jnp.float32)

    fetch(1).wait()
    fetch(2).wait()
    exchange_wait(s_copy)
    shear[0] = s_recv[0]

    @pl.when(b < nb - 1)
    def _():
        shear[dx + 1] = permute(s_recv[1], 1)

    @pl.when(b == nb - 1)
    def _():
        shear[dx + 1] = shear[dx]

    def rows_near(v, low, high):
        half = dy // 2
        at = row[:half]
        parts = [v[:half], v[half:]]
        down = [pltpu.roll(part, 1, 0) for part in parts]
        up = [pltpu.roll(part, half - 1, 0) for part in parts]
        low = jnp.broadcast_to(low[:half], parts[0].shape)
        high = jnp.broadcast_to(high[:half], parts[0].shape)
        m = [jnp.where(at == 0, low, down[0]), jnp.where(at == 0, down[0], down[1])]
        p = [
            jnp.where(at == half - 1, up[1], up[0]),
            jnp.where(at == half - 1, high, up[1]),
        ]
        return jnp.concatenate(m, axis=0), jnp.concatenate(p, axis=0)

    def z_near(v):
        return pltpu.roll(v, 1, 1), pltpu.roll(v, dz - 1, 1)

    def h_copy(turn, slot):
        deep = DEPTH

        def copy(d):
            if d == 0:
                src = u.at[slot, :, dx + 1 - deep : dx + 1]
                dst = recv_x.at[turn, 0, :, 2 - deep : 2]
            elif d == 1:
                src = u.at[slot, :, 1 : 1 + deep]
                dst = recv_x.at[turn, 1, :, 0:deep]
            else:
                src = y_send.at[turn, d - 2, 0:deep]
                dst = recv_y.at[turn, d - 2, 0:deep]
            return remote(src, dst, h_ssem.at[turn, d], h_rsem.at[turn, d], peers[d])
        return copy

    def corner_copy(turn, k):
        return remote(
            corner_send.at[turn, k], recv_d.at[turn, 3 - k],
            h_ssem.at[turn, 4 + k], h_rsem.at[turn, 7 - k], corner_peer[k],
        )

    def corner_arrival(turn, k):
        return remote(
            corner_send.at[turn, k], recv_d.at[turn, k],
            h_ssem.at[turn, 4 + k], h_rsem.at[turn, 4 + k], corner_peer[k],
        )

    even = lax.rem(b, 2) == 0

    def send_faces(turn, slot):
        copy = h_copy(turn, slot)

        @pl.when(sends[1] & even)
        def _():
            copy(1).start()

        exchange_start(copy, (0,))

        @pl.when(sends[1] & jnp.logical_not(even))
        def _():
            copy(1).start()

    def send_corners(turn, slot):
        for c in range(3):
            bottom, top = u[slot, c, 1], u[slot, c, dx]
            mixed_low, mixed_high = permute(bottom, 3), permute(top, 0)
            mixed[0, c] = mixed_low
            mixed[1, c] = mixed_high
            for k, (sx, sy) in enumerate(corners):
                y = (dy - 1) * sy
                plane, other = ((bottom, mixed_low), (top, mixed_high))[sx]
                corner_send[turn, k, c : c + 1, :] = plane[y : y + 1]
                corner_send[turn, k, 3 + c : 4 + c, :] = other[y : y + 1]
        for k in range(4):
            @pl.when(has_corner[k])
            def _():
                corner_copy(turn, k).start()

    def send_rows(turn, slot):
        exchange_start(h_copy(turn, slot), (2, 3))

    def store_rows(turn, c, i, value):
        y_send[turn, 0, 0, c, pl.ds(i, 1), :] = value[dy - 1 : dy]
        y_send[turn, 1, 0, c, pl.ds(i, 1), :] = value[0:1]
        y_send[turn, 0, 1, c, pl.ds(i, 1), :] = value[dy - 2 : dy - 1]
        y_send[turn, 1, 1, c, pl.ds(i, 1), :] = value[1:2]

    def corners_wait(turn):
        for k in range(4):
            @pl.when(has_corner[k])
            def _():
                corner_arrival(turn, k).wait_recv()
        for k in range(4):
            @pl.when(has_corner[k])
            def _():
                corner_copy(turn, k).wait_send()

    def nearest(turn, s, c):
        return recv_x[turn, s, c, 1 - s]

    def place_faces(turn, slot):
        for c in range(3):
            u[slot, c, 0] = permute(nearest(turn, 0, c), 2)
            u[slot, c, dx + 1] = permute(nearest(turn, 1, c), 1)

    def sweep_send(plane, turn, slot, carry):
        for i in range(DEPTH):
            carry = plane(i, carry)
            carry = plane(dx - 1 - i, carry)
        send_faces(turn, slot)
        send_corners(turn, slot)
        carry = lax.fori_loop(DEPTH, dx - DEPTH, plane, carry, unroll=INNER)
        send_rows(turn, slot)
        return carry

    def sweep_receive(plane, turn, slot, carry, faces_done):
        exchange_wait(h_copy(turn, slot), (2, 3))
        carry = lax.fori_loop(1, dx - 1, plane, carry, unroll=SWEEP)
        exchange_wait(h_copy(turn, slot), (0, 1))
        corners_wait(turn)
        place_faces(turn, slot)
        faces_done()
        carry = plane(0, carry)
        carry = plane(dx - 1, carry)
        return carry

    wx[0] = 0.5 * (shear[0] + shear[1])
    wx[dx] = 0.5 * (shear[dx] + shear[dx + 1])

    def weight_plane(i, best):
        s = shear[i + 1]
        xp = 0.5 * (s + shear[i + 2])
        wx[i + 1] = xp
        xm = 0.5 * (s + shear[i])
        ym, yp = rows_near(s, s_recv[2, pl.ds(i, 1), :], s_recv[3, pl.ds(i, 1), :])
        ym = 0.5 * (s + ym)
        yp = 0.5 * (s + yp)
        zm, zp = z_near(s)
        zm = 0.5 * (s + zm)
        zp = 0.5 * (s + zp)
        wyp[i] = yp
        wym[i] = ym
        wzp[i] = jnp.where(lane == dz - 1, 0.0, zp)
        wzm[i] = jnp.where(lane == 0, 0.0, zm)
        total = xp + xm + yp + ym + jnp.where(lane == dz - 1, s, zp) + jnp.where(lane == 0, s, zm)
        bulk = hb[i]
        diagonal = total + 1.5 * bulk
        inv = 1.0 / diagonal
        invd[i] = inv
        dg[i] = total + bulk
        hb[i] = 0.5 * bulk
        for c in range(3):
            d0 = rhs[c, i] * inv
            u[0, c, i + 1] = d0
            store_rows(0, c, i, d0)
        return jnp.maximum(best, (2.0 * total + 2.5 * bulk) / diagonal)

    best = jnp.zeros((dy, dz), jnp.float32)
    best = lax.fori_loop(0, dx, weight_plane, best, unroll=UNROLL)
    m_own[...] = jnp.broadcast_to(jnp.max(best, axis=0, keepdims=True), m_own.shape)

    def m_copy(k):
        peer = (b if k < ng else partner, lax.rem(g + k, ng))
        return remote(m_own, m_all.at[k], m_ssem.at[k], m_rsem.at[k], peer)

    def m2_copy(k):
        peer = (lax.rem(b + k * stride, nb), g)
        return remote(m2_own, m2_all.at[k], m2_ssem.at[k], m2_rsem.at[k], peer)

    m_copies = [m_copy(k) for k in range(1, 2 * ng if paired else ng)]
    m2_copies = [m2_copy(k) for k in range(1, nb // stride)]
    for copy in m_copies[::-1]:
        copy.start()
    send_faces(0, 0)
    send_rows(0, 0)
    exchange_wait(t_copy, (4,))
    index[2] = index_recv[...]
    undo_below = jnp.zeros((dy, dz), jnp.int32)
    for k in range(dy):
        at = jnp.broadcast_to(index_recv[k : k + 1, :], (dy, dz))
        undo_below = jnp.where(row == at, k, undo_below)
    index[3] = undo_below
    below_shear = permute(shear[1], 3)
    faces[0] = below_shear
    for k, (sx, sy) in enumerate(corners):
        y = (dy - 1) * sy
        plane = shear[(1, dx)[sx]]
        other = (below_shear, s_send_up[...])[sx]
        corner_send[0, k, 6:7, :] = plane[y : y + 1]
        corner_send[0, k, 7:8, :] = other[y : y + 1]
    send_corners(0, 0)

    def apply_plane(i, slot, low, high):
        v = [u[slot, c, i + 1] for c in range(3)]
        coupled = hb[i] * (v[0] + v[1] + v[2])
        out = []
        for c in range(3):
            ym, yp = rows_near(v[c], low(c, i), high(c, i))
            zm, zp = z_near(v[c])
            near = wx[i] * u[slot, c, i] + wx[i + 1] * u[slot, c, i + 2]
            near = near + wym[i] * ym + wyp[i] * yp + wzm[i] * zm + wzp[i] * zp
            out.append(dg[i] * v[c] + coupled - near)
        return v, out

    def recv_rows(turn):
        return (
            lambda c, i: recv_y[turn, 0, 0, c, pl.ds(i, 1), :],
            lambda c, i: recv_y[turn, 1, 0, c, pl.ds(i, 1), :],
        )

    ghost_rows = (
        lambda c, i: gy[0, c, pl.ds(i, 1), :],
        lambda c, i: gy[1, c, pl.ds(i, 1), :],
    )

    def bcoef(k):
        return jnp.broadcast_to(coef[k : k + 1, :], (dy, dz))

    def ghost_weights(d, cross, low, high):
        near, far, bulk = [static_recv[d, k] for k in range(3)]
        inner = 0.5 * (near + far)
        across = 0.5 * (near + cross)
        rm, rp = rows_near(near, low, high)
        rm = 0.5 * (near + rm)
        rp = 0.5 * (near + rp)
        zm, zp = z_near(near)
        zm = 0.5 * (near + zm)
        zp = 0.5 * (near + zp)
        total = inner + across + rm + rp
        total = total + jnp.where(lane == dz - 1, near, zp) + jnp.where(lane == 0, near, zm)
        inv = jnp.where(has[d], 1.0, 0.0) / (total + 1.5 * bulk)
        zm = jnp.where(lane == 0, 0.0, zm)
        zp = jnp.where(lane == dz - 1, 0.0, zp)
        for k, value in enumerate(
            (inner, across, rm, rp, zm, zp, total + bulk, 0.5 * bulk, inv)
        ):
            ghost[d, k] = value

    def all_ghost_weights():
        def edge(inside, corner, at, own):
            return jnp.where(inside, recv_d[0, corner, at : at + 1, :], own)

        for d in range(4):
            s = d % 2
            near = static_recv[d, 0]
            ends = near[0:1], near[dy - 1 : dy]
            if d < 2:
                cross = (faces[0], s_send_up[...])[s]
                low = edge(has[2], 2 * s, 6, ends[0])
                high = edge(has[3], 2 * s + 1, 6, ends[1])
            else:
                cross = s_send_y[1 - s]
                low = edge(has[0], s, 7, ends[0])
                high = edge(has[1], 2 + s, 7, ends[1])
            ghost_weights(d, cross, low, high)

    def ghost_apply(d, v, inner, cross, low, high):
        w = [ghost[d, k] for k in range(9)]
        coupled = w[7] * (v[0] + v[1] + v[2])
        out = []
        for c in range(3):
            rm, rp = rows_near(v[c], low[c], high[c])
            zm, zp = z_near(v[c])
            near = w[0] * inner[c] + w[1] * cross[c] + w[2] * rm + w[3] * rp
            near = near + w[4] * zm + w[5] * zp
            out.append(w[8] * (w[6] * v[c] + coupled - near))
        return out

    def ghost_step(turn, other, update, directions=(0, 1, 2, 3), ends=True):
        none = [jnp.zeros((1, dz), jnp.float32)] * 3
        for d in directions:
            s = d % 2
            if d < 2:
                v = [nearest(turn, s, c) for c in range(3)]
                inner = [recv_x[turn, s, c, s] for c in range(3)]
                cross = [mixed[s, c] for c in range(3)]
                low = [recv_d[turn, 2 * s, c : c + 1, :] for c in range(3)]
                high = [recv_d[turn, 2 * s + 1, c : c + 1, :] for c in range(3)]
            else:
                v = [recv_y[turn, s, 0, c] for c in range(3)]
                inner = [recv_y[turn, s, 1, c] for c in range(3)]
                cross = [y_send[turn, 1 - s, 0, c] for c in range(3)]
                low, high = none, none
                if ends:
                    low = [recv_d[turn, s, 3 + c : 4 + c, :] for c in range(3)]
                    high = [recv_d[turn, 2 + s, 3 + c : 4 + c, :] for c in range(3)]
            out = ghost_apply(d, v, inner, cross, low, high)
            for c in range(3):
                new = update(d, c, v[c], out[c])
                if d < 2:
                    u[other, c, (dx + 1) * s] = permute(new, 2 - s)
                else:
                    gy[s, c] = new

    top = m_own[...]
    for k, copy in enumerate(m_copies):
        copy.wait()
        top = jnp.maximum(top, m_all[k + 1])
    m2_own[...] = top
    for copy in m2_copies:
        copy.start()

    for d in range(2):
        i = (dx - 2, 1)[d]
        pack_send[d, 0] = invd[i]
        pack_send[d, 1] = hb[i]
        pack_send[d, 2] = jnp.where(row == 0, wym[i], jnp.where(row == dy - 1, wyp[i], 0.0))
    for d, y in ((2, dy - 2), (3, 1)):
        pack_send[d, 2] = zero_face
        pack_send[d, 2, 0:1, :] = wx[0, y : y + 1, :]
        pack_send[d, 2, dx - 1 : dx, :] = wx[dx, y : y + 1, :]
        for i in range(dx):
            pack_send[d, 0, i : i + 1, :] = invd[i, y : y + 1, :]
            pack_send[d, 1, i : i + 1, :] = hb[i, y : y + 1, :]
    for sx in range(2):
        i = (dx - 1) * sx
        values = (
            invd[i], hb[i], wx[dx * sx],
            jnp.where(row == 0, wym[i], 0.0), jnp.where(row == dy - 1, wyp[i], 0.0),
            shear[i + 1],
        )
        for k, value in enumerate(values):
            other = permute(value, (3, 0)[sx])
            for sy in range(2):
                y = (dy - 1) * sy
                corner_pack[2 * sx + sy, k : k + 1, :] = value[y : y + 1]
                corner_pack[2 * sx + sy, 8 + k : 9 + k, :] = other[y : y + 1]

    def p_copy(d):
        return remote(
            pack_send.at[d], pack_recv.at[d], p_ssem.at[d], p_rsem.at[d], peers[d]
        )

    def k_copy(k, at):
        return remote(
            corner_pack.at[k], recv_k.at[at], p_ssem.at[4 + k], p_rsem.at[4 + at],
            corner_peer[k],
        )

    exchange_start(p_copy)
    for k in range(4):
        @pl.when(has_corner[k])
        def _():
            k_copy(k, 3 - k).start()
    exchange_wait(t_copy)

    low, high = recv_rows(0)

    def first_plane(i, _):
        _, out = apply_plane(i, 0, low, high)
        inv = invd[i]
        for c in range(3):
            r[c, i] = out[c]
            u[1, c, i + 1] = out[c] * inv
        return 0

    def first_ghosts():
        all_ghost_weights()

        def update(d, c, v, out):
            before[d, c] = out
            return out

        ghost_step(0, 1, update)

    sweep_receive(first_plane, 0, 0, 0, first_ghosts)

    def second_plane(i, _):
        _, out = apply_plane(i, 1, *ghost_rows)
        for c in range(3):
            res[c, i] = out[c]
        return 0

    lax.fori_loop(0, dx, second_plane, 0, unroll=8)

    for k, copy in enumerate(m2_copies):
        copy.wait()
        top = jnp.maximum(top, m2_all[k + 1])
    upper = BOUND_MARGIN * jnp.broadcast_to(jnp.max(top, axis=1, keepdims=True), top.shape)
    lower = LOW_RATIO * upper
    theta = 0.5 * (upper + lower)
    delta = 0.5 * (upper - lower)
    sigma = theta / delta
    damping = 1.0 / sigma
    inv_theta = 1.0 / theta
    coef[0:8] = inv_theta
    rows = []
    for turn in range(1, CHEB):
        following = 1.0 / (2.0 * sigma - damping)
        rows.append((following * damping, 2.0 * following / delta))
        damping = following
    for turn, (a, c2) in enumerate(rows):
        coef[8 + 2 * turn : 9 + 2 * turn] = a[0:1]
        coef[9 + 2 * turn : 10 + 2 * turn] = c2[0:1]
    coef[14:15] = (rows[0][0] * inv_theta + rows[0][1])[0:1]
    coef[15:16] = (rows[0][1] * inv_theta)[0:1]
    (a, c2), (a_next, c_next) = rows[1], rows[2]
    ratio = c_next / c2
    coef[16:17] = (a_next + ratio)[0:1]
    coef[17:18] = (ratio * a)[0:1]
    coef[18:19] = (rows[0][0] + rows[0][1] * theta)[0:1]

    alpha, beta, it = bcoef(14), bcoef(15), bcoef(0)
    both_it = alpha + it
    a_two, c_two = bcoef(10), bcoef(11)

    def combine_plane(i, _):
        inv = invd[i]
        for c in range(3):
            d0 = u[0, c, i + 1]
            one = alpha * d0 - beta * u[1, c, i + 1]
            sol[c, i] = it * d0 + one
            rest = rhs[c, i] - both_it * r[c, i] + beta * res[c, i]
            res[c, i] = rest
            two = a_two * one + c_two * (rest * inv)
            u[0, c, i + 1] = two
            store_rows(1, c, i, two)
        return 0

    sweep_send(combine_plane, 1, 0, 0)
    for d in range(4):
        for c in range(3):
            v = nearest(0, d, c) if d < 2 else recv_y[0, d - 2, 0, c]
            before[d, c] = alpha * v - beta * before[d, c]

    def step_plane(slot, low, high, a, c2, following, summed=False, rows_of=None):
        other = 1 - slot

        def plane(i, sums):
            v, out = apply_plane(i, slot, low, high)
            inv = invd[i]
            new = []
            for c in range(3):
                rest = res[c, i] - out[c]
                res[c, i] = rest
                sol[c, i] = sol[c, i] + v[c]
                if summed:
                    new.append(sums[c] + rest)
                if not following:
                    continue
                ahead = c2 * (rest * inv)
                if a is not None:
                    ahead = ahead + a * v[c]
                u[other, c, i + 1] = ahead
                if rows_of is not None:
                    store_rows(rows_of, c, i, ahead)
            return tuple(new)
        return plane

    def pair_ghosts(turn, other):
        def done(directions=(0, 1, 2, 3), ends=True):
            e1, e2, e3 = bcoef(16), bcoef(17), bcoef(13)

            def update(d, c, v, out):
                return e1 * v - e2 * before[d, c] - e3 * out

            ghost_step(turn, other, update, directions, ends)
        return done

    def pair_receive(turn, slot, first, second, carry, ghosts):
        exchange_wait(h_copy(turn, slot), (2, 3))
        lax.fori_loop(1, dx - 1, first, (), unroll=SWEEP)
        ghosts((2, 3), False)
        carry = lax.fori_loop(2, dx - 2, second, carry, unroll=INNER)
        exchange_wait(h_copy(turn, slot), (0, 1))
        corners_wait(turn)
        place_faces(turn, slot)
        ghosts()
        for i in (0, dx - 1):
            first(i, ())
        for i in (0, 1, dx - 2, dx - 1):
            carry = second(i, carry)
        return carry

    def i_copy(d):
        return remote(inverse, inv_recv.at[d], i_ssem.at[d], i_rsem.at[d], peers[d])

    exchange_start(i_copy, (0, 1))
    first = step_plane(0, *recv_rows(1), bcoef(12), bcoef(13), True)
    second = step_plane(1, *ghost_rows, None, bcoef(0), True, summed=True, rows_of=2)
    init = tuple(jnp.zeros((dy, dz), jnp.float32) for _ in range(3))
    sums = pair_receive(1, 0, first, second, init, pair_ghosts(1, 1))

    c_own[...] = jnp.zeros(c_own.shape, jnp.float32)
    for c in range(3):
        c_own[c : c + 1, :] = jnp.sum(sums[c], axis=0, keepdims=True)
    c_all[1, g] = c_own[...]

    def c_copy(q, k):
        slot = q * ng + k
        return remote(
            c_own, c_all.at[q, g], c_ssem.at[slot], c_rsem.at[slot],
            (b + 1 - q, lax.rem(g + k, ng)),
        )

    def c_arrival(q, k):
        slot = q * ng + k
        source = lax.rem(g + ng - k, ng)
        return remote(
            c_own, c_all.at[q, source], c_ssem.at[slot], c_rsem.at[slot],
            (b + 1 - q, lax.rem(g + k, ng)),
        )

    def coarse_all(to_do, flags):
        for q in (0, 2, 1):
            first = 1 if q == 1 else 0
            if q == 1:
                for k in range(first, ng):
                    to_do(q, k)
                continue

            @pl.when(flags[q])
            def _():
                for k in range(first, ng):
                    to_do(q, k)

    coarse_all(lambda q, k: c_copy(q, k).start(), {0: has[1], 2: has[0]})
    send_faces(2, 0)
    send_corners(2, 0)
    send_rows(2, 0)
    f_all[...] = jnp.zeros(f_all.shape, jnp.float32)
    exchange_wait(p_copy)
    for k in range(4):
        @pl.when(has_corner[k])
        def _():
            k_copy(k, k).wait_recv()
    for k in range(4):
        @pl.when(has_corner[k])
        def _():
            k_copy(k, k).wait_send()
    for k in range(4):
        for n in range(6):
            for side in range(2):
                at = 2 * k + side
                corner_rows[n, at : at + 1, :] = recv_k[k, 8 * side + n : 8 * side + n + 1, :]
    exchange_wait(i_copy, (0, 1))
    coarse_all(lambda q, k: c_arrival(q, k).wait_recv(), {0: has[0], 2: has[1]})
    coarse_all(lambda q, k: c_copy(q, k).wait_send(), {0: has[1], 2: has[0]})

    cells_z = dz // BLOCK_Z
    size = 3 * cells_z * ng
    flat = c_all[...].reshape(3 * ng * 8, dz)
    li = lax.broadcasted_iota(jnp.int32, (dz, size), 0)
    ki = lax.broadcasted_iota(jnp.int32, (dz, size), 1)
    gather = jnp.where(li // BLOCK_Z == ki % cells_z, 1.0 / (dx * dy * BLOCK_Z), 0.0)
    spread = jnp.dot(flat, gather, precision=HIGHEST, preferred_element_type=jnp.float32)
    ri = lax.broadcasted_iota(jnp.int32, (ng * 8, size), 0)
    kk = lax.broadcasted_iota(jnp.int32, (ng * 8, size), 1) // cells_z
    mine = (ri // 8 == kk // 3) & (ri % 8 == kk % 3)
    bi = lax.broadcasted_iota(jnp.int32, (size, dz), 0)
    bl = lax.broadcasted_iota(jnp.int32, (size, dz), 1)
    placed = bi % cells_z == bl // BLOCK_Z
    for q in range(3):
        part = spread[q * ng * 8 : (q + 1) * ng * 8]
        vector = jnp.sum(jnp.where(mine, part, 0.0), axis=0, keepdims=True)
        matrix = inverse[...] if q == 1 else inv_recv[q // 2]
        correction = jnp.sum(matrix * vector, axis=1, keepdims=True)
        table = jnp.where(placed, jnp.broadcast_to(correction, (size, dz)), 0.0)
        for k in range(ng):
            for c in range(3):
                start = (k * 3 + c) * cells_z
                f_all[q, k + 1, c : c + 1, :] = jnp.sum(
                    table[start : start + cells_z], axis=0, keepdims=True
                )

    def full(q, at, c):
        return jnp.broadcast_to(f_all[q, at, c : c + 1, :], (dy, dz))

    own_fine = [full(1, g + 1, c) for c in range(3)]

    fine_sides = [z_near(own_fine[c]) for c in range(3)]
    fine_rows = [
        (
            jnp.where(row == 0, full(1, g, c), own_fine[c]),
            jnp.where(row == dy - 1, full(1, g + 2, c), own_fine[c]),
        )
        for c in range(3)
    ]
    fine_sum = own_fine[0] + own_fine[1] + own_fine[2]
    it = bcoef(0)

    def fine_plane(i, _):
        inv = invd[i]
        coupled = hb[i] * fine_sum
        for c in range(3):
            f = own_fine[c]
            first, last = isinstance(i, int) and i == 0, isinstance(i, int) and i == dx - 1
            xm = full(0, g + 1, c) if first else f
            xp = full(2, g + 1, c) if last else f
            near = wx[i] * xm + wx[i + 1] * xp
            near = near + wym[i] * fine_rows[c][0] + wyp[i] * fine_rows[c][1]
            near = near + wzm[i] * fine_sides[c][0] + wzp[i] * fine_sides[c][1]
            rest = res[c, i] - (dg[i] * f + coupled - near)
            res[c, i] = rest
            sol[c, i] = sol[c, i] + f
            ahead = it * (rest * inv)
            u[0, c, i + 1] = ahead
            y_send[2, 0, 0, c, pl.ds(i, 1), :] = ahead[dy - 1 : dy]
            y_send[2, 1, 0, c, pl.ds(i, 1), :] = ahead[0:1]
        return 0

    exchange_wait(h_copy(2, 0))
    corners_wait(2)
    for i in range(4):
        fine_plane(i, 0)
        fine_plane(dx - 1 - i, 0)
    for c in range(3):
        mixed[0, c] = permute(u[0, c, 1], 3)
        mixed[1, c] = permute(u[0, c, dx], 0)

    def fine_far(here, low, high, inv, half, w_low, w_high, near, across=None):
        lanes = lane[: near.shape[0]]
        zm, zp = z_near(near)
        zm = jnp.where(lanes == 0, 0.0, 0.5 * (near + zm))
        zp = jnp.where(lanes == dz - 1, 0.0, 0.5 * (near + zp))
        rim = jnp.where((lanes == 0) | (lanes == dz - 1), near, 0.0)
        weight = 2.0 * half + w_low + w_high + zm + zp + rim
        if across is not None:
            weight = weight + across[0]
        coupled = half * (here[0] + here[1] + here[2])
        out = []
        for c in range(3):
            fm, fp = z_near(here[c])
            value = weight * here[c] + coupled - zm * fm - zp * fp
            value = value - w_low * low[c] - w_high * high[c]
            if across is not None:
                value = value - across[0] * across[1][c]
            out.append(inv * value)
        return out

    for d in range(4):
        s = d % 2
        if d < 2:
            spots = (2 * s, g + 1), (2 * s, g), (2 * s, g + 2)
        else:
            at = g + 2 * s
            spots = (1, at), (0, at), (2, at)
        here, low, high = [[full(*spot, c) for c in range(3)] for spot in spots]
        out = ghost_apply(d, here, here, own_fine, low, high)
        inv, half, rim = [pack_recv[d, k] for k in range(3)]
        w_low = jnp.where(row == 0, rim, 0.0)
        w_high = jnp.where(row == dy - 1, rim, 0.0)
        far = fine_far(here, low, high, inv, half, w_low, w_high, static_recv[d, 1])
        for c in range(3):
            if d < 2:
                recv_x[2, s, c, 1 - s] = nearest(2, s, c) - it * out[c]
                recv_x[2, s, c, s] = recv_x[2, s, c, s] - it * far[c]
            else:
                recv_y[2, s, 0, c] = recv_y[2, s, 0, c] - it * out[c]
                recv_y[2, s, 1, c] = recv_y[2, s, 1, c] - it * far[c]

    for k, (sx, sy) in enumerate(corners):
        q, at = 2 * sx, g + 2 * sy
        spots = (q, at), (q, jnp.maximum(at - 1, 0)), (q, jnp.minimum(at + 1, ng + 1)), (1, at)
        for n, spot in enumerate(spots):
            for c in range(3):
                value = f_all[(*spot, slice(c, c + 1))]
                spread_k[n, c, 2 * k : 2 * k + 1, :] = value
                spread_k[n, c, 2 * k + 1 : 2 * k + 2, :] = value
        for c in range(3):
            for n in range(2):
                at = 2 * k + n
                spread_k[4, c, at : at + 1, :] = recv_d[2, k, 3 * n + c : 3 * n + c + 1, :]
    here, low, high, beside = [[spread_k[n, c] for c in range(3)] for n in range(4)]
    inv, half, cross, w_low, w_high, near = [corner_rows[n] for n in range(6)]
    out = fine_far(here, low, high, inv, half, w_low, w_high, near, (cross, beside))
    for c in range(3):
        spread_k[4, c] = spread_k[4, c] - it[0:8] * out[c]
    for k in range(4):
        for c in range(3):
            for n in range(2):
                at = 2 * k + n
                recv_d[2, k, 3 * n + c : 3 * n + c + 1, :] = spread_k[4, c, at : at + 1, :]

    place_faces(2, 0)
    e1, e3 = bcoef(18), bcoef(9)

    def first_update(d, c, v, out):
        new = e1 * v - e3 * out
        before[d, c] = new
        return new

    first = step_plane(0, *recv_rows(2), bcoef(8), bcoef(9), True)
    second = step_plane(1, *ghost_rows, bcoef(10), bcoef(11), True, rows_of=3)
    ghost_step(2, 1, first_update)
    for i in range(3):
        first(i, ())
        first(dx - 1 - i, ())
    for i in range(2):
        second(i, ())
        second(dx - 1 - i, ())
    send_faces(3, 0)
    send_corners(3, 0)
    lax.fori_loop(4, dx - 4, fine_plane, 0, unroll=8)
    ghost_step(2, 1, first_update, (2, 3))
    lax.fori_loop(3, dx - 3, first, (), unroll=5)
    lax.fori_loop(2, dx - 2, second, (), unroll=INNER)
    send_rows(3, 0)
    first = step_plane(0, *recv_rows(3), bcoef(12), bcoef(13), True)
    second = step_plane(1, *ghost_rows, None, None, False)
    pair_receive(3, 0, first, second, (), pair_ghosts(3, 1))


def per_device(rhs, material, level, mortar, mu, lam, inverse):
    nb = lax.axis_size("bricks")
    ng = lax.axis_size("group")
    dx, dy, dz = material.shape
    f32 = jnp.float32
    vmem = pl.BlockSpec(memory_space=pltpu.VMEM)
    smem = pl.BlockSpec(memory_space=pltpu.SMEM)
    hbm = pl.BlockSpec(memory_space=pltpu.HBM)
    dma = pltpu.SemaphoreType.DMA
    grid = pltpu.VMEM((dx, dy, dz), f32)
    cg = inverse.shape[1]
    scratch = [
        pltpu.VMEM((3, dx, dy, dz), f32),
        pltpu.VMEM((dx, dy, dz), jnp.int32),
        pltpu.VMEM((cg, cg), f32),
        pltpu.VMEM((2, 3, dx + 2, dy, dz), f32),
        pltpu.VMEM((3, dx, dy, dz), f32),
        pltpu.VMEM((dx + 2, dy, dz), f32),
        pltpu.VMEM((dx + 1, dy, dz), f32),
        grid, grid, grid, grid, grid, grid, grid,
        pltpu.VMEM((24, dz), f32),
        pltpu.VMEM((dy, dz), f32),
        pltpu.VMEM((2, dx, dz), f32),
        pltpu.VMEM((4, dx, dz), f32),
        pltpu.VMEM((4, 3, dx, dz), f32),
        pltpu.VMEM((4, 3, dx, dz), f32),
        pltpu.VMEM((dy, dz), jnp.int32),
        pltpu.VMEM((dy, dz), jnp.int32),
        pltpu.VMEM((4, dy, dz), jnp.int32),
        pltpu.VMEM((1, dy, dz), f32),
        pltpu.VMEM((2, 3, dy, dz), f32),
        pltpu.VMEM((ROUNDS, 2, 2, 3, dx, dz), f32),
        pltpu.VMEM((ROUNDS, 4, 8, dz), f32),
        pltpu.VMEM((ROUNDS, 2, 3, 2, dy, dz), f32),
        pltpu.VMEM((ROUNDS, 2, 2, 3, dx, dz), f32),
        pltpu.VMEM((ROUNDS, 4, 8, dz), f32),
        pltpu.VMEM((4, 9, dy, dz), f32),
        pltpu.VMEM((2, 3, dx, dz), f32),
        pltpu.VMEM((4, 3, dy, dz), f32),
        pltpu.VMEM((4, 3, dx, dz), f32),
        pltpu.VMEM((4, 3, dx, dz), f32),
        pltpu.VMEM((4, 16, dz), f32),
        pltpu.VMEM((4, 16, dz), f32),
        pltpu.VMEM((6, 8, dz), f32),
        pltpu.VMEM((5, 3, 8, dz), f32),
        pltpu.VMEM((8, dz), f32),
        pltpu.VMEM((2 * ng, 8, dz), f32),
        pltpu.VMEM((8, dz), f32),
        pltpu.VMEM((nb, 8, dz), f32),
        pltpu.VMEM((8, dz), f32),
        pltpu.VMEM((3, ng, 8, dz), f32),
        pltpu.VMEM((3, ng + 2, 8, dz), f32),
        pltpu.VMEM((2, cg, cg), f32),
        dma((3,)),
        dma((4,)), dma((4,)),
        dma((5,)), dma((5,)),
        dma((ROUNDS, 8)), dma((ROUNDS, 8)),
        dma((8,)), dma((8,)),
        dma((2 * ng,)), dma((2 * ng,)),
        dma((nb,)), dma((nb,)),
        dma((3 * ng,)), dma((3 * ng,)),
        dma((2,)), dma((2,)),
    ]
    rhs, material, inverse, mortar, mu, lam = (
        pltpu.with_memory_space_constraint(x, pltpu.HBM)
        for x in (rhs, material, inverse, mortar, mu, lam)
    )
    both = pl.pallas_call(
        functools.partial(kernel, nb, ng, dx, dy, dz),
        out_shape=jax.ShapeDtypeStruct((2, *rhs.shape), f32),
        in_specs=[hbm, hbm, vmem, smem, smem, smem, hbm],
        out_specs=vmem,
        scratch_shapes=scratch,
        compiler_params=pltpu.CompilerParams(
            collective_id=0, has_side_effects=True, vmem_limit_bytes=16 * 2**20
        ),
    )(rhs, material, level, mortar, mu, lam, inverse)
    return both[0], both[1]


def solution(mesh):
    return jax.shard_map(
        per_device,
        mesh=mesh,
        in_specs=(
            P(None, "bricks", "group", None),
            P("bricks", "group", None),
            P("bricks", "group"),
            P("bricks", "group", None),
            P(),
            P(),
            P("bricks", None, None),
        ),
        out_specs=(P(None, "bricks", "group", None), P(None, "bricks", "group", None)),
        check_vma=False,
    )
```

```python
import functools

import jax
import jax.numpy as jnp
from jax import lax
from jax.experimental import pallas as pl
from jax.experimental.pallas import tpu as pltpu
from jax.sharding import PartitionSpec as P

BLOCK_Z = 32
CHEB = 4
LOW_RATIO = 0.15
BOUND_MARGIN = 1.1
ROUNDS = 4
UNROLL = 4
DEPTH = 2
SWEEP = 14
INNER = 12
HIGHEST = lax.Precision.HIGHEST


def kernel(
    nb, ng, dx, dy, dz,
    rhs_in, material_in, level, mortar, mu, lam, inverse_in,
    result, rhs, material, inverse,
    u, r, shear, wx, wyp, wym, wzp, wzm, dg, hb, invd, coef,
    s_send_up, s_send_y, s_recv, static_send, static_recv, index_send, index_recv, index,
    faces, mixed, y_send, corner_send, recv_x, recv_y, recv_d, ghost, gy, before,
    pack_send, pack_recv, corner_pack, recv_k, corner_rows, spread_k,
    m_own, m_all, m2_own, m2_all, c_own, c_all, f_all, inv_recv, in_sem,
    s_ssem, s_rsem, t_ssem, t_rsem, h_ssem, h_rsem, p_ssem, p_rsem,
    m_ssem, m_rsem, m2_ssem, m2_rsem, c_ssem, c_rsem, i_ssem, i_rsem,
):
    sol, res = result.at[0], result.at[1]
    b = lax.axis_index("bricks")
    g = lax.axis_index("group")
    has = [b > 0, b < nb - 1, g > 0, g < ng - 1]
    sends = [has[1], has[0], has[3], has[2]]
    peers = [(b + 1, g), (b - 1, g), (b, g + 1), (b, g - 1)]
    corners = [(0, 0), (0, 1), (1, 0), (1, 1)]
    has_corner = [has[sx] & has[2 + sy] for sx, sy in corners]
    corner_peer = [(b + 2 * sx - 1, g + 2 * sy - 1) for sx, sy in corners]

    def remote(src, dst, ssem, rsem, peer):
        return pltpu.make_async_remote_copy(
            src_ref=src, dst_ref=dst, send_sem=ssem, recv_sem=rsem,
            device_id=peer, device_id_type=pl.DeviceIdType.MESH,
        )

    barrier = pltpu.get_barrier_semaphore()
    paired = nb % 2 == 0
    stride = 2 if paired else 1
    partner = b + 1 - 2 * lax.rem(b, 2)
    others = [(b, lax.rem(g + k, ng)) for k in range(1, ng)]
    others += [(lax.rem(b + k, nb), g) for k in range(stride, nb, stride)]
    around = [lax.rem(g + k, ng) for k in range(0 if paired else 1, ng)]
    for peer in others:
        pl.semaphore_signal(
            barrier, inc=1, device_id=peer, device_id_type=pl.DeviceIdType.MESH
        )
    for d in range(2):
        @pl.when(has[d])
        def _():
            for at in around:
                pl.semaphore_signal(
                    barrier, inc=1, device_id=(b - 1 + 2 * d, at),
                    device_id_type=pl.DeviceIdType.MESH,
                )

    def fetch(k):
        source = [material_in, rhs_in, inverse_in.at[0]][k]
        return pltpu.make_async_copy(source, [material, rhs, inverse][k], in_sem.at[k])

    for k in range(3):
        fetch(k).start()

    row = lax.broadcasted_iota(jnp.int32, (dy, dz), 0)
    lane = lax.broadcasted_iota(jnp.int32, (dy, dz), 1)
    grade = jnp.broadcast_to(level[...], (dy, dz))
    scale = jnp.where(grade == 0, 1.0, jnp.where(grade == 1, 4.0, 16.0))
    zero_face = jnp.zeros((dy, dz), jnp.float32)

    order = [mortar[0, 0, k] for k in range(dy)]
    order_here = jnp.zeros((dy, dz), jnp.int32)
    undo_here = jnp.zeros((dy, dz), jnp.int32)
    for k in range(dy):
        order_here = jnp.where(row == k, order[k], order_here)
        undo_here = jnp.where(row == order[k], k, undo_here)
    index_send[...] = order_here
    index[0] = order_here
    index[1] = undo_here

    def permute(value, k):
        half = dy // 2
        parts = []
        for h in range(2):
            at = index[k, h * half : (h + 1) * half]
            within = jnp.bitwise_and(at, half - 1)
            low = jnp.take_along_axis(value[:half], within, axis=0)
            high = jnp.take_along_axis(value[half:], within, axis=0)
            parts.append(jnp.where(at < half, low, high))
        return jnp.concatenate(parts, axis=0)

    def lookup(ids, table):
        total = jnp.where(ids == 0, table[0], 0.0)
        for entry in range(1, 4):
            total = jnp.where(ids == entry, table[entry], total)
        return total * scale

    def shear_plane(i, _):
        ids = material[i]
        plane = lookup(ids, mu)
        bulk = lookup(ids, lam)
        shear[i + 1] = plane
        hb[i] = bulk
        s_send_y[0, pl.ds(i, 1), :] = plane[dy - 1 : dy]
        s_send_y[1, pl.ds(i, 1), :] = plane[0:1]
        for d, near, far in ((2, dy - 1, dy - 2), (3, 0, 1)):
            static_send[d, 0, pl.ds(i, 1), :] = plane[near : near + 1]
            static_send[d, 1, pl.ds(i, 1), :] = plane[far : far + 1]
            static_send[d, 2, pl.ds(i, 1), :] = bulk[near : near + 1]
        return 0

    fetch(0).wait()
    lax.fori_loop(0, dx, shear_plane, 0, unroll=UNROLL)
    s_send_up[...] = permute(shear[dx], 0)
    for d, near, far in ((0, dx - 1, dx - 2), (1, 0, 1)):
        static_send[d, 0] = shear[near + 1]
        static_send[d, 1] = shear[far + 1]
        static_send[d, 2] = hb[near]

    both = jnp.where(has[0], len(around), 0) + jnp.where(has[1], len(around), 0)
    pl.semaphore_wait(barrier, len(others) + both)

    def s_copy(d):
        src = [s_send_up, shear.at[1], s_send_y.at[0], s_send_y.at[1]][d]
        return remote(src, s_recv.at[d], s_ssem.at[d], s_rsem.at[d], peers[d])

    def t_copy(d):
        if d == 4:
            return remote(index_send, index_recv, t_ssem.at[4], t_rsem.at[4], peers[0])
        return remote(
            static_send.at[d], static_recv.at[d], t_ssem.at[d], t_rsem.at[d], peers[d]
        )

    def exchange_start(copy, directions=(0, 1, 2, 3)):
        for d in directions:
            @pl.when(sends[d % 4])
            def _():
                copy(d).start()

    def arrive_wait(copy, directions=(0, 1, 2, 3)):
        for d in directions:
            @pl.when(has[d % 4])
            def _():
                copy(d).wait_recv()

    def sent_wait(copy, directions=(0, 1, 2, 3)):
        for d in directions:
            @pl.when(sends[d % 4])
            def _():
                copy(d).wait_send()

    def exchange_wait(copy, directions=(0, 1, 2, 3)):
        arrive_wait(copy, directions)
        sent_wait(copy, directions)

    exchange_start(s_copy)
    exchange_start(t_copy, (4, 0, 1, 2, 3))

    @pl.when(b == 0)
    def _():
        s_recv[0] = shear[1]
        index_recv[...] = row

    @pl.when(b == nb - 1)
    def _():
        s_recv[1] = shear[dx]

    @pl.when(g == 0)
    def _():
        s_recv[2] = s_send_y[1]

    @pl.when(g == ng - 1)
    def _():
        s_recv[3] = s_send_y[0]

    for d in range(4):
        @pl.when(jnp.logical_not(has[d]))
        def _():
            one = jnp.ones((dy, dz), jnp.float32)
            for k in range(3):
                static_recv[d, k] = one
                pack_recv[d, k] = zero_face
            for turn in range(ROUNDS):
                for c in range(3):
                    for j in range(2):
                        if d < 2:
                            recv_x[turn, d, c, j] = zero_face
                        else:
                            recv_y[turn, d - 2, j, c] = zero_face
            if d < 2:
                inv_recv[d] = jnp.zeros(inv_recv.shape[1:], jnp.float32)
                c_all[2 * d] = jnp.zeros(c_all.shape[1:], jnp.float32)

    for k in range(4):
        @pl.when(jnp.logical_not(has_corner[k]))
        def _():
            for turn in range(ROUNDS):
                recv_d[turn, k] = jnp.zeros(recv_d.shape[2:], jnp.float32)
            recv_k[k] = jnp.zeros(recv_k.shape[1:], jnp.float32)

    fetch(1).wait()
    fetch(2).wait()
    exchange_wait(s_copy)
    shear[0] = s_recv[0]

    @pl.when(b < nb - 1)
    def _():
        shear[dx + 1] = permute(s_recv[1], 1)

    @pl.when(b == nb - 1)
    def _():
        shear[dx + 1] = shear[dx]

    def rows_near(v, low, high):
        half = dy // 2
        at = row[:half]
        parts = [v[:half], v[half:]]
        down = [pltpu.roll(part, 1, 0) for part in parts]
        up = [pltpu.roll(part, half - 1, 0) for part in parts]
        low = jnp.broadcast_to(low[:half], parts[0].shape)
        high = jnp.broadcast_to(high[:half], parts[0].shape)
        m = [jnp.where(at == 0, low, down[0]), jnp.where(at == 0, down[0], down[1])]
        p = [
            jnp.where(at == half - 1, up[1], up[0]),
            jnp.where(at == half - 1, high, up[1]),
        ]
        return jnp.concatenate(m, axis=0), jnp.concatenate(p, axis=0)

    def z_near(v):
        return pltpu.roll(v, 1, 1), pltpu.roll(v, dz - 1, 1)

    def h_copy(turn, slot):
        deep = DEPTH

        def copy(d):
            if d == 0:
                src = u.at[slot, :, dx + 1 - deep : dx + 1]
                dst = recv_x.at[turn, 0, :, 2 - deep : 2]
            elif d == 1:
                src = u.at[slot, :, 1 : 1 + deep]
                dst = recv_x.at[turn, 1, :, 0:deep]
            else:
                src = y_send.at[turn, d - 2, 0:deep]
                dst = recv_y.at[turn, d - 2, 0:deep]
            return remote(src, dst, h_ssem.at[turn, d], h_rsem.at[turn, d], peers[d])
        return copy

    def corner_copy(turn, k):
        return remote(
            corner_send.at[turn, k], recv_d.at[turn, 3 - k],
            h_ssem.at[turn, 4 + k], h_rsem.at[turn, 7 - k], corner_peer[k],
        )

    def corner_arrival(turn, k):
        return remote(
            corner_send.at[turn, k], recv_d.at[turn, k],
            h_ssem.at[turn, 4 + k], h_rsem.at[turn, 4 + k], corner_peer[k],
        )

    even = lax.rem(b, 2) == 0

    def send_faces(turn, slot):
        copy = h_copy(turn, slot)

        @pl.when(sends[1] & even)
        def _():
            copy(1).start()

        exchange_start(copy, (0,))

        @pl.when(sends[1] & jnp.logical_not(even))
        def _():
            copy(1).start()

    def send_corners(turn, slot):
        for c in range(3):
            bottom, top = u[slot, c, 1], u[slot, c, dx]
            mixed_low, mixed_high = permute(bottom, 3), permute(top, 0)
            mixed[0, c] = mixed_low
            mixed[1, c] = mixed_high
            for k, (sx, sy) in enumerate(corners):
                y = (dy - 1) * sy
                plane, other = ((bottom, mixed_low), (top, mixed_high))[sx]
                corner_send[turn, k, c : c + 1, :] = plane[y : y + 1]
                corner_send[turn, k, 3 + c : 4 + c, :] = other[y : y + 1]
        for k in range(4):
            @pl.when(has_corner[k])
            def _():
                corner_copy(turn, k).start()

    def send_rows(turn, slot):
        exchange_start(h_copy(turn, slot), (2, 3))

    def store_rows(turn, c, i, value):
        y_send[turn, 0, 0, c, pl.ds(i, 1), :] = value[dy - 1 : dy]
        y_send[turn, 1, 0, c, pl.ds(i, 1), :] = value[0:1]
        y_send[turn, 0, 1, c, pl.ds(i, 1), :] = value[dy - 2 : dy - 1]
        y_send[turn, 1, 1, c, pl.ds(i, 1), :] = value[1:2]

    def corners_wait(turn):
        for k in range(4):
            @pl.when(has_corner[k])
            def _():
                corner_arrival(turn, k).wait_recv()
        for k in range(4):
            @pl.when(has_corner[k])
            def _():
                corner_copy(turn, k).wait_send()

    def nearest(turn, s, c):
        return recv_x[turn, s, c, 1 - s]

    def place_faces(turn, slot):
        for c in range(3):
            u[slot, c, 0] = permute(nearest(turn, 0, c), 2)
            u[slot, c, dx + 1] = permute(nearest(turn, 1, c), 1)

    def sweep_send(plane, turn, slot, carry):
        for i in range(DEPTH):
            carry = plane(i, carry)
            carry = plane(dx - 1 - i, carry)
        send_faces(turn, slot)
        send_corners(turn, slot)
        carry = lax.fori_loop(DEPTH, dx - DEPTH, plane, carry, unroll=INNER)
        send_rows(turn, slot)
        return carry

    def sweep_receive(plane, turn, slot, carry, faces_done):
        exchange_wait(h_copy(turn, slot), (2, 3))
        carry = lax.fori_loop(1, dx - 1, plane, carry, unroll=SWEEP)
        exchange_wait(h_copy(turn, slot), (0, 1))
        corners_wait(turn)
        place_faces(turn, slot)
        faces_done()
        carry = plane(0, carry)
        carry = plane(dx - 1, carry)
        return carry

    wx[0] = 0.5 * (shear[0] + shear[1])
    wx[dx] = 0.5 * (shear[dx] + shear[dx + 1])

    def weight_plane(i, best):
        s = shear[i + 1]
        xp = 0.5 * (s + shear[i + 2])
        wx[i + 1] = xp
        xm = 0.5 * (s + shear[i])
        ym, yp = rows_near(s, s_recv[2, pl.ds(i, 1), :], s_recv[3, pl.ds(i, 1), :])
        ym = 0.5 * (s + ym)
        yp = 0.5 * (s + yp)
        zm, zp = z_near(s)
        zm = 0.5 * (s + zm)
        zp = 0.5 * (s + zp)
        wyp[i] = yp
        wym[i] = ym
        wzp[i] = jnp.where(lane == dz - 1, 0.0, zp)
        wzm[i] = jnp.where(lane == 0, 0.0, zm)
        total = xp + xm + yp + ym + jnp.where(lane == dz - 1, s, zp) + jnp.where(lane == 0, s, zm)
        bulk = hb[i]
        diagonal = total + 1.5 * bulk
        inv = 1.0 / diagonal
        invd[i] = inv
        dg[i] = total + bulk
        hb[i] = 0.5 * bulk
        for c in range(3):
            d0 = rhs[c, i] * inv
            u[0, c, i + 1] = d0
            store_rows(0, c, i, d0)
        return jnp.maximum(best, (2.0 * total + 2.5 * bulk) / diagonal)

    best = jnp.zeros((dy, dz), jnp.float32)
    best = lax.fori_loop(0, dx, weight_plane, best, unroll=16)
    m_own[...] = jnp.broadcast_to(jnp.max(best, axis=0, keepdims=True), m_own.shape)

    def m_copy(k):
        peer = (b if k < ng else partner, lax.rem(g + k, ng))
        return remote(m_own, m_all.at[k], m_ssem.at[k], m_rsem.at[k], peer)

    def m2_copy(k):
        peer = (lax.rem(b + k * stride, nb), g)
        return remote(m2_own, m2_all.at[k], m2_ssem.at[k], m2_rsem.at[k], peer)

    m_copies = [m_copy(k) for k in range(1, 2 * ng if paired else ng)]
    m2_copies = [m2_copy(k) for k in range(1, nb // stride)]
    for copy in m_copies[::-1]:
        copy.start()
    send_faces(0, 0)
    send_rows(0, 0)
    exchange_wait(t_copy, (4,))
    index[2] = index_recv[...]
    undo_below = jnp.zeros((dy, dz), jnp.int32)
    for k in range(dy):
        at = jnp.broadcast_to(index_recv[k : k + 1, :], (dy, dz))
        undo_below = jnp.where(row == at, k, undo_below)
    index[3] = undo_below
    below_shear = permute(shear[1], 3)
    faces[0] = below_shear
    for k, (sx, sy) in enumerate(corners):
        y = (dy - 1) * sy
        plane = shear[(1, dx)[sx]]
        other = (below_shear, s_send_up[...])[sx]
        corner_send[0, k, 6:7, :] = plane[y : y + 1]
        corner_send[0, k, 7:8, :] = other[y : y + 1]
    send_corners(0, 0)

    def apply_plane(i, slot, low, high):
        v = [u[slot, c, i + 1] for c in range(3)]
        coupled = hb[i] * (v[0] + v[1] + v[2])
        out = []
        for c in range(3):
            ym, yp = rows_near(v[c], low(c, i), high(c, i))
            zm, zp = z_near(v[c])
            near = wx[i] * u[slot, c, i] + wx[i + 1] * u[slot, c, i + 2]
            near = near + wym[i] * ym + wyp[i] * yp + wzm[i] * zm + wzp[i] * zp
            out.append(dg[i] * v[c] + coupled - near)
        return v, out

    def recv_rows(turn):
        return (
            lambda c, i: recv_y[turn, 0, 0, c, pl.ds(i, 1), :],
            lambda c, i: recv_y[turn, 1, 0, c, pl.ds(i, 1), :],
        )

    ghost_rows = (
        lambda c, i: gy[0, c, pl.ds(i, 1), :],
        lambda c, i: gy[1, c, pl.ds(i, 1), :],
    )

    def bcoef(k):
        return jnp.broadcast_to(coef[k : k + 1, :], (dy, dz))

    def ghost_weights(d, cross, low, high):
        near, far, bulk = [static_recv[d, k] for k in range(3)]
        inner = 0.5 * (near + far)
        across = 0.5 * (near + cross)
        rm, rp = rows_near(near, low, high)
        rm = 0.5 * (near + rm)
        rp = 0.5 * (near + rp)
        zm, zp = z_near(near)
        zm = 0.5 * (near + zm)
        zp = 0.5 * (near + zp)
        total = inner + across + rm + rp
        total = total + jnp.where(lane == dz - 1, near, zp) + jnp.where(lane == 0, near, zm)
        inv = jnp.where(has[d], 1.0, 0.0) / (total + 1.5 * bulk)
        zm = jnp.where(lane == 0, 0.0, zm)
        zp = jnp.where(lane == dz - 1, 0.0, zp)
        for k, value in enumerate(
            (inner, across, rm, rp, zm, zp, total + bulk, 0.5 * bulk, inv)
        ):
            ghost[d, k] = value

    def all_ghost_weights():
        def edge(inside, corner, at, own):
            return jnp.where(inside, recv_d[0, corner, at : at + 1, :], own)

        for d in range(4):
            s = d % 2
            near = static_recv[d, 0]
            ends = near[0:1], near[dy - 1 : dy]
            if d < 2:
                cross = (faces[0], s_send_up[...])[s]
                low = edge(has[2], 2 * s, 6, ends[0])
                high = edge(has[3], 2 * s + 1, 6, ends[1])
            else:
                cross = s_send_y[1 - s]
                low = edge(has[0], s, 7, ends[0])
                high = edge(has[1], 2 + s, 7, ends[1])
            ghost_weights(d, cross, low, high)

    def ghost_apply(d, v, inner, cross, low, high):
        w = [ghost[d, k] for k in range(9)]
        coupled = w[7] * (v[0] + v[1] + v[2])
        out = []
        for c in range(3):
            rm, rp = rows_near(v[c], low[c], high[c])
            zm, zp = z_near(v[c])
            near = w[0] * inner[c] + w[1] * cross[c] + w[2] * rm + w[3] * rp
            near = near + w[4] * zm + w[5] * zp
            out.append(w[8] * (w[6] * v[c] + coupled - near))
        return out

    def ghost_step(turn, other, update, directions=(0, 1, 2, 3), ends=True):
        none = [jnp.zeros((1, dz), jnp.float32)] * 3
        for d in directions:
            s = d % 2
            if d < 2:
                v = [nearest(turn, s, c) for c in range(3)]
                inner = [recv_x[turn, s, c, s] for c in range(3)]
                cross = [mixed[s, c] for c in range(3)]
                low = [recv_d[turn, 2 * s, c : c + 1, :] for c in range(3)]
                high = [recv_d[turn, 2 * s + 1, c : c + 1, :] for c in range(3)]
            else:
                v = [recv_y[turn, s, 0, c] for c in range(3)]
                inner = [recv_y[turn, s, 1, c] for c in range(3)]
                cross = [y_send[turn, 1 - s, 0, c] for c in range(3)]
                low, high = none, none
                if ends:
                    low = [recv_d[turn, s, 3 + c : 4 + c, :] for c in range(3)]
                    high = [recv_d[turn, 2 + s, 3 + c : 4 + c, :] for c in range(3)]
            out = ghost_apply(d, v, inner, cross, low, high)
            for c in range(3):
                new = update(d, c, v[c], out[c])
                if d < 2:
                    u[other, c, (dx + 1) * s] = permute(new, 2 - s)
                else:
                    gy[s, c] = new

    top = m_own[...]
    for k, copy in enumerate(m_copies):
        copy.wait()
        top = jnp.maximum(top, m_all[k + 1])
    m2_own[...] = top
    for copy in m2_copies:
        copy.start()

    for d in range(2):
        i = (dx - 2, 1)[d]
        pack_send[d, 0] = invd[i]
        pack_send[d, 1] = hb[i]
        pack_send[d, 2] = jnp.where(row == 0, wym[i], jnp.where(row == dy - 1, wyp[i], 0.0))
    for d, y in ((2, dy - 2), (3, 1)):
        pack_send[d, 2] = zero_face
        pack_send[d, 2, 0:1, :] = wx[0, y : y + 1, :]
        pack_send[d, 2, dx - 1 : dx, :] = wx[dx, y : y + 1, :]
        for i in range(dx):
            pack_send[d, 0, i : i + 1, :] = invd[i, y : y + 1, :]
            pack_send[d, 1, i : i + 1, :] = hb[i, y : y + 1, :]
    for sx in range(2):
        i = (dx - 1) * sx
        values = (
            invd[i], hb[i], wx[dx * sx],
            jnp.where(row == 0, wym[i], 0.0), jnp.where(row == dy - 1, wyp[i], 0.0),
            shear[i + 1],
        )
        for k, value in enumerate(values):
            other = permute(value, (3, 0)[sx])
            for sy in range(2):
                y = (dy - 1) * sy
                corner_pack[2 * sx + sy, k : k + 1, :] = value[y : y + 1]
                corner_pack[2 * sx + sy, 8 + k : 9 + k, :] = other[y : y + 1]

    def p_copy(d):
        return remote(
            pack_send.at[d], pack_recv.at[d], p_ssem.at[d], p_rsem.at[d], peers[d]
        )

    def k_copy(k, at):
        return remote(
            corner_pack.at[k], recv_k.at[at], p_ssem.at[4 + k], p_rsem.at[4 + at],
            corner_peer[k],
        )

    exchange_start(p_copy)
    for k in range(4):
        @pl.when(has_corner[k])
        def _():
            k_copy(k, 3 - k).start()
    exchange_wait(t_copy)

    low, high = recv_rows(0)

    def first_plane(i, _):
        _, out = apply_plane(i, 0, low, high)
        inv = invd[i]
        for c in range(3):
            r[c, i] = out[c]
            u[1, c, i + 1] = out[c] * inv
        return 0

    def first_ghosts():
        all_ghost_weights()

        def update(d, c, v, out):
            before[d, c] = out
            return out

        ghost_step(0, 1, update)

    sweep_receive(first_plane, 0, 0, 0, first_ghosts)

    def second_plane(i, _):
        _, out = apply_plane(i, 1, *ghost_rows)
        for c in range(3):
            res[c, i] = out[c]
        return 0

    lax.fori_loop(0, dx, second_plane, 0, unroll=16)

    for k, copy in enumerate(m2_copies):
        copy.wait()
        top = jnp.maximum(top, m2_all[k + 1])
    upper = BOUND_MARGIN * jnp.broadcast_to(jnp.max(top, axis=1, keepdims=True), top.shape)
    lower = LOW_RATIO * upper
    theta = 0.5 * (upper + lower)
    delta = 0.5 * (upper - lower)
    sigma = theta / delta
    damping = 1.0 / sigma
    inv_theta = 1.0 / theta
    coef[0:8] = inv_theta
    rows = []
    for turn in range(1, CHEB):
        following = 1.0 / (2.0 * sigma - damping)
        rows.append((following * damping, 2.0 * following / delta))
        damping = following
    for turn, (a, c2) in enumerate(rows):
        coef[8 + 2 * turn : 9 + 2 * turn] = a[0:1]
        coef[9 + 2 * turn : 10 + 2 * turn] = c2[0:1]
    coef[14:15] = (rows[0][0] * inv_theta + rows[0][1])[0:1]
    coef[15:16] = (rows[0][1] * inv_theta)[0:1]
    (a, c2), (a_next, c_next) = rows[1], rows[2]
    ratio = c_next / c2
    coef[16:17] = (a_next + ratio)[0:1]
    coef[17:18] = (ratio * a)[0:1]
    coef[18:19] = (rows[0][0] + rows[0][1] * theta)[0:1]

    alpha, beta, it = bcoef(14), bcoef(15), bcoef(0)
    both_it = alpha + it
    a_two, c_two = bcoef(10), bcoef(11)

    def combine_plane(i, _):
        inv = invd[i]
        for c in range(3):
            d0 = u[0, c, i + 1]
            one = alpha * d0 - beta * u[1, c, i + 1]
            sol[c, i] = it * d0 + one
            rest = rhs[c, i] - both_it * r[c, i] + beta * res[c, i]
            res[c, i] = rest
            two = a_two * one + c_two * (rest * inv)
            u[0, c, i + 1] = two
            store_rows(1, c, i, two)
        return 0

    sweep_send(combine_plane, 1, 0, 0)
    for d in range(4):
        for c in range(3):
            v = nearest(0, d, c) if d < 2 else recv_y[0, d - 2, 0, c]
            before[d, c] = alpha * v - beta * before[d, c]

    def step_plane(slot, low, high, a, c2, following, summed=False, rows_of=None):
        other = 1 - slot

        def plane(i, sums):
            v, out = apply_plane(i, slot, low, high)
            inv = invd[i]
            new = []
            for c in range(3):
                rest = res[c, i] - out[c]
                res[c, i] = rest
                sol[c, i] = sol[c, i] + v[c]
                if summed:
                    new.append(sums[c] + rest)
                if not following:
                    continue
                ahead = c2 * (rest * inv)
                if a is not None:
                    ahead = ahead + a * v[c]
                u[other, c, i + 1] = ahead
                if rows_of is not None:
                    store_rows(rows_of, c, i, ahead)
            return tuple(new)
        return plane

    def pair_ghosts(turn, other):
        def done(directions=(0, 1, 2, 3), ends=True):
            e1, e2, e3 = bcoef(16), bcoef(17), bcoef(13)

            def update(d, c, v, out):
                return e1 * v - e2 * before[d, c] - e3 * out

            ghost_step(turn, other, update, directions, ends)
        return done

    def pair_receive(turn, slot, first, second, carry, ghosts):
        exchange_wait(h_copy(turn, slot), (2, 3))
        lax.fori_loop(1, dx - 1, first, (), unroll=SWEEP)
        ghosts((2, 3), False)
        carry = lax.fori_loop(2, dx - 2, second, carry, unroll=INNER)
        exchange_wait(h_copy(turn, slot), (0, 1))
        corners_wait(turn)
        place_faces(turn, slot)
        ghosts()
        for i in (0, dx - 1):
            first(i, ())
        for i in (0, 1, dx - 2, dx - 1):
            carry = second(i, carry)
        return carry

    def i_copy(d):
        return remote(inverse, inv_recv.at[d], i_ssem.at[d], i_rsem.at[d], peers[d])

    exchange_start(i_copy, (0, 1))
    first = step_plane(0, *recv_rows(1), bcoef(12), bcoef(13), True)
    second = step_plane(1, *ghost_rows, None, bcoef(0), True, summed=True, rows_of=2)
    init = tuple(jnp.zeros((dy, dz), jnp.float32) for _ in range(3))
    sums = pair_receive(1, 0, first, second, init, pair_ghosts(1, 1))

    c_own[...] = jnp.zeros(c_own.shape, jnp.float32)
    for c in range(3):
        c_own[c : c + 1, :] = jnp.sum(sums[c], axis=0, keepdims=True)
    c_all[1, g] = c_own[...]

    def c_copy(q, k):
        slot = q * ng + k
        return remote(
            c_own, c_all.at[q, g], c_ssem.at[slot], c_rsem.at[slot],
            (b + 1 - q, lax.rem(g + k, ng)),
        )

    def c_arrival(q, k):
        slot = q * ng + k
        source = lax.rem(g + ng - k, ng)
        return remote(
            c_own, c_all.at[q, source], c_ssem.at[slot], c_rsem.at[slot],
            (b + 1 - q, lax.rem(g + k, ng)),
        )

    def coarse_all(to_do, flags):
        for q in (0, 2, 1):
            first = 1 if q == 1 else 0
            if q == 1:
                for k in range(first, ng):
                    to_do(q, k)
                continue

            @pl.when(flags[q])
            def _():
                for k in range(first, ng):
                    to_do(q, k)

    coarse_all(lambda q, k: c_copy(q, k).start(), {0: has[1], 2: has[0]})
    send_faces(2, 0)
    send_corners(2, 0)
    send_rows(2, 0)
    f_all[...] = jnp.zeros(f_all.shape, jnp.float32)
    exchange_wait(p_copy)
    for k in range(4):
        @pl.when(has_corner[k])
        def _():
            k_copy(k, k).wait_recv()
    for k in range(4):
        @pl.when(has_corner[k])
        def _():
            k_copy(k, k).wait_send()
    for k in range(4):
        for n in range(6):
            for side in range(2):
                at = 2 * k + side
                corner_rows[n, at : at + 1, :] = recv_k[k, 8 * side + n : 8 * side + n + 1, :]
    exchange_wait(i_copy, (0, 1))
    cells_z = dz // BLOCK_Z
    size = 3 * cells_z * ng
    li = lax.broadcasted_iota(jnp.int32, (dz, size), 0)
    ki = lax.broadcasted_iota(jnp.int32, (dz, size), 1)
    gather = jnp.where(li // BLOCK_Z == ki % cells_z, 1.0 / (dx * dy * BLOCK_Z), 0.0)
    ri = lax.broadcasted_iota(jnp.int32, (ng * 8, size), 0)
    kk = lax.broadcasted_iota(jnp.int32, (ng * 8, size), 1) // cells_z
    mine = (ri // 8 == kk // 3) & (ri % 8 == kk % 3)
    bi = lax.broadcasted_iota(jnp.int32, (size, dz), 0)
    bl = lax.broadcasted_iota(jnp.int32, (size, dz), 1)
    placed = bi % cells_z == bl // BLOCK_Z
    coarse_all(lambda q, k: c_arrival(q, k).wait_recv(), {0: has[0], 2: has[1]})
    coarse_all(lambda q, k: c_copy(q, k).wait_send(), {0: has[1], 2: has[0]})

    flat = c_all[...].reshape(3 * ng * 8, dz)
    spread = jnp.dot(flat, gather, precision=HIGHEST, preferred_element_type=jnp.float32)
    for q in range(3):
        part = spread[q * ng * 8 : (q + 1) * ng * 8]
        vector = jnp.sum(jnp.where(mine, part, 0.0), axis=0, keepdims=True)
        matrix = inverse[...] if q == 1 else inv_recv[q // 2]
        correction = jnp.sum(matrix * vector, axis=1, keepdims=True)
        table = jnp.where(placed, jnp.broadcast_to(correction, (size, dz)), 0.0)
        for k in range(ng):
            for c in range(3):
                start = (k * 3 + c) * cells_z
                f_all[q, k + 1, c : c + 1, :] = jnp.sum(
                    table[start : start + cells_z], axis=0, keepdims=True
                )

    def full(q, at, c):
        return jnp.broadcast_to(f_all[q, at, c : c + 1, :], (dy, dz))

    own_fine = [full(1, g + 1, c) for c in range(3)]

    fine_sides = [z_near(own_fine[c]) for c in range(3)]
    fine_rows = [
        (
            jnp.where(row == 0, full(1, g, c), own_fine[c]),
            jnp.where(row == dy - 1, full(1, g + 2, c), own_fine[c]),
        )
        for c in range(3)
    ]
    fine_sum = own_fine[0] + own_fine[1] + own_fine[2]
    it = bcoef(0)

    def fine_plane(i, _):
        inv = invd[i]
        coupled = hb[i] * fine_sum
        for c in range(3):
            f = own_fine[c]
            first, last = isinstance(i, int) and i == 0, isinstance(i, int) and i == dx - 1
            xm = full(0, g + 1, c) if first else f
            xp = full(2, g + 1, c) if last else f
            near = wx[i] * xm + wx[i + 1] * xp
            near = near + wym[i] * fine_rows[c][0] + wyp[i] * fine_rows[c][1]
            near = near + wzm[i] * fine_sides[c][0] + wzp[i] * fine_sides[c][1]
            rest = res[c, i] - (dg[i] * f + coupled - near)
            res[c, i] = rest
            sol[c, i] = sol[c, i] + f
            ahead = it * (rest * inv)
            u[0, c, i + 1] = ahead
            y_send[2, 0, 0, c, pl.ds(i, 1), :] = ahead[dy - 1 : dy]
            y_send[2, 1, 0, c, pl.ds(i, 1), :] = ahead[0:1]
        return 0

    sent_wait(h_copy(2, 0))
    for i in range(4):
        fine_plane(i, 0)
        fine_plane(dx - 1 - i, 0)
    arrive_wait(h_copy(2, 0))
    corners_wait(2)
    for c in range(3):
        mixed[0, c] = permute(u[0, c, 1], 3)
        mixed[1, c] = permute(u[0, c, dx], 0)

    def fine_far(here, low, high, inv, half, w_low, w_high, near, across=None):
        lanes = lane[: near.shape[0]]
        zm, zp = z_near(near)
        zm = jnp.where(lanes == 0, 0.0, 0.5 * (near + zm))
        zp = jnp.where(lanes == dz - 1, 0.0, 0.5 * (near + zp))
        rim = jnp.where((lanes == 0) | (lanes == dz - 1), near, 0.0)
        weight = 2.0 * half + w_low + w_high + zm + zp + rim
        if across is not None:
            weight = weight + across[0]
        coupled = half * (here[0] + here[1] + here[2])
        out = []
        for c in range(3):
            fm, fp = z_near(here[c])
            value = weight * here[c] + coupled - zm * fm - zp * fp
            value = value - w_low * low[c] - w_high * high[c]
            if across is not None:
                value = value - across[0] * across[1][c]
            out.append(inv * value)
        return out

    for d in range(4):
        s = d % 2
        if d < 2:
            spots = (2 * s, g + 1), (2 * s, g), (2 * s, g + 2)
        else:
            at = g + 2 * s
            spots = (1, at), (0, at), (2, at)
        here, low, high = [[full(*spot, c) for c in range(3)] for spot in spots]
        out = ghost_apply(d, here, here, own_fine, low, high)
        inv, half, rim = [pack_recv[d, k] for k in range(3)]
        w_low = jnp.where(row == 0, rim, 0.0)
        w_high = jnp.where(row == dy - 1, rim, 0.0)
        far = fine_far(here, low, high, inv, half, w_low, w_high, static_recv[d, 1])
        for c in range(3):
            if d < 2:
                recv_x[2, s, c, 1 - s] = nearest(2, s, c) - it * out[c]
                recv_x[2, s, c, s] = recv_x[2, s, c, s] - it * far[c]
            else:
                recv_y[2, s, 0, c] = recv_y[2, s, 0, c] - it * out[c]
                recv_y[2, s, 1, c] = recv_y[2, s, 1, c] - it * far[c]

    for k, (sx, sy) in enumerate(corners):
        q, at = 2 * sx, g + 2 * sy
        spots = (q, at), (q, jnp.maximum(at - 1, 0)), (q, jnp.minimum(at + 1, ng + 1)), (1, at)
        for n, spot in enumerate(spots):
            for c in range(3):
                value = f_all[(*spot, slice(c, c + 1))]
                spread_k[n, c, 2 * k : 2 * k + 1, :] = value
                spread_k[n, c, 2 * k + 1 : 2 * k + 2, :] = value
        for c in range(3):
            for n in range(2):
                at = 2 * k + n
                spread_k[4, c, at : at + 1, :] = recv_d[2, k, 3 * n + c : 3 * n + c + 1, :]
    here, low, high, beside = [[spread_k[n, c] for c in range(3)] for n in range(4)]
    inv, half, cross, w_low, w_high, near = [corner_rows[n] for n in range(6)]
    out = fine_far(here, low, high, inv, half, w_low, w_high, near, (cross, beside))
    for c in range(3):
        spread_k[4, c] = spread_k[4, c] - it[0:8] * out[c]
    for k in range(4):
        for c in range(3):
            for n in range(2):
                at = 2 * k + n
                recv_d[2, k, 3 * n + c : 3 * n + c + 1, :] = spread_k[4, c, at : at + 1, :]

    place_faces(2, 0)
    e1, e3 = bcoef(18), bcoef(9)

    def first_update(d, c, v, out):
        new = e1 * v - e3 * out
        before[d, c] = new
        return new

    first = step_plane(0, *recv_rows(2), bcoef(8), bcoef(9), True)
    second = step_plane(1, *ghost_rows, bcoef(10), bcoef(11), True, rows_of=3)
    ghost_step(2, 1, first_update)
    for i in range(3):
        first(i, ())
        first(dx - 1 - i, ())
    for i in range(2):
        second(i, ())
        second(dx - 1 - i, ())
    send_faces(3, 0)
    send_corners(3, 0)
    lax.fori_loop(4, dx - 4, fine_plane, 0, unroll=8)
    ghost_step(2, 1, first_update, (2, 3))
    lax.fori_loop(3, dx - 3, first, (), unroll=10)
    lax.fori_loop(2, dx - 2, second, (), unroll=INNER)
    send_rows(3, 0)
    first = step_plane(0, *recv_rows(3), bcoef(12), bcoef(13), True)
    second = step_plane(1, *ghost_rows, None, None, False)
    pair_receive(3, 0, first, second, (), pair_ghosts(3, 1))


def per_device(rhs, material, level, mortar, mu, lam, inverse):
    nb = lax.axis_size("bricks")
    ng = lax.axis_size("group")
    dx, dy, dz = material.shape
    f32 = jnp.float32
    vmem = pl.BlockSpec(memory_space=pltpu.VMEM)
    smem = pl.BlockSpec(memory_space=pltpu.SMEM)
    hbm = pl.BlockSpec(memory_space=pltpu.HBM)
    dma = pltpu.SemaphoreType.DMA
    grid = pltpu.VMEM((dx, dy, dz), f32)
    cg = inverse.shape[1]
    scratch = [
        pltpu.VMEM((3, dx, dy, dz), f32),
        pltpu.VMEM((dx, dy, dz), jnp.int32),
        pltpu.VMEM((cg, cg), f32),
        pltpu.VMEM((2, 3, dx + 2, dy, dz), f32),
        pltpu.VMEM((3, dx, dy, dz), f32),
        pltpu.VMEM((dx + 2, dy, dz), f32),
        pltpu.VMEM((dx + 1, dy, dz), f32),
        grid, grid, grid, grid, grid, grid, grid,
        pltpu.VMEM((24, dz), f32),
        pltpu.VMEM((dy, dz), f32),
        pltpu.VMEM((2, dx, dz), f32),
        pltpu.VMEM((4, dx, dz), f32),
        pltpu.VMEM((4, 3, dx, dz), f32),
        pltpu.VMEM((4, 3, dx, dz), f32),
        pltpu.VMEM((dy, dz), jnp.int32),
        pltpu.VMEM((dy, dz), jnp.int32),
        pltpu.VMEM((4, dy, dz), jnp.int32),
        pltpu.VMEM((1, dy, dz), f32),
        pltpu.VMEM((2, 3, dy, dz), f32),
        pltpu.VMEM((ROUNDS, 2, 2, 3, dx, dz), f32),
        pltpu.VMEM((ROUNDS, 4, 8, dz), f32),
        pltpu.VMEM((ROUNDS, 2, 3, 2, dy, dz), f32),
        pltpu.VMEM((ROUNDS, 2, 2, 3, dx, dz), f32),
        pltpu.VMEM((ROUNDS, 4, 8, dz), f32),
        pltpu.VMEM((4, 9, dy, dz), f32),
        pltpu.VMEM((2, 3, dx, dz), f32),
        pltpu.VMEM((4, 3, dy, dz), f32),
        pltpu.VMEM((4, 3, dx, dz), f32),
        pltpu.VMEM((4, 3, dx, dz), f32),
        pltpu.VMEM((4, 16, dz), f32),
        pltpu.VMEM((4, 16, dz), f32),
        pltpu.VMEM((6, 8, dz), f32),
        pltpu.VMEM((5, 3, 8, dz), f32),
        pltpu.VMEM((8, dz), f32),
        pltpu.VMEM((2 * ng, 8, dz), f32),
        pltpu.VMEM((8, dz), f32),
        pltpu.VMEM((nb, 8, dz), f32),
        pltpu.VMEM((8, dz), f32),
        pltpu.VMEM((3, ng, 8, dz), f32),
        pltpu.VMEM((3, ng + 2, 8, dz), f32),
        pltpu.VMEM((2, cg, cg), f32),
        dma((3,)),
        dma((4,)), dma((4,)),
        dma((5,)), dma((5,)),
        dma((ROUNDS, 8)), dma((ROUNDS, 8)),
        dma((8,)), dma((8,)),
        dma((2 * ng,)), dma((2 * ng,)),
        dma((nb,)), dma((nb,)),
        dma((3 * ng,)), dma((3 * ng,)),
        dma((2,)), dma((2,)),
    ]
    rhs, material, inverse, mortar, mu, lam = (
        pltpu.with_memory_space_constraint(x, pltpu.HBM)
        for x in (rhs, material, inverse, mortar, mu, lam)
    )
    both = pl.pallas_call(
        functools.partial(kernel, nb, ng, dx, dy, dz),
        out_shape=jax.ShapeDtypeStruct((2, *rhs.shape), f32),
        in_specs=[hbm, hbm, vmem, smem, smem, smem, hbm],
        out_specs=vmem,
        scratch_shapes=scratch,
        compiler_params=pltpu.CompilerParams(
            collective_id=0, has_side_effects=True, vmem_limit_bytes=16 * 2**20
        ),
    )(rhs, material, level, mortar, mu, lam, inverse)
    return both[0], both[1]


def solution(mesh):
    return jax.shard_map(
        per_device,
        mesh=mesh,
        in_specs=(
            P(None, "bricks", "group", None),
            P("bricks", "group", None),
            P("bricks", "group"),
            P("bricks", "group", None),
            P(),
            P(),
            P("bricks", None, None),
        ),
        out_specs=(P(None, "bricks", "group", None), P(None, "bricks", "group", None)),
        check_vma=False,
    )
```
